32 devices in a mesh: design: 2 (over x), tile: 8 (over z, y), mode: 2 (over core).
Axes of the slice: x: 2, y: 2, z: 4, core: 2. Of those that a mesh axis runs over, the one named last changes fastest.
Arguments:
- forward: bfloat16 [4, 2, 4096, 4096], P(('design', 'mode'), None, 'tile'), parts along dimension 0, may hold values from -6 to 6
- adjoint_next: bfloat16 [4, 2, 4096, 4096], P(('design', 'mode'), None, 'tile'), parts along dimension 0, may hold values from -6 to 6
- phase: float32 [8192, 4096], P(('design', 'tile'), 'mode'), parts along dimension 0, may hold values from -3.140625 to 3.140625
- blocks: bfloat16 [2, 128, 4, 64, 64], P(None, 'design'), parts along dimension 1, may hold values from -0.25 to 0.25
- offsets: int32 [128, 4], P('design'), parts along dimension 0, may hold values from -2 to 2, as said below
Outputs:
- phase_next: float32 [8192, 4096], P(('design', 'tile'), 'mode'), parts along dimension 0
- forward_next: bfloat16 [4, 2, 4096, 4096], P(('design', 'mode'), None, 'tile'), parts along dimension 0
The draws below stay inside these ranges and needn't reach their ends.
There are 2 independent parts, one for each index of `design`. The reference program is written for one: setup_inputs(seed, part) draws one part's arguments, and reference() takes and returns one part's arrays. A program takes and returns all parts, laid end to end along the dimension named above; each array names one. Nothing has to cross between parts.
Inputs may be any that keep to these rules, and one draw needn't show every extreme that they name: Each row of offsets holds 4 different values, all of -2 to 2 but one; row 0 holds both -2 and 2.
All inputs are finite; a program needn't handle non-finite values.
Results may differ from the reference program's by a relative error of at most 0.02.
Values may be sent and summed in bfloat16 or wider, within the bound.
A program may use at most 256 MiB of HBM per device.

```python
import jax
import jax.numpy as jnp
from jax import lax

N = 4096
BLK = 64
RADIUS = 2
BANDS = 4
MODES = 2
NB = 64


def draw_offsets(key, part):
    missing = jax.random.randint(key, (NB,), 0, 2 * RADIUS + 1).astype(jnp.int32)
    missing = jnp.where(jnp.arange(NB, dtype=jnp.int32) == 0, RADIUS, missing)
    slots = jnp.arange(BANDS, dtype=jnp.int32)[None, :]
    return (slots + (slots >= missing[:, None]).astype(jnp.int32) - RADIUS).astype(jnp.int32)


def level_of(own_key, dims, cuts, least, largest):
    gain, own = 1.0, jax.random.fold_in(own_key, 6)
    for dim, shards_of in cuts:
        steps = jnp.exp(jax.random.uniform(jax.random.fold_in(own, dim), (shards_of,), jnp.float32, least / len(cuts), largest / len(cuts)))
        gain = gain * jnp.repeat(steps, dims[dim] // shards_of).reshape([-1 if axis == dim else 1 for axis in range(len(dims))])
    return gain


def bell_draw(rng, shape, width, bound, split=(), kind=jnp.bfloat16):
    level = level_of(rng, shape, split, -0.22, 0.18) if split else 1.0
    values = jax.random.normal(rng, shape, jnp.float32) * width * level
    return jnp.minimum(jnp.maximum(values, -bound), bound).astype(kind)


def setup_inputs(seed: int = 0, part: int = 0) -> dict:
    splits = jax.random.split(jax.random.key(seed), 6)
    part_keys = jax.random.split(jax.random.fold_in(splits[5], part), 6)
    forward = bell_draw(part_keys[0], (MODES, 2, N, N), 1.0, 6.0, ((0, 2), (2, 8)))
    adjoint_next = bell_draw(part_keys[1], (MODES, 2, N, N), 1.0, 6.0, ((0, 2), (2, 8)))
    phase = jnp.clip(jax.random.uniform(part_keys[2], (N, N), jnp.float32, -3.140625, 3.140625), -3.140625, 3.140625)
    blocks = bell_draw(part_keys[3], (2, NB, BANDS, BLK, BLK), (2 * BANDS * BLK) ** -0.5, 0.25)
    offsets = draw_offsets(jax.random.fold_in(jax.random.fold_in(splits[5], part), 71), part)
    return dict(forward=forward, adjoint_next=adjoint_next, phase=phase, blocks=blocks, offsets=offsets)


def along_columns(field_in, real_part, imag_part, index_table):
    row_count = field_in.shape[1]
    pieces = field_in.reshape(2, row_count, NB, BLK)
    picked = jnp.take(pieces, index_table, axis=2)
    real_sum = jnp.einsum("prckj,ckij->prci", picked, real_part)
    imag_sum = jnp.einsum("prckj,ckij->prci", picked, imag_part)
    result = jnp.stack([real_sum[0] - imag_sum[1], imag_sum[0] + real_sum[1]])
    return result.reshape(2, row_count, NB * BLK)


def propagate(field_in, real_part, imag_part, index_table):
    middle = along_columns(field_in.astype(jnp.float32), real_part, imag_part, index_table).astype(jnp.bfloat16)
    turned = jnp.swapaxes(middle, 1, 2).astype(jnp.float32)
    return jnp.swapaxes(along_columns(turned, real_part, imag_part, index_table), 1, 2)


def reference(forward, adjoint_next, phase, blocks, offsets):
    raw_index = jnp.arange(NB, dtype=jnp.int32)[:, None] + offsets.astype(jnp.int32)
    inside = (raw_index >= 0) & (raw_index < NB)
    index_table = jnp.clip(raw_index, 0, NB - 1).astype(jnp.int32)
    zero_block = jnp.zeros((), blocks.dtype)
    real_blocks = jnp.where(inside[:, :, None, None], blocks[0], zero_block).astype(jnp.float32)
    imag_blocks = jnp.where(inside[:, :, None, None], blocks[1], zero_block).astype(jnp.float32)
    cos_old = jnp.cos(phase)
    sin_old = jnp.sin(phase)

    def mode_terms(pair):
        field_fwd, field_adj = pair
        adjoint_here = propagate(field_adj, real_blocks, -imag_blocks, index_table).astype(jnp.bfloat16)
        adjoint_here = lax.optimization_barrier(adjoint_here).astype(jnp.float32)
        fwd_real = field_fwd[0].astype(jnp.float32)
        fwd_imag = field_fwd[1].astype(jnp.float32)
        lit_real = cos_old * fwd_real - sin_old * fwd_imag
        lit_imag = sin_old * fwd_real + cos_old * fwd_imag
        term_real = adjoint_here[0] * lit_real + adjoint_here[1] * lit_imag
        term_imag = adjoint_here[0] * lit_imag - adjoint_here[1] * lit_real
        return jnp.stack([term_real, term_imag])

    terms = lax.map(mode_terms, (forward, adjoint_next))
    intersections = jnp.sum(terms, axis=(2, 3))
    gradient = jnp.sum(intersections[:, 0, None, None] * terms[:, 1] - intersections[:, 1, None, None] * terms[:, 0], axis=0)
    phase_next = phase - gradient / (4.0 * N * MODES)
    cos_new = jnp.cos(phase_next)
    sin_new = jnp.sin(phase_next)

    def launch(field_fwd):
        fwd_real = field_fwd[0].astype(jnp.float32)
        fwd_imag = field_fwd[1].astype(jnp.float32)
        launched = jnp.stack([cos_new * fwd_real - sin_new * fwd_imag, sin_new * fwd_real + cos_new * fwd_imag]).astype(jnp.bfloat16)
        return propagate(launched, real_blocks, imag_blocks, index_table).astype(jnp.bfloat16)

    forward_next = lax.map(launch, forward)
    return phase_next, forward_next
```

```python
import functools

import jax
import jax.numpy as jnp
from jax import lax
from jax.experimental import pallas as pl
from jax.experimental.pallas import tpu as pltpu
from jax.sharding import PartitionSpec as P

BLK = 64
RADIUS = 2
EDGE = RADIUS * BLK
WIDE = 256
VMEM_LIMIT = 44 * 1024 * 1024

F32 = jnp.float32
BF16 = jnp.bfloat16


def params():
    return pltpu.CompilerParams(vmem_limit_bytes=VMEM_LIMIT)


def cost(flops, moved):
    return pl.CostEstimate(flops=int(flops), bytes_accessed=int(moved), transcendentals=0)


def sincos(x):
    turns = jnp.round(x * 0.6366197723675814)
    r = x - turns * 1.5703125
    r = r - turns * 4.837512969970703125e-4
    r = r - turns * 7.549789954891882e-8
    quadrant = turns.astype(jnp.int32)
    z = r * r
    s = r + r * z * (-1.6666654611e-1 + z * (8.3321608736e-3 + z * -1.9515295891e-4))
    c = 1.0 - 0.5 * z + z * z * (4.166664568298827e-2 + z * (-1.388731625493765e-3 + z * 2.443315711809948e-5))
    swap = (quadrant & 1) == 1
    sine = jnp.where(swap, c, s)
    cosine = jnp.where(swap, s, c)
    sine = jnp.where((quadrant & 2) == 2, -sine, sine)
    cosine = jnp.where(((quadrant + 1) & 2) == 2, -cosine, cosine)
    return sine, cosine


def dot(a, b):
    return jnp.dot(a, b, preferred_element_type=F32)


def build_kernel(pos_ref, blk_ref, out_ref, *, group, transposed):
    base = pl.program_id(0) * group
    zero = jnp.zeros((BLK, BLK), F32)
    for part in range(2):
        strips = []
        for r in range(group):
            own = [blk_ref[part, r, k].astype(F32) for k in range(blk_ref.shape[2])]
            pieces = [zero] * r
            for d in range(2 * RADIUS + 1):
                piece = zero
                for k, block in enumerate(own):
                    piece = jnp.where(pos_ref[base + r, k] == d, block, piece)
                pieces.append(piece)
            pieces += [zero] * (group - 1 - r)
            strips.append(jnp.concatenate(pieces, axis=1))
        full = jnp.concatenate(strips, axis=0)
        if transposed:
            full = full.T
        out_ref[0, part] = full.astype(BF16)


def build(blocks, pos, group, transposed):
    _, rows, bands, _, _ = blocks.shape
    tall, wide = group * BLK, (group + 2 * RADIUS) * BLK
    if transposed:
        tall, wide = wide, tall
    count = rows // group
    return pl.pallas_call(
        functools.partial(build_kernel, group=group, transposed=transposed),
        out_shape=jax.ShapeDtypeStruct((count, 2, tall, wide), BF16),
        grid_spec=pltpu.PrefetchScalarGridSpec(
            num_scalar_prefetch=1,
            grid=(count,),
            in_specs=[pl.BlockSpec((2, group, bands, BLK, BLK), lambda g, p: (0, g, 0, 0, 0))],
            out_specs=pl.BlockSpec((1, 2, tall, wide), lambda g, p: (g, 0, 0, 0)),
        ),
        compiler_params=params(),
        cost_estimate=cost(0, 16 * rows * bands * BLK * BLK),
        name="build_operator",
    )(pos, blocks)


def window_specs(rows, groups):
    last = 2 * groups - 1
    return [
        pl.BlockSpec((2, rows, 128), lambda j: (0, 0, jnp.maximum(2 * j - 1, 0))),
        pl.BlockSpec((2, rows, WIDE), lambda j: (0, 0, j)),
        pl.BlockSpec((2, rows, 128), lambda j: (0, 0, jnp.minimum(2 * j + 2, last))),
    ]


def window(left, mid, right, part):
    return jnp.concatenate([left[part], mid[part], right[part]], axis=1)


def column_product(x_re, x_im, op_ref, conj):
    op_re, op_im = op_ref[0, 0], op_ref[0, 1]
    rr, ii = dot(x_re, op_re), dot(x_im, op_im)
    ri, ir = dot(x_re, op_im), dot(x_im, op_re)
    if conj:
        return (rr + ii).astype(BF16), (ri - ir).astype(BF16)
    return (rr - ii).astype(BF16), (ri + ir).astype(BF16)


def column_kernel(left, mid, right, op_ref, out_ref, *, conj):
    out_re, out_im = column_product(
        window(left, mid, right, 0), window(left, mid, right, 1), op_ref, conj
    )
    out_ref[0] = out_re
    out_ref[1] = out_im


def column_pass(field, op, conj):
    _, rows, width = field.shape
    groups = width // WIDE
    return pl.pallas_call(
        functools.partial(column_kernel, conj=conj),
        out_shape=jax.ShapeDtypeStruct(field.shape, BF16),
        grid=(groups,),
        in_specs=window_specs(rows, groups)
        + [pl.BlockSpec((1, 2, op.shape[2], WIDE), lambda j: (j, 0, 0, 0))],
        out_specs=pl.BlockSpec((2, rows, WIDE), lambda j: (0, 0, j)),
        compiler_params=params(),
        cost_estimate=cost(8 * rows * width * op.shape[2], 12 * rows * width + 2 * op.size),
        name="column_pass",
    )(field, field, field, op)


def row_groups(top, main, bottom, row_op):
    whole_re = jnp.concatenate([top[0], main[0], bottom[0]], axis=0)
    whole_im = jnp.concatenate([top[1], main[1], bottom[1]], axis=0)
    count, _, tall, deep = row_op.shape
    for i in range(count):
        m_re = whole_re[i * tall : i * tall + deep]
        m_im = whole_im[i * tall : i * tall + deep]
        op_re, op_im = row_op[i, 0], row_op[i, 1]
        out_re = dot(op_re, m_re) - dot(op_im, m_im)
        out_im = dot(op_re, m_im) + dot(op_im, m_re)
        yield i * tall, tall, out_re, out_im


def adjoint_row_kernel(tl, tm, tr, bl, bm, br, op_ref, main, row_op, lit, terms, sums):
    x_re = jnp.concatenate([window(tl, tm, tr, 0), window(bl, bm, br, 0)], axis=0)
    x_im = jnp.concatenate([window(tl, tm, tr, 1), window(bl, bm, br, 1)], axis=0)
    halo_re, halo_im = column_product(x_re, x_im, op_ref, True)

    @pl.when(pl.program_id(0) == 0)
    def _():
        sums[...] = jnp.zeros_like(sums)

    top = (halo_re[:EDGE], halo_im[:EDGE])
    bottom = (halo_re[EDGE:], halo_im[EDGE:])
    for low, tall, cj_re, cj_im in row_groups(top, main, bottom, row_op):
        cj_re = cj_re.astype(BF16).astype(F32)
        cj_im = cj_im.astype(BF16).astype(F32)
        lit_re = lit[0, low : low + tall].astype(F32)
        lit_im = lit[1, low : low + tall].astype(F32)
        t_re = cj_re * lit_re - cj_im * lit_im
        t_im = cj_re * lit_im + cj_im * lit_re
        terms[0, low : low + tall] = t_re.astype(BF16)
        terms[1, low : low + tall] = t_im.astype(BF16)
        sums[0] += jnp.sum(t_re.reshape(tall // 8, 8, WIDE), axis=0)
        sums[1] += jnp.sum(t_im.reshape(tall // 8, 8, WIDE), axis=0)


def adjoint_rows(top, bottom, op, main, row_op, lit):
    _, rows, width = main.shape
    groups = width // WIDE
    edge = window_specs(EDGE, groups)
    tile = pl.BlockSpec((2, rows, WIDE), lambda j: (0, 0, j))
    return pl.pallas_call(
        adjoint_row_kernel,
        out_shape=(
            jax.ShapeDtypeStruct(main.shape, BF16),
            jax.ShapeDtypeStruct((2, 8, WIDE), F32),
        ),
        grid=(groups,),
        in_specs=edge
        + edge
        + [
            pl.BlockSpec((1, 2, op.shape[2], WIDE), lambda j: (j, 0, 0, 0)),
            tile,
            pl.BlockSpec(row_op.shape, lambda j: (0, 0, 0, 0)),
            tile,
        ],
        out_specs=(tile, pl.BlockSpec((2, 8, WIDE), lambda j: (0, 0, 0))),
        compiler_params=params(),
        cost_estimate=cost(12 * rows * width * op.shape[2], 16 * rows * width),
        name="adjoint_rows",
    )(top, top, top, bottom, bottom, bottom, op, main, row_op, lit)


def forward_row_kernel(top, main, bottom, row_op, out):
    for low, tall, out_re, out_im in row_groups(top, main, bottom, row_op):
        out[0, 0, low : low + tall] = out_re.astype(BF16)
        out[0, 1, low : low + tall] = out_im.astype(BF16)


def forward_rows(top, main, bottom, row_op):
    _, rows, width = main.shape
    groups = width // WIDE
    edge = pl.BlockSpec((2, EDGE, WIDE), lambda j: (0, 0, j))
    return pl.pallas_call(
        forward_row_kernel,
        out_shape=jax.ShapeDtypeStruct((1,) + main.shape, BF16),
        grid=(groups,),
        in_specs=[
            edge,
            pl.BlockSpec((2, rows, WIDE), lambda j: (0, 0, j)),
            edge,
            pl.BlockSpec(row_op.shape, lambda j: (0, 0, 0, 0)),
        ],
        out_specs=pl.BlockSpec((1, 2, rows, WIDE), lambda j: (0, 0, 0, j)),
        compiler_params=params(),
        cost_estimate=cost(8 * rows * width * row_op.shape[3], 10 * rows * width),
        name="forward_rows",
    )(top, main, bottom, row_op)


def lit_kernel(phase, fwd, lit):
    sine, cosine = sincos(phase[0])
    f_re, f_im = fwd[0, 0].astype(F32), fwd[0, 1].astype(F32)
    lit[0] = (cosine * f_re - sine * f_im).astype(BF16)
    lit[1] = (sine * f_re + cosine * f_im).astype(BF16)


def light(phases, forward):
    _, _, rows, width = forward.shape
    half = phases.shape[2] // WIDE
    return pl.pallas_call(
        lit_kernel,
        out_shape=jax.ShapeDtypeStruct(forward.shape[1:], BF16),
        grid=(width // WIDE,),
        in_specs=[
            pl.BlockSpec((1, rows, WIDE), lambda j: (j // half, 0, j % half)),
            pl.BlockSpec((1, 2, rows, WIDE), lambda j: (0, 0, 0, j)),
        ],
        out_specs=pl.BlockSpec((2, rows, WIDE), lambda j: (0, 0, j)),
        compiler_params=params(),
        cost_estimate=cost(60 * rows * width, 12 * rows * width),
        name="light",
    )(phases, forward)


def launch_values(coef, terms, other, phase, fwd, launched):
    gradient = (coef[0] * terms[1].astype(F32) - coef[1] * terms[0].astype(F32)) + (
        coef[2] * other[1].astype(F32) - coef[3] * other[0].astype(F32)
    )
    updated = phase[0] - gradient
    sine, cosine = sincos(updated)
    f_re, f_im = fwd[0, 0].astype(F32), fwd[0, 1].astype(F32)
    launched[0] = (cosine * f_re - sine * f_im).astype(BF16)
    launched[1] = (sine * f_re + cosine * f_im).astype(BF16)
    return updated


def launch_kernel(coef, terms, other, phase, fwd, launched, phase_next):
    phase_next[0] = launch_values(coef, terms, other, phase, fwd, launched)


def launch(coef, terms, other, phases, forward):
    _, _, rows, width = forward.shape
    half = phases.shape[2] // WIDE
    tile = pl.BlockSpec((2, rows, WIDE), lambda j, c: (0, 0, j))
    plane = pl.BlockSpec((1, rows, WIDE), lambda j, c: (j // half, 0, j % half))
    return pl.pallas_call(
        launch_kernel,
        out_shape=(
            jax.ShapeDtypeStruct(forward.shape[1:], BF16),
            jax.ShapeDtypeStruct(phases.shape, F32),
        ),
        grid_spec=pltpu.PrefetchScalarGridSpec(
            num_scalar_prefetch=1,
            grid=(width // WIDE,),
            in_specs=[
                tile,
                tile,
                plane,
                pl.BlockSpec((1, 2, rows, WIDE), lambda j, c: (0, 0, 0, j)),
            ],
            out_specs=(tile, plane),
        ),
        compiler_params=params(),
        cost_estimate=cost(60 * rows * width, 24 * rows * width),
        name="launch",
    )(coef, terms, other, phases, forward)


def launch_edge_kernel(coef, terms, other, phase, fwd, launched):
    launch_values(coef, terms, other, phase, fwd, launched)


def launch_edges(coef, terms, other, phases, forward):
    _, _, rows, width = forward.shape
    wide = 2 * WIDE
    half = phases.shape[2] // wide
    far = rows // EDGE - 1
    tile = pl.BlockSpec((2, EDGE, wide), lambda e, j, c: (0, e * far, j))
    return pl.pallas_call(
        launch_edge_kernel,
        out_shape=jax.ShapeDtypeStruct((2, 2 * EDGE, width), BF16),
        grid_spec=pltpu.PrefetchScalarGridSpec(
            num_scalar_prefetch=1,
            grid=(2, width // wide),
            in_specs=[
                tile,
                tile,
                pl.BlockSpec((1, EDGE, wide), lambda e, j, c: (j // half, e * far, j % half)),
                pl.BlockSpec((1, 2, EDGE, wide), lambda e, j, c: (0, 0, e * far, j)),
            ],
            out_specs=pl.BlockSpec((2, EDGE, wide), lambda e, j, c: (0, e, j)),
        ),
        compiler_params=params(),
        cost_estimate=cost(120 * EDGE * width, 48 * EDGE * width),
        name="launch_edges",
    )(coef, terms, other, phases, forward)


def complex_rows(op_re, op_im, m_re, m_im):
    return dot(op_re, m_re) - dot(op_im, m_im), dot(op_re, m_im) + dot(op_im, m_re)


def add_terms(cj_re, cj_im, lit_re, lit_im, terms, sums, low):
    tall = cj_re.shape[0]
    cj_re = cj_re.astype(BF16).astype(F32)
    cj_im = cj_im.astype(BF16).astype(F32)
    lit_re, lit_im = lit_re.astype(F32), lit_im.astype(F32)
    t_re = cj_re * lit_re - cj_im * lit_im
    t_im = cj_re * lit_im + cj_im * lit_re
    terms[0, low : low + tall] = t_re.astype(BF16)
    terms[1, low : low + tall] = t_im.astype(BF16)
    sums[0] += jnp.sum(t_re.reshape(tall // 8, 8, WIDE), axis=0)
    sums[1] += jnp.sum(t_im.reshape(tall // 8, 8, WIDE), axis=0)


def adjoint_inner_kernel(main, row_op, lit, terms, sums):
    @pl.when(pl.program_id(0) == 0)
    def _():
        sums[...] = jnp.zeros_like(sums)

    rows = main.shape[1]
    cj_re, cj_im = complex_rows(row_op[0, 0], row_op[0, 1], main[0], main[1])
    add_terms(cj_re, cj_im, lit[0, EDGE : rows - EDGE], lit[1, EDGE : rows - EDGE], terms, sums, 0)


def adjoint_inner(main, row_op, lit):
    _, rows, width = main.shape
    inner = rows - 2 * EDGE
    tile = pl.BlockSpec((2, rows, WIDE), lambda j: (0, 0, j))
    return pl.pallas_call(
        adjoint_inner_kernel,
        out_shape=(
            jax.ShapeDtypeStruct((2, inner, width), BF16),
            jax.ShapeDtypeStruct((2, 8, WIDE), F32),
        ),
        grid=(width // WIDE,),
        in_specs=[tile, pl.BlockSpec(row_op.shape, lambda j: (0, 0, 0, 0)), tile],
        out_specs=(
            pl.BlockSpec((2, inner, WIDE), lambda j: (0, 0, j)),
            pl.BlockSpec((2, 8, WIDE), lambda j: (0, 0, 0)),
        ),
        compiler_params=params(),
        cost_estimate=cost(8 * inner * width * rows, 12 * rows * width),
        name="adjoint_inner",
    )(main, row_op, lit)


def edge_windows(main, part, top, bottom):
    rows = main.shape[1]
    return (
        jnp.concatenate([top, main[part, : 2 * EDGE]], axis=0),
        jnp.concatenate([main[part, rows - 2 * EDGE :], bottom], axis=0),
    )


def adjoint_edge_kernel(tl, tm, tr, bl, bm, br, op_ref, main, edge_op, lit, before, terms, sums):
    x_re = jnp.concatenate([window(tl, tm, tr, 0), window(bl, bm, br, 0)], axis=0)
    x_im = jnp.concatenate([window(tl, tm, tr, 1), window(bl, bm, br, 1)], axis=0)
    halo_re, halo_im = column_product(x_re, x_im, op_ref, True)

    @pl.when(pl.program_id(0) == 0)
    def _():
        sums[...] = before[...]

    rows = main.shape[1]
    res = edge_windows(main, 0, halo_re[:EDGE], halo_re[EDGE:])
    ims = edge_windows(main, 1, halo_im[:EDGE], halo_im[EDGE:])
    for i, low in enumerate((0, rows - EDGE)):
        cj_re, cj_im = complex_rows(edge_op[i, 0], edge_op[i, 1], res[i], ims[i])
        add_terms(cj_re, cj_im, lit[0, low : low + EDGE], lit[1, low : low + EDGE], terms, sums, i * EDGE)


def adjoint_edges(top, bottom, op, main, edge_op, lit, before):
    _, rows, width = main.shape
    groups = width // WIDE
    edge = window_specs(EDGE, groups)
    tile = pl.BlockSpec((2, rows, WIDE), lambda j: (0, 0, j))
    return pl.pallas_call(
        adjoint_edge_kernel,
        out_shape=(
            jax.ShapeDtypeStruct((2, 2 * EDGE, width), BF16),
            jax.ShapeDtypeStruct((2, 8, WIDE), F32),
        ),
        grid=(groups,),
        in_specs=edge
        + edge
        + [
            pl.BlockSpec((1, 2, op.shape[2], WIDE), lambda j: (j, 0, 0, 0)),
            tile,
            pl.BlockSpec(edge_op.shape, lambda j: (0, 0, 0, 0)),
            tile,
            pl.BlockSpec((2, 8, WIDE), lambda j: (0, 0, 0)),
        ],
        out_specs=(
            pl.BlockSpec((2, 2 * EDGE, WIDE), lambda j: (0, 0, j)),
            pl.BlockSpec((2, 8, WIDE), lambda j: (0, 0, 0)),
        ),
        compiler_params=params(),
        cost_estimate=cost(32 * EDGE * width * op.shape[2], 16 * rows * width),
        name="adjoint_edges",
    )(top, top, top, bottom, bottom, bottom, op, main, edge_op, lit, before)


def forward_inner_kernel(main, row_op, out):
    out_re, out_im = complex_rows(row_op[0, 0], row_op[0, 1], main[0], main[1])
    out[0, 0] = out_re.astype(BF16)
    out[0, 1] = out_im.astype(BF16)


def forward_inner(main, row_op):
    _, rows, width = main.shape
    inner = rows // EDGE - 2
    deep = row_op.shape[3]
    return pl.pallas_call(
        forward_inner_kernel,
        out_shape=jax.ShapeDtypeStruct((1,) + main.shape, BF16),
        grid=(width // WIDE, inner),
        in_specs=[
            pl.BlockSpec((2, rows, WIDE), lambda j, i: (0, 0, j)),
            pl.BlockSpec((1, 2, EDGE, deep), lambda j, i: (0, 0, i, 0)),
        ],
        out_specs=pl.BlockSpec((1, 2, EDGE, WIDE), lambda j, i: (0, 0, i + 1, j)),
        compiler_params=params(),
        cost_estimate=cost(8 * inner * EDGE * width * rows, 8 * rows * width),
        name="forward_inner",
    )(main, row_op)


def forward_edge_kernel(top, main, bottom, edge_op, whole, out):
    side = pl.program_id(1)

    def run(m_re, m_im):
        out_re, out_im = complex_rows(edge_op[0, 0], edge_op[0, 1], m_re, m_im)
        out[0, 0] = out_re.astype(BF16)
        out[0, 1] = out_im.astype(BF16)

    @pl.when(side == 0)
    def _():
        run(*[jnp.concatenate([top[p], main[p]], axis=0) for p in range(2)])

    @pl.when(side == 1)
    def _():
        run(*[jnp.concatenate([main[p], bottom[p]], axis=0) for p in range(2)])


def forward_edges(top, main, bottom, edge_op, whole):
    _, rows, width = main.shape
    wide = 2 * WIDE
    near = rows // (2 * EDGE) - 1
    far = rows // EDGE - 1
    halo = pl.BlockSpec((2, EDGE, wide), lambda j, i: (0, 0, j))
    return pl.pallas_call(
        forward_edge_kernel,
        out_shape=jax.ShapeDtypeStruct(whole.shape, BF16),
        grid=(width // wide, 2),
        in_specs=[
            halo,
            pl.BlockSpec((2, 2 * EDGE, wide), lambda j, i: (0, i * near, j)),
            halo,
            pl.BlockSpec((1, 2, EDGE, edge_op.shape[3]), lambda j, i: (i, 0, 0, 0)),
            pl.BlockSpec(memory_space=pl.ANY),
        ],
        out_specs=pl.BlockSpec((1, 2, EDGE, wide), lambda j, i: (0, 0, i * far, j)),
        input_output_aliases={4: 0},
        compiler_params=params(),
        cost_estimate=cost(16 * EDGE * width * edge_op.shape[3], 24 * EDGE * width),
        name="forward_edges",
    )(top, main, bottom, edge_op, whole)


def gradient_of(coef, terms, other, rows):
    return (coef[0] * terms[1, rows].astype(F32) - coef[1] * terms[0, rows].astype(F32)) + (
        coef[2] * other[1, rows].astype(F32) - coef[3] * other[0, rows].astype(F32)
    )


def turned(phase, f_re, f_im):
    sine, cosine = sincos(phase)
    f_re, f_im = f_re.astype(F32), f_im.astype(F32)
    return (cosine * f_re - sine * f_im).astype(BF16), (sine * f_re + cosine * f_im).astype(BF16)


def ring_edge_kernel(coef, terms, other, p_top, p_bottom, f_top, f_bottom, op_ref, first, last, ring):
    step = pl.program_id(0)

    @pl.when(step == 0)
    def _():
        ring[3] = jnp.zeros(ring.shape[1:], BF16)

    left, mid, right = (step + 1) % 4, (step + 2) % 4, (step + 3) % 4

    def part(k):
        return jnp.concatenate(
            [ring[left, k, :, WIDE - EDGE :], ring[mid, k], ring[right, k, :, :EDGE]], axis=1
        )

    out_re, out_im = column_product(part(0), part(1), op_ref, False)
    first[0] = out_re[:EDGE]
    first[1] = out_im[:EDGE]
    last[0] = out_re[EDGE:]
    last[1] = out_im[EDGE:]
    for i, (phase, fwd) in enumerate(((p_top, f_top), (p_bottom, f_bottom))):
        span = slice(i * EDGE, (i + 1) * EDGE)
        updated = phase[0] - gradient_of(coef, terms, other, span)
        l_re, l_im = turned(updated, fwd[0, 0], fwd[0, 1])
        ring[step % 4, 0, span] = l_re
        ring[step % 4, 1, span] = l_im


def ring_edges(coef, terms, other, phases, forward, op):
    _, _, rows, width = forward.shape
    groups = width // WIDE
    half = phases.shape[2] // WIDE
    far = rows // EDGE - 1

    def chunk(j):
        return jnp.minimum(j, groups - 1)

    tile = pl.BlockSpec((2, 2 * EDGE, WIDE), lambda j, c: (0, 0, chunk(j)))
    out = pl.BlockSpec((2, EDGE, WIDE), lambda j, c: (0, 0, jnp.maximum(j - 2, 0)))
    shape = jax.ShapeDtypeStruct((2, EDGE, width), BF16)
    return pl.pallas_call(
        ring_edge_kernel,
        out_shape=(shape, shape),
        grid_spec=pltpu.PrefetchScalarGridSpec(
            num_scalar_prefetch=1,
            grid=(groups + 2,),
            in_specs=[
                tile,
                tile,
                pl.BlockSpec((1, EDGE, WIDE), lambda j, c: (chunk(j) // half, 0, chunk(j) % half)),
                pl.BlockSpec((1, EDGE, WIDE), lambda j, c: (chunk(j) // half, far, chunk(j) % half)),
                pl.BlockSpec((1, 2, EDGE, WIDE), lambda j, c: (0, 0, 0, chunk(j))),
                pl.BlockSpec((1, 2, EDGE, WIDE), lambda j, c: (0, 0, far, chunk(j))),
                pl.BlockSpec((1, 2, op.shape[2], WIDE), lambda j, c: (jnp.maximum(j - 2, 0), 0, 0, 0)),
            ],
            out_specs=(out, out),
            scratch_shapes=[pltpu.VMEM((4, 2, 2 * EDGE, WIDE), BF16)],
        ),
        compiler_params=params(),
        cost_estimate=cost(16 * EDGE * width * op.shape[2], 24 * EDGE * width),
        name="ring_edges",
    )(coef, terms, other, phases, phases, forward, forward, op)


def launch_split_kernel(coef, t_in, o_in, t_edge, o_edge, phase, fwd, launched, phase_next):
    rows = phase.shape[1]
    pieces = (
        (t_edge, o_edge, slice(0, EDGE), slice(0, EDGE)),
        (t_in, o_in, slice(0, rows - 2 * EDGE), slice(EDGE, rows - EDGE)),
        (t_edge, o_edge, slice(EDGE, 2 * EDGE), slice(rows - EDGE, rows)),
    )
    for terms, other, span, place in pieces:
        updated = phase[0, place] - gradient_of(coef, terms, other, span)
        phase_next[0, place] = updated
        l_re, l_im = turned(updated, fwd[0, 0, place], fwd[0, 1, place])
        launched[0, place] = l_re
        launched[1, place] = l_im


def launch_split(coef, t_in, o_in, t_edge, o_edge, phases, forward):
    _, _, rows, width = forward.shape
    half = phases.shape[2] // WIDE
    inner = pl.BlockSpec((2, rows - 2 * EDGE, WIDE), lambda j, c: (0, 0, j))
    edge = pl.BlockSpec((2, 2 * EDGE, WIDE), lambda j, c: (0, 0, j))
    plane = pl.BlockSpec((1, rows, WIDE), lambda j, c: (j // half, 0, j % half))
    return pl.pallas_call(
        launch_split_kernel,
        out_shape=(
            jax.ShapeDtypeStruct(forward.shape[1:], BF16),
            jax.ShapeDtypeStruct(phases.shape, F32),
        ),
        grid_spec=pltpu.PrefetchScalarGridSpec(
            num_scalar_prefetch=1,
            grid=(width // WIDE,),
            in_specs=[
                inner,
                inner,
                edge,
                edge,
                plane,
                pl.BlockSpec((1, 2, rows, WIDE), lambda j, c: (0, 0, 0, j)),
            ],
            out_specs=(pl.BlockSpec((2, rows, WIDE), lambda j, c: (0, 0, j)), plane),
        ),
        compiler_params=params(),
        cost_estimate=cost(60 * rows * width, 24 * rows * width),
        name="launch",
    )(coef, t_in, o_in, t_edge, o_edge, phases, forward)


PAD = EDGE
MESH = pl.DeviceIdType.MESH


def band_rows(offs, blk, first, base, group, part, total):
    zero = jnp.zeros((BLK, BLK), F32)
    strips = []
    for r in range(group):
        row = base + r
        own = [blk[part, first + r, k].astype(F32) for k in range(blk.shape[2])]
        pieces = [zero] * r
        for d in range(2 * RADIUS + 1):
            place = row + (d - RADIUS)
            inside = (place >= 0) & (place < total)
            piece = zero
            for k, block in enumerate(own):
                piece = jnp.where(inside & (offs[row, k] == d - RADIUS), block, piece)
            pieces.append(piece)
        pieces += [zero] * (group - 1 - r)
        strips.append(jnp.concatenate(pieces, axis=1))
    return jnp.concatenate(strips, axis=0)


def stacked(re, im):
    return jnp.concatenate(
        [jnp.concatenate([re, -im], axis=1), jnp.concatenate([im, re], axis=1)], axis=0
    ).astype(BF16)


def exchange_kernel(
    tiles, offs, blocks, adjoint, forward, phase,
    mid, lau, t_in, o_in, phases, updated, halo2, rin_out, red_out,
    halo1, col_op, rin, red, lit_e, te, oe, ends, sums, slots, coef,
    ph_sem, s1, r1, ti_sem, te_s, te_r, ar_s, ar_r, s2, r2, loc_sem,
):
    d = lax.axis_index("design")
    t = lax.axis_index("tile")
    m = lax.axis_index("mode")
    peers = 2 * tiles
    me = 2 * t + m
    nxt, prv = lax.rem(t + 1, tiles), lax.rem(t + tiles - 1, tiles)
    rows, width = adjoint.shape[1], adjoint.shape[2]
    groups = width // WIDE
    total = blocks.shape[1]
    own_rows = total // tiles
    has_next, has_prev = t < tiles - 1, t > 0

    def device(tile, mode):
        return {"tile": tile, "mode": mode}

    def peer(p):
        who = lax.rem(me + p, peers)
        return device(who // 2, lax.rem(who, 2))

    barrier = pltpu.get_barrier_semaphore()
    for p in range(1, peers):
        pl.semaphore_signal(barrier, inc=1, device_id=peer(p), device_id_type=MESH)
    pl.semaphore_wait(barrier, peers - 1)

    def remote(src, dst, send, recv, tile, mode):
        return pltpu.make_async_remote_copy(
            src_ref=src, dst_ref=dst, send_sem=send, recv_sem=recv,
            device_id=device(tile, mode), device_id_type=MESH,
        )

    def cols(c, lead=0, wide=WIDE):
        return pl.ds(pl.multiple_of(c * WIDE + lead, 128), wide)

    def down1(c):
        return remote(
            adjoint.at[:, pl.ds(rows - EDGE, EDGE), cols(c)],
            halo1.at[0, :, :, cols(c, PAD)], s1.at[0, c], r1.at[0, c], nxt, m)

    def up1(c):
        return remote(
            adjoint.at[:, pl.ds(0, EDGE), cols(c)],
            halo1.at[1, :, :, cols(c, PAD)], s1.at[1, c], r1.at[1, c], prv, m)

    def down2(c):
        return remote(
            ends.at[1, :, :, cols(c)], halo2.at[0, :, :, cols(c)],
            s2.at[0, c], r2.at[0, c], nxt, m)

    def up2(c):
        return remote(
            ends.at[0, :, :, cols(c)], halo2.at[1, :, :, cols(c)],
            s2.at[1, c], r2.at[1, c], prv, m)

    def each(n, fn):
        def step(c, carry):
            fn(c)
            return carry
        lax.fori_loop(0, n, step, 0)

    @pl.when(has_next)
    def _():
        each(groups, lambda c: down1(c).start())

    @pl.when(has_prev)
    def _():
        each(groups, lambda c: up1(c).start())

    share = remote(phase, phases.at[m], ph_sem.at[0], ph_sem.at[1], t, 1 - m)
    share.start()

    halo1[:, :, :, 0:PAD] = jnp.zeros((2, 2, EDGE, PAD), BF16)
    halo1[:, :, :, PAD + width : PAD + width + PAD] = jnp.zeros((2, 2, EDGE, PAD), BF16)
    sums[...] = jnp.zeros_like(sums)

    def blank(side):
        def step(c, carry):
            halo1[side, :, :, cols(c, PAD)] = jnp.zeros((2, EDGE, WIDE), BF16)
            return carry
        lax.fori_loop(0, groups, step, 0)
        copy = pltpu.make_async_copy(halo1.at[side, :, :, pl.ds(PAD, width)], halo2.at[side], loc_sem.at[0])
        copy.start()
        copy.wait()

    @pl.when(t == 0)
    def _():
        blank(0)

    @pl.when(t == tiles - 1)
    def _():
        blank(1)

    def build_columns(blk):
        g = pl.program_id(0)
        for part in range(2):
            full = band_rows(offs, blk, 0, g * (WIDE // BLK), WIDE // BLK, part, total)
            col_op[g, part] = full.T.astype(BF16)

    pltpu.emit_pipeline(
        build_columns, grid=(groups,),
        in_specs=[pl.BlockSpec((2, WIDE // BLK, blocks.shape[2], BLK, BLK), lambda g: (0, g, 0, 0, 0))],
    )(blocks)

    def build_rows(blk):
        base = t * own_rows
        inner = own_rows - 2 * RADIUS
        rin[...] = stacked(*[band_rows(offs, blk, RADIUS, base + RADIUS, inner, p, total) for p in range(2)])
        red[0] = stacked(*[band_rows(offs, blk, 0, base, RADIUS, p, total) for p in range(2)])
        low = own_rows - RADIUS
        red[1] = stacked(*[band_rows(offs, blk, low, base + low, RADIUS, p, total) for p in range(2)])

    pltpu.emit_pipeline(
        build_rows, grid=(1,),
        in_specs=[pl.BlockSpec((2, own_rows, blocks.shape[2], BLK, BLK), lambda g: (0, t, 0, 0, 0))],
    )(blocks)
    rin_copy = pltpu.make_async_copy(rin, rin_out, loc_sem.at[1])
    red_copy = pltpu.make_async_copy(red, red_out, loc_sem.at[2])
    rin_copy.start()
    red_copy.start()

    tile = pl.BlockSpec((2, rows, WIDE), lambda j: (0, 0, j))

    def columns(conj):
        def run(left, middle, right, out):
            j = pl.program_id(0)
            op_re, op_im = col_op[j, 0], col_op[j, 1]
            x_re, x_im = window(left, middle, right, 0), window(left, middle, right, 1)
            rr, ii = dot(x_re, op_re), dot(x_im, op_im)
            ri, ir = dot(x_re, op_im), dot(x_im, op_re)
            if conj:
                out[0], out[1] = (rr + ii).astype(BF16), (ri - ir).astype(BF16)
            else:
                out[0], out[1] = (rr - ii).astype(BF16), (ri + ir).astype(BF16)
        return pltpu.emit_pipeline(run, grid=(groups,), in_specs=window_specs(rows, groups), out_specs=[tile])

    columns(True)(adjoint, adjoint, adjoint, mid)

    half = phase.shape[1] // WIDE

    def keep(src, dst):
        dst[0] = src[...]

    pltpu.emit_pipeline(
        keep, grid=(half,),
        in_specs=[pl.BlockSpec((rows, WIDE), lambda j: (0, j))],
        out_specs=[pl.BlockSpec((1, rows, WIDE), lambda j: (m, 0, j))],
    )(phase, phases)
    share.wait()
    plane = pl.BlockSpec((1, rows, WIDE), lambda j: (j // half, 0, j % half))
    inner_tile = pl.BlockSpec((2, rows - 2 * EDGE, WIDE), lambda j: (0, 0, j))

    def count(sum_re, sum_im):
        tall = sum_re.shape[0]
        sums[0] += jnp.sum(sum_re.reshape(tall // 8, 8, WIDE), axis=0)
        sums[1] += jnp.sum(sum_im.reshape(tall // 8, 8, WIDE), axis=0)

    def product(both, lit_re, lit_im):
        tall = both.shape[0] // 2
        cj_re = both[:tall].astype(BF16).astype(F32)
        cj_im = both[tall:].astype(BF16).astype(F32)
        lit_re, lit_im = lit_re.astype(F32), lit_im.astype(F32)
        t_re = cj_re * lit_re - cj_im * lit_im
        t_im = cj_re * lit_im + cj_im * lit_re
        count(t_re, t_im)
        return t_re.astype(BF16), t_im.astype(BF16)

    def inner_terms(ph, fwd, main, out):
        j = pl.program_id(0)
        low, high = EDGE, rows - EDGE
        for i, (a, b) in enumerate(((0, EDGE), (high, rows))):
            lit_e[0, i * EDGE : (i + 1) * EDGE, cols(j)], lit_e[1, i * EDGE : (i + 1) * EDGE, cols(j)] = turned(
                ph[0, a:b], fwd[0, a:b], fwd[1, a:b])
        lit_re, lit_im = turned(ph[0, low:high], fwd[0, low:high], fwd[1, low:high])
        both = dot(rin[...], jnp.concatenate([main[0], main[1]], axis=0))
        out[0], out[1] = product(both, lit_re, lit_im)

    pltpu.emit_pipeline(
        inner_terms, grid=(groups,), in_specs=[plane, tile, tile], out_specs=[inner_tile],
    )(phases, forward, mid, t_in)

    swap_in = remote(t_in, o_in, ti_sem.at[0], ti_sem.at[1], t, 1 - m)
    swap_in.start()

    def swap_edge(c):
        return remote(te.at[:, :, cols(c)], oe.at[:, :, cols(c)], te_s.at[c], te_r.at[c], t, 1 - m)

    def arrived(c):
        @pl.when(has_prev)
        def _():
            down1(c).wait_recv()

        @pl.when(has_next)
        def _():
            up1(c).wait_recv()

    arrived(0)

    def edge_terms(main):
        j = pl.program_id(0)

        @pl.when(j < groups - 1)
        def _():
            arrived(j + 1)

        op_re, op_im = col_op[j, 0], col_op[j, 1]
        x = [jnp.concatenate([halo1[s, p, :, cols(j, 0, 2 * WIDE)] for s in range(2)], axis=0) for p in range(2)]
        rr, ii = dot(x[0], op_re), dot(x[1], op_im)
        ri, ir = dot(x[0], op_im), dot(x[1], op_re)
        h = ((rr + ii).astype(BF16), (ri - ir).astype(BF16))
        top = jnp.concatenate([h[0][:EDGE], main[0, : 2 * EDGE], h[1][:EDGE], main[1, : 2 * EDGE]], axis=0)
        low = rows - 2 * EDGE
        bottom = jnp.concatenate([main[0, low:], h[0][EDGE:], main[1, low:], h[1][EDGE:]], axis=0)
        for i, field in enumerate((top, bottom)):
            span = slice(i * EDGE, (i + 1) * EDGE)
            te[0, span, cols(j)], te[1, span, cols(j)] = product(
                dot(red[i], field), lit_e[0, span, cols(j)], lit_e[1, span, cols(j)])
        swap_edge(j).start()

    pltpu.emit_pipeline(edge_terms, grid=(groups,), in_specs=[tile])(mid)

    slots[me] = sums[:, :, :128] + sums[:, :, 128:]

    def report(p):
        who = peer(p)
        return pltpu.make_async_remote_copy(
            src_ref=slots.at[me], dst_ref=slots.at[me], send_sem=ar_s.at[p], recv_sem=ar_r.at[p],
            device_id=who, device_id_type=MESH)

    def heard(p):
        who = lax.rem(me + peers - p, peers)
        return pltpu.make_async_remote_copy(
            src_ref=slots.at[who], dst_ref=slots.at[who], send_sem=ar_s.at[p], recv_sem=ar_r.at[p],
            device_id=peer(p), device_id_type=MESH)

    for p in range(1, peers):
        report(p).start()
    for p in range(1, peers):
        heard(p).wait_recv()
    for i, who in enumerate((m, 1 - m)):
        value = slots[who]
        for k in range(1, tiles):
            value = value + slots[2 * k + who]
        for part in range(2):
            coef[2 * i + part] = jnp.sum(value[part]) * (1.0 / (4.0 * width * 2))

    def gradient(own_re, own_im, other_re, other_im):
        return (coef[0] * own_im.astype(F32) - coef[1] * own_re.astype(F32)) + (
            coef[2] * other_im.astype(F32) - coef[3] * other_re.astype(F32))

    far = rows // EDGE - 1

    def chunk(j):
        return jnp.minimum(j, groups - 1)

    def edge_launch(p_top, p_bottom, f_top, f_bottom):
        j = pl.program_id(0)

        @pl.when(j < groups)
        def _():
            swap_edge(j).wait_recv()
            for i, (ph, fwd) in enumerate(((p_top, f_top), (p_bottom, f_bottom))):
                span = slice(i * EDGE, (i + 1) * EDGE)
                after = ph[0] - gradient(te[0, span, cols(j)], te[1, span, cols(j)],
                                         oe[0, span, cols(j)], oe[1, span, cols(j)])
                halo1[i, 0, :, cols(j, PAD)], halo1[i, 1, :, cols(j, PAD)] = turned(after, fwd[0], fwd[1])

        @pl.when(j > 0)
        def _():
            g = j - 1
            op_re, op_im = col_op[g, 0], col_op[g, 1]
            x = [jnp.concatenate([halo1[s, p, :, cols(g, 0, 2 * WIDE)] for s in range(2)], axis=0) for p in range(2)]
            rr, ii = dot(x[0], op_re), dot(x[1], op_im)
            ri, ir = dot(x[0], op_im), dot(x[1], op_re)
            o_re, o_im = (rr - ii).astype(BF16), (ri + ir).astype(BF16)
            for s in range(2):
                ends[s, 0, :, cols(g)] = o_re[s * EDGE : (s + 1) * EDGE]
                ends[s, 1, :, cols(g)] = o_im[s * EDGE : (s + 1) * EDGE]

            @pl.when(has_next)
            def _():
                down2(g).start()

            @pl.when(has_prev)
            def _():
                up2(g).start()

    pltpu.emit_pipeline(
        edge_launch, grid=(groups + 1,),
        in_specs=[
            pl.BlockSpec((1, EDGE, WIDE), lambda j: (chunk(j) // half, 0, chunk(j) % half)),
            pl.BlockSpec((1, EDGE, WIDE), lambda j: (chunk(j) // half, far, chunk(j) % half)),
            pl.BlockSpec((2, EDGE, WIDE), lambda j: (0, 0, chunk(j))),
            pl.BlockSpec((2, EDGE, WIDE), lambda j: (0, far, chunk(j))),
        ],
    )(phases, phases, forward, forward)

    swap_in.wait()

    def launch_tile(own, other, ph, fwd, out, after_out):
        j = pl.program_id(0)
        for k, (a, b) in enumerate(((0, EDGE), (EDGE, rows - EDGE), (rows - EDGE, rows))):
            if k == 1:
                grad = gradient(own[0], own[1], other[0], other[1])
            else:
                span = slice((k // 2) * EDGE, (k // 2 + 1) * EDGE)
                grad = gradient(te[0, span, cols(j)], te[1, span, cols(j)],
                                oe[0, span, cols(j)], oe[1, span, cols(j)])
            after = ph[0, a:b] - grad
            after_out[0, a:b] = after
            out[0, a:b], out[1, a:b] = turned(after, fwd[0, a:b], fwd[1, a:b])

    pltpu.emit_pipeline(
        launch_tile, grid=(groups,),
        in_specs=[inner_tile, inner_tile, plane, tile], out_specs=[tile, plane],
    )(t_in, o_in, phases, forward, lau, updated)

    columns(False)(lau, lau, lau, mid)

    rin_copy.wait()
    red_copy.wait()
    for p in range(1, peers):
        report(p).wait_send()
    each(groups, lambda c: swap_edge(c).wait_send())

    @pl.when(has_next)
    def _():
        each(groups, lambda c: down1(c).wait_send())
        each(groups, lambda c: down2(c).wait_send())
        each(groups, lambda c: up2(c).wait_recv())

    @pl.when(has_prev)
    def _():
        each(groups, lambda c: up1(c).wait_send())
        each(groups, lambda c: up2(c).wait_send())
        each(groups, lambda c: down2(c).wait_recv())


def exchange(forward, adjoint, phase, blocks, offsets):
    tiles = lax.axis_size("tile")
    _, rows, width = forward.shape
    half = phase.shape[1]
    groups = width // WIDE
    inner = rows - 2 * EDGE
    hbm = pl.BlockSpec(memory_space=pl.ANY)
    dma = pltpu.SemaphoreType.DMA
    field = jax.ShapeDtypeStruct((2, rows, width), BF16)
    plane = jax.ShapeDtypeStruct((2, rows, half), F32)
    rin = (2 * inner, 2 * rows)
    red = (2, 2 * EDGE, 6 * EDGE)
    shapes = (
        field, field,
        jax.ShapeDtypeStruct((2, inner, width), BF16),
        jax.ShapeDtypeStruct((2, inner, width), BF16),
        plane, plane,
        jax.ShapeDtypeStruct((2, 2, EDGE, width), BF16),
        jax.ShapeDtypeStruct(rin, BF16),
        jax.ShapeDtypeStruct(red, BF16),
    )
    edge = pltpu.VMEM((2, 2 * EDGE, width), BF16)
    peers = 2 * tiles
    out = pl.pallas_call(
        functools.partial(exchange_kernel, tiles),
        out_shape=shapes,
        in_specs=[pl.BlockSpec(memory_space=pltpu.SMEM)] + [hbm] * 4,
        out_specs=(hbm,) * len(shapes),
        scratch_shapes=[
            pltpu.VMEM((2, 2, EDGE, width + 2 * PAD), BF16),
            pltpu.VMEM((groups, 2, WIDE + 2 * EDGE, WIDE), BF16),
            pltpu.VMEM(rin, BF16),
            pltpu.VMEM(red, BF16),
            edge, edge, edge,
            pltpu.VMEM((2, 2, EDGE, width), BF16),
            pltpu.VMEM((2, 8, WIDE), F32),
            pltpu.VMEM((peers, 2, 8, 128), F32),
            pltpu.SMEM((4,), F32),
            dma((2,)), dma((2, groups)), dma((2, groups)), dma((2,)),
            dma((groups,)), dma((groups,)), dma((peers,)), dma((peers,)),
            dma((2, groups)), dma((2, groups)), dma((3,)),
        ],
        compiler_params=pltpu.CompilerParams(
            vmem_limit_bytes=56 * 1024 * 1024, collective_id=0, has_side_effects=True),
        cost_estimate=cost(50 * rows * width * 512, 100 * rows * width),
        name="exchange",
    )(offsets, blocks, adjoint, forward, phase)
    mid, updated, halo2, rin, red = out[0], out[5], out[6], out[7], out[8]
    return mid, updated, halo2, rin, red


def finish_kernel(which, top, main, bottom, rin, red, after, out, phase_next):
    rows = main.shape[1]
    phase_next[...] = after[0]
    low = rows - 2 * EDGE
    pieces = (
        (EDGE, rin[...], [main[0], main[1]]),
        (0, red[0], [top[0, 0], main[0, : 2 * EDGE], top[0, 1], main[1, : 2 * EDGE]]),
        (rows - EDGE, red[1], [main[0, low:], bottom[0, 0], main[1, low:], bottom[0, 1]]),
    )
    for start, op, parts in pieces:
        both = dot(op, jnp.concatenate(parts, axis=0)).astype(BF16)
        tall = both.shape[0] // 2
        out[0, 0, start : start + tall] = both[:tall]
        out[0, 1, start : start + tall] = both[tall:]


def finish(mode, mid, updated, halo2, rin, red):
    _, rows, width = mid.shape
    groups = width // WIDE
    narrow = updated.shape[2] // groups
    return pl.pallas_call(
        finish_kernel,
        out_shape=(
            jax.ShapeDtypeStruct((1,) + mid.shape, BF16),
            jax.ShapeDtypeStruct(updated.shape[1:], F32),
        ),
        grid_spec=pltpu.PrefetchScalarGridSpec(
            num_scalar_prefetch=1,
            grid=(groups,),
            in_specs=[
                pl.BlockSpec((1, 2, EDGE, WIDE), lambda j, w: (0, 0, 0, j)),
                pl.BlockSpec((2, rows, WIDE), lambda j, w: (0, 0, j)),
                pl.BlockSpec((1, 2, EDGE, WIDE), lambda j, w: (1, 0, 0, j)),
                pl.BlockSpec(rin.shape, lambda j, w: (0, 0)),
                pl.BlockSpec(red.shape, lambda j, w: (0, 0, 0)),
                pl.BlockSpec((1, rows, narrow), lambda j, w: (w[0], 0, j)),
            ],
            out_specs=(
                pl.BlockSpec((1, 2, rows, WIDE), lambda j, w: (0, 0, 0, j)),
                pl.BlockSpec((rows, narrow), lambda j, w: (0, j)),
            ),
        ),
        compiler_params=params(),
        cost_estimate=cost(8 * rows * width * 512, 16 * rows * width),
        name="finish",
    )(mode, halo2, mid, halo2, rin, red, updated)


def exchange_edges(first, last):
    tiles = lax.axis_size("tile")
    top = lax.ppermute(last, "tile", [(t, t + 1) for t in range(tiles - 1)])
    bottom = lax.ppermute(first, "tile", [(t + 1, t) for t in range(tiles - 1)])
    return top, bottom


def body(forward, adjoint_next, phase, blocks, offsets):
    block_total = offsets.shape[0]
    tiles = lax.axis_size("tile")
    modes = lax.axis_size("mode")
    mode = lax.axis_index("mode")
    rows, width = forward.shape[2], forward.shape[3]
    adjoint = adjoint_next[0]
    if modes == 2 and rows // BLK == 2 * RADIUS + WIDE // BLK:
        parts = exchange(forward[0], adjoint, phase, blocks, offsets)
        forward_next, phase_next = finish(mode.astype(jnp.int32)[None], *parts)
        return phase_next, forward_next
    top, bottom = exchange_edges(adjoint[:, :EDGE], adjoint[:, rows - EDGE :])
    phases = lax.all_gather(phase, "mode", axis=0, tiled=False)

    raw_index = jnp.arange(block_total, dtype=jnp.int32)[:, None] + offsets
    inside = (raw_index >= 0) & (raw_index < block_total)
    pos = jnp.where(inside, offsets + RADIUS, -1).astype(jnp.int32)
    own_blocks = block_total // tiles
    split = own_blocks == 2 * RADIUS + WIDE // BLK
    start = lax.axis_index("tile") * own_blocks
    column_op = build(blocks, pos, WIDE // BLK, True)
    own_part = lax.dynamic_slice_in_dim(blocks, start, own_blocks, 1)
    own_pos = lax.dynamic_slice_in_dim(pos, start, own_blocks, 0)
    if split:
        inner = slice(RADIUS, own_blocks - RADIUS)
        row_op = build(own_part[:, inner], own_pos[inner], WIDE // BLK, False)
        ends = [own_part[:, :RADIUS], own_part[:, own_blocks - RADIUS :]]
        end_pos = [own_pos[:RADIUS], own_pos[own_blocks - RADIUS :]]
        edge_op = build(jnp.concatenate(ends, 1), jnp.concatenate(end_pos, 0), RADIUS, False)
    else:
        row_op = build(own_part, own_pos, min(WIDE // BLK, own_blocks), False)

    back_middle = column_pass(adjoint, column_op, True)
    lit = light(phases, forward)
    swap = [(m, (m + 1) % modes) for m in range(modes)]
    if split:
        t_in, s_in = adjoint_inner(back_middle, row_op, lit)
        o_in = lax.ppermute(t_in, "mode", swap)
        terms, sums = adjoint_edges(top, bottom, column_op, back_middle, edge_op, lit, s_in)
    else:
        terms, sums = adjoint_rows(top, bottom, column_op, back_middle, row_op, lit)
    other = lax.ppermute(terms, "mode", swap)
    own = jnp.sum(sums, axis=(1, 2))
    table = jnp.where(jnp.arange(modes)[:, None] == mode, own[None, :], 0.0)
    table = lax.psum(table, ("tile", "mode"))
    order = jnp.where(mode == 0, table, table[::-1])
    coef = order.reshape(-1) * (1.0 / (4.0 * width * modes))

    if split:
        first, last = ring_edges(coef, terms, other, phases, forward, column_op)
        top, bottom = exchange_edges(first, last)
        launched, updated = launch_split(coef, t_in, o_in, terms, other, phases, forward)
    else:
        edges = launch_edges(coef, terms, other, phases, forward)
        edges = column_pass(edges, column_op, False)
        top, bottom = exchange_edges(edges[:, :EDGE], edges[:, EDGE:])
        launched, updated = launch(coef, terms, other, phases, forward)
    middle = column_pass(launched, column_op, False)
    phase_next = lax.dynamic_index_in_dim(updated, mode, 0, keepdims=False)
    if split:
        whole = forward_inner(middle, row_op)
        return phase_next, forward_edges(top, middle, bottom, edge_op, whole)
    return phase_next, forward_rows(top, middle, bottom, row_op)


def solution(mesh):
    placed = (
        P(("design", "mode"), None, "tile", None),
        P(("design", "mode"), None, "tile", None),
        P(("design", "tile"), "mode"),
        P(None, "design", None, None, None),
        P("design", None),
    )
    return jax.shard_map(
        body,
        mesh=mesh,
        in_specs=placed,
        out_specs=(P(("design", "tile"), "mode"), P(("design", "mode"), None, "tile", None)),
        check_vma=False,
    )
```

```python
import functools

import jax
import jax.numpy as jnp
from jax import lax
from jax.experimental import pallas as pl
from jax.experimental.pallas import tpu as pltpu
from jax.sharding import PartitionSpec as P

BLK = 64
RADIUS = 2
EDGE = RADIUS * BLK
WIDE = 256
VMEM_LIMIT = 44 * 1024 * 1024

F32 = jnp.float32
BF16 = jnp.bfloat16


def params():
    return pltpu.CompilerParams(vmem_limit_bytes=VMEM_LIMIT)


def cost(flops, moved):
    return pl.CostEstimate(flops=int(flops), bytes_accessed=int(moved), transcendentals=0)


def sincos(x):
    turns = jnp.round(x * 0.15915494309189535)
    r = x - turns * 6.28125
    r = r - turns * 1.935307179586232e-3
    z = r * r
    half_sine = r * (0.7071067690849304 + z * (-0.029462767764925957 + z * (
        0.00036827221629209816 + z * (-2.1885971364099532e-06 + z * 7.195012585725635e-09))))
    half_cosine = 1.4142135381698608 + z * (-0.17677634954452515 + z * (
        0.003682573325932026 + z * (-3.0612263799412176e-05 + z * 1.2788676428954204e-07)))
    return half_sine * half_cosine, 1.0 - half_sine * half_sine


def dot(a, b):
    return jnp.dot(a, b, preferred_element_type=F32)


def build_kernel(pos_ref, blk_ref, out_ref, *, group, transposed):
    base = pl.program_id(0) * group
    zero = jnp.zeros((BLK, BLK), F32)
    for part in range(2):
        strips = []
        for r in range(group):
            own = [blk_ref[part, r, k].astype(F32) for k in range(blk_ref.shape[2])]
            pieces = [zero] * r
            for d in range(2 * RADIUS + 1):
                piece = zero
                for k, block in enumerate(own):
                    piece = jnp.where(pos_ref[base + r, k] == d, block, piece)
                pieces.append(piece)
            pieces += [zero] * (group - 1 - r)
            strips.append(jnp.concatenate(pieces, axis=1))
        full = jnp.concatenate(strips, axis=0)
        if transposed:
            full = full.T
        out_ref[0, part] = full.astype(BF16)


def build(blocks, pos, group, transposed):
    _, rows, bands, _, _ = blocks.shape
    tall, wide = group * BLK, (group + 2 * RADIUS) * BLK
    if transposed:
        tall, wide = wide, tall
    count = rows // group
    return pl.pallas_call(
        functools.partial(build_kernel, group=group, transposed=transposed),
        out_shape=jax.ShapeDtypeStruct((count, 2, tall, wide), BF16),
        grid_spec=pltpu.PrefetchScalarGridSpec(
            num_scalar_prefetch=1,
            grid=(count,),
            in_specs=[pl.BlockSpec((2, group, bands, BLK, BLK), lambda g, p: (0, g, 0, 0, 0))],
            out_specs=pl.BlockSpec((1, 2, tall, wide), lambda g, p: (g, 0, 0, 0)),
        ),
        compiler_params=params(),
        cost_estimate=cost(0, 16 * rows * bands * BLK * BLK),
        name="build_operator",
    )(pos, blocks)


def window_specs(rows, groups):
    last = 2 * groups - 1
    return [
        pl.BlockSpec((2, rows, 128), lambda j: (0, 0, jnp.maximum(2 * j - 1, 0))),
        pl.BlockSpec((2, rows, WIDE), lambda j: (0, 0, j)),
        pl.BlockSpec((2, rows, 128), lambda j: (0, 0, jnp.minimum(2 * j + 2, last))),
    ]


def window(left, mid, right, part):
    return jnp.concatenate([left[part], mid[part], right[part]], axis=1)


def column_product(x_re, x_im, op_ref, conj):
    op_re, op_im = op_ref[0, 0], op_ref[0, 1]
    rr, ii = dot(x_re, op_re), dot(x_im, op_im)
    ri, ir = dot(x_re, op_im), dot(x_im, op_re)
    if conj:
        return (rr + ii).astype(BF16), (ri - ir).astype(BF16)
    return (rr - ii).astype(BF16), (ri + ir).astype(BF16)


def column_kernel(left, mid, right, op_ref, out_ref, *, conj):
    out_re, out_im = column_product(
        window(left, mid, right, 0), window(left, mid, right, 1), op_ref, conj
    )
    out_ref[0] = out_re
    out_ref[1] = out_im


def column_pass(field, op, conj):
    _, rows, width = field.shape
    groups = width // WIDE
    return pl.pallas_call(
        functools.partial(column_kernel, conj=conj),
        out_shape=jax.ShapeDtypeStruct(field.shape, BF16),
        grid=(groups,),
        in_specs=window_specs(rows, groups)
        + [pl.BlockSpec((1, 2, op.shape[2], WIDE), lambda j: (j, 0, 0, 0))],
        out_specs=pl.BlockSpec((2, rows, WIDE), lambda j: (0, 0, j)),
        compiler_params=params(),
        cost_estimate=cost(8 * rows * width * op.shape[2], 12 * rows * width + 2 * op.size),
        name="column_pass",
    )(field, field, field, op)


def row_groups(top, main, bottom, row_op):
    whole_re = jnp.concatenate([top[0], main[0], bottom[0]], axis=0)
    whole_im = jnp.concatenate([top[1], main[1], bottom[1]], axis=0)
    count, _, tall, deep = row_op.shape
    for i in range(count):
        m_re = whole_re[i * tall : i * tall + deep]
        m_im = whole_im[i * tall : i * tall + deep]
        op_re, op_im = row_op[i, 0], row_op[i, 1]
        out_re = dot(op_re, m_re) - dot(op_im, m_im)
        out_im = dot(op_re, m_im) + dot(op_im, m_re)
        yield i * tall, tall, out_re, out_im


def adjoint_row_kernel(tl, tm, tr, bl, bm, br, op_ref, main, row_op, lit, terms, sums):
    x_re = jnp.concatenate([window(tl, tm, tr, 0), window(bl, bm, br, 0)], axis=0)
    x_im = jnp.concatenate([window(tl, tm, tr, 1), window(bl, bm, br, 1)], axis=0)
    halo_re, halo_im = column_product(x_re, x_im, op_ref, True)

    @pl.when(pl.program_id(0) == 0)
    def _():
        sums[...] = jnp.zeros_like(sums)

    top = (halo_re[:EDGE], halo_im[:EDGE])
    bottom = (halo_re[EDGE:], halo_im[EDGE:])
    for low, tall, cj_re, cj_im in row_groups(top, main, bottom, row_op):
        cj_re = cj_re.astype(BF16).astype(F32)
        cj_im = cj_im.astype(BF16).astype(F32)
        lit_re = lit[0, low : low + tall].astype(F32)
        lit_im = lit[1, low : low + tall].astype(F32)
        t_re = cj_re * lit_re - cj_im * lit_im
        t_im = cj_re * lit_im + cj_im * lit_re
        terms[0, low : low + tall] = t_re.astype(BF16)
        terms[1, low : low + tall] = t_im.astype(BF16)
        sums[0] += jnp.sum(t_re.reshape(tall // 8, 8, WIDE), axis=0)
        sums[1] += jnp.sum(t_im.reshape(tall // 8, 8, WIDE), axis=0)


def adjoint_rows(top, bottom, op, main, row_op, lit):
    _, rows, width = main.shape
    groups = width // WIDE
    edge = window_specs(EDGE, groups)
    tile = pl.BlockSpec((2, rows, WIDE), lambda j: (0, 0, j))
    return pl.pallas_call(
        adjoint_row_kernel,
        out_shape=(
            jax.ShapeDtypeStruct(main.shape, BF16),
            jax.ShapeDtypeStruct((2, 8, WIDE), F32),
        ),
        grid=(groups,),
        in_specs=edge
        + edge
        + [
            pl.BlockSpec((1, 2, op.shape[2], WIDE), lambda j: (j, 0, 0, 0)),
            tile,
            pl.BlockSpec(row_op.shape, lambda j: (0, 0, 0, 0)),
            tile,
        ],
        out_specs=(tile, pl.BlockSpec((2, 8, WIDE), lambda j: (0, 0, 0))),
        compiler_params=params(),
        cost_estimate=cost(12 * rows * width * op.shape[2], 16 * rows * width),
        name="adjoint_rows",
    )(top, top, top, bottom, bottom, bottom, op, main, row_op, lit)


def forward_row_kernel(top, main, bottom, row_op, out):
    for low, tall, out_re, out_im in row_groups(top, main, bottom, row_op):
        out[0, 0, low : low + tall] = out_re.astype(BF16)
        out[0, 1, low : low + tall] = out_im.astype(BF16)


def forward_rows(top, main, bottom, row_op):
    _, rows, width = main.shape
    groups = width // WIDE
    edge = pl.BlockSpec((2, EDGE, WIDE), lambda j: (0, 0, j))
    return pl.pallas_call(
        forward_row_kernel,
        out_shape=jax.ShapeDtypeStruct((1,) + main.shape, BF16),
        grid=(groups,),
        in_specs=[
            edge,
            pl.BlockSpec((2, rows, WIDE), lambda j: (0, 0, j)),
            edge,
            pl.BlockSpec(row_op.shape, lambda j: (0, 0, 0, 0)),
        ],
        out_specs=pl.BlockSpec((1, 2, rows, WIDE), lambda j: (0, 0, 0, j)),
        compiler_params=params(),
        cost_estimate=cost(8 * rows * width * row_op.shape[3], 10 * rows * width),
        name="forward_rows",
    )(top, main, bottom, row_op)


def lit_kernel(phase, fwd, lit):
    sine, cosine = sincos(phase[0])
    f_re, f_im = fwd[0, 0].astype(F32), fwd[0, 1].astype(F32)
    lit[0] = (cosine * f_re - sine * f_im).astype(BF16)
    lit[1] = (sine * f_re + cosine * f_im).astype(BF16)


def light(phases, forward):
    _, _, rows, width = forward.shape
    half = phases.shape[2] // WIDE
    return pl.pallas_call(
        lit_kernel,
        out_shape=jax.ShapeDtypeStruct(forward.shape[1:], BF16),
        grid=(width // WIDE,),
        in_specs=[
            pl.BlockSpec((1, rows, WIDE), lambda j: (j // half, 0, j % half)),
            pl.BlockSpec((1, 2, rows, WIDE), lambda j: (0, 0, 0, j)),
        ],
        out_specs=pl.BlockSpec((2, rows, WIDE), lambda j: (0, 0, j)),
        compiler_params=params(),
        cost_estimate=cost(60 * rows * width, 12 * rows * width),
        name="light",
    )(phases, forward)


def launch_values(coef, terms, other, phase, fwd, launched):
    gradient = (coef[0] * terms[1].astype(F32) - coef[1] * terms[0].astype(F32)) + (
        coef[2] * other[1].astype(F32) - coef[3] * other[0].astype(F32)
    )
    updated = phase[0] - gradient
    sine, cosine = sincos(updated)
    f_re, f_im = fwd[0, 0].astype(F32), fwd[0, 1].astype(F32)
    launched[0] = (cosine * f_re - sine * f_im).astype(BF16)
    launched[1] = (sine * f_re + cosine * f_im).astype(BF16)
    return updated


def launch_kernel(coef, terms, other, phase, fwd, launched, phase_next):
    phase_next[0] = launch_values(coef, terms, other, phase, fwd, launched)


def launch(coef, terms, other, phases, forward):
    _, _, rows, width = forward.shape
    half = phases.shape[2] // WIDE
    tile = pl.BlockSpec((2, rows, WIDE), lambda j, c: (0, 0, j))
    plane = pl.BlockSpec((1, rows, WIDE), lambda j, c: (j // half, 0, j % half))
    return pl.pallas_call(
        launch_kernel,
        out_shape=(
            jax.ShapeDtypeStruct(forward.shape[1:], BF16),
            jax.ShapeDtypeStruct(phases.shape, F32),
        ),
        grid_spec=pltpu.PrefetchScalarGridSpec(
            num_scalar_prefetch=1,
            grid=(width // WIDE,),
            in_specs=[
                tile,
                tile,
                plane,
                pl.BlockSpec((1, 2, rows, WIDE), lambda j, c: (0, 0, 0, j)),
            ],
            out_specs=(tile, plane),
        ),
        compiler_params=params(),
        cost_estimate=cost(60 * rows * width, 24 * rows * width),
        name="launch",
    )(coef, terms, other, phases, forward)


def launch_edge_kernel(coef, terms, other, phase, fwd, launched):
    launch_values(coef, terms, other, phase, fwd, launched)


def launch_edges(coef, terms, other, phases, forward):
    _, _, rows, width = forward.shape
    wide = 2 * WIDE
    half = phases.shape[2] // wide
    far = rows // EDGE - 1
    tile = pl.BlockSpec((2, EDGE, wide), lambda e, j, c: (0, e * far, j))
    return pl.pallas_call(
        launch_edge_kernel,
        out_shape=jax.ShapeDtypeStruct((2, 2 * EDGE, width), BF16),
        grid_spec=pltpu.PrefetchScalarGridSpec(
            num_scalar_prefetch=1,
            grid=(2, width // wide),
            in_specs=[
                tile,
                tile,
                pl.BlockSpec((1, EDGE, wide), lambda e, j, c: (j // half, e * far, j % half)),
                pl.BlockSpec((1, 2, EDGE, wide), lambda e, j, c: (0, 0, e * far, j)),
            ],
            out_specs=pl.BlockSpec((2, EDGE, wide), lambda e, j, c: (0, e, j)),
        ),
        compiler_params=params(),
        cost_estimate=cost(120 * EDGE * width, 48 * EDGE * width),
        name="launch_edges",
    )(coef, terms, other, phases, forward)


def complex_rows(op_re, op_im, m_re, m_im):
    return dot(op_re, m_re) - dot(op_im, m_im), dot(op_re, m_im) + dot(op_im, m_re)


def add_terms(cj_re, cj_im, lit_re, lit_im, terms, sums, low):
    tall = cj_re.shape[0]
    cj_re = cj_re.astype(BF16).astype(F32)
    cj_im = cj_im.astype(BF16).astype(F32)
    lit_re, lit_im = lit_re.astype(F32), lit_im.astype(F32)
    t_re = cj_re * lit_re - cj_im * lit_im
    t_im = cj_re * lit_im + cj_im * lit_re
    terms[0, low : low + tall] = t_re.astype(BF16)
    terms[1, low : low + tall] = t_im.astype(BF16)
    sums[0] += jnp.sum(t_re.reshape(tall // 8, 8, WIDE), axis=0)
    sums[1] += jnp.sum(t_im.reshape(tall // 8, 8, WIDE), axis=0)


def adjoint_inner_kernel(main, row_op, lit, terms, sums):
    @pl.when(pl.program_id(0) == 0)
    def _():
        sums[...] = jnp.zeros_like(sums)

    rows = main.shape[1]
    cj_re, cj_im = complex_rows(row_op[0, 0], row_op[0, 1], main[0], main[1])
    add_terms(cj_re, cj_im, lit[0, EDGE : rows - EDGE], lit[1, EDGE : rows - EDGE], terms, sums, 0)


def adjoint_inner(main, row_op, lit):
    _, rows, width = main.shape
    inner = rows - 2 * EDGE
    tile = pl.BlockSpec((2, rows, WIDE), lambda j: (0, 0, j))
    return pl.pallas_call(
        adjoint_inner_kernel,
        out_shape=(
            jax.ShapeDtypeStruct((2, inner, width), BF16),
            jax.ShapeDtypeStruct((2, 8, WIDE), F32),
        ),
        grid=(width // WIDE,),
        in_specs=[tile, pl.BlockSpec(row_op.shape, lambda j: (0, 0, 0, 0)), tile],
        out_specs=(
            pl.BlockSpec((2, inner, WIDE), lambda j: (0, 0, j)),
            pl.BlockSpec((2, 8, WIDE), lambda j: (0, 0, 0)),
        ),
        compiler_params=params(),
        cost_estimate=cost(8 * inner * width * rows, 12 * rows * width),
        name="adjoint_inner",
    )(main, row_op, lit)


def edge_windows(main, part, top, bottom):
    rows = main.shape[1]
    return (
        jnp.concatenate([top, main[part, : 2 * EDGE]], axis=0),
        jnp.concatenate([main[part, rows - 2 * EDGE :], bottom], axis=0),
    )


def adjoint_edge_kernel(tl, tm, tr, bl, bm, br, op_ref, main, edge_op, lit, before, terms, sums):
    x_re = jnp.concatenate([window(tl, tm, tr, 0), window(bl, bm, br, 0)], axis=0)
    x_im = jnp.concatenate([window(tl, tm, tr, 1), window(bl, bm, br, 1)], axis=0)
    halo_re, halo_im = column_product(x_re, x_im, op_ref, True)

    @pl.when(pl.program_id(0) == 0)
    def _():
        sums[...] = before[...]

    rows = main.shape[1]
    res = edge_windows(main, 0, halo_re[:EDGE], halo_re[EDGE:])
    ims = edge_windows(main, 1, halo_im[:EDGE], halo_im[EDGE:])
    for i, low in enumerate((0, rows - EDGE)):
        cj_re, cj_im = complex_rows(edge_op[i, 0], edge_op[i, 1], res[i], ims[i])
        add_terms(cj_re, cj_im, lit[0, low : low + EDGE], lit[1, low : low + EDGE], terms, sums, i * EDGE)


def adjoint_edges(top, bottom, op, main, edge_op, lit, before):
    _, rows, width = main.shape
    groups = width // WIDE
    edge = window_specs(EDGE, groups)
    tile = pl.BlockSpec((2, rows, WIDE), lambda j: (0, 0, j))
    return pl.pallas_call(
        adjoint_edge_kernel,
        out_shape=(
            jax.ShapeDtypeStruct((2, 2 * EDGE, width), BF16),
            jax.ShapeDtypeStruct((2, 8, WIDE), F32),
        ),
        grid=(groups,),
        in_specs=edge
        + edge
        + [
            pl.BlockSpec((1, 2, op.shape[2], WIDE), lambda j: (j, 0, 0, 0)),
            tile,
            pl.BlockSpec(edge_op.shape, lambda j: (0, 0, 0, 0)),
            tile,
            pl.BlockSpec((2, 8, WIDE), lambda j: (0, 0, 0)),
        ],
        out_specs=(
            pl.BlockSpec((2, 2 * EDGE, WIDE), lambda j: (0, 0, j)),
            pl.BlockSpec((2, 8, WIDE), lambda j: (0, 0, 0)),
        ),
        compiler_params=params(),
        cost_estimate=cost(32 * EDGE * width * op.shape[2], 16 * rows * width),
        name="adjoint_edges",
    )(top, top, top, bottom, bottom, bottom, op, main, edge_op, lit, before)


def forward_inner_kernel(main, row_op, out):
    out_re, out_im = complex_rows(row_op[0, 0], row_op[0, 1], main[0], main[1])
    out[0, 0] = out_re.astype(BF16)
    out[0, 1] = out_im.astype(BF16)


def forward_inner(main, row_op):
    _, rows, width = main.shape
    inner = rows // EDGE - 2
    deep = row_op.shape[3]
    return pl.pallas_call(
        forward_inner_kernel,
        out_shape=jax.ShapeDtypeStruct((1,) + main.shape, BF16),
        grid=(width // WIDE, inner),
        in_specs=[
            pl.BlockSpec((2, rows, WIDE), lambda j, i: (0, 0, j)),
            pl.BlockSpec((1, 2, EDGE, deep), lambda j, i: (0, 0, i, 0)),
        ],
        out_specs=pl.BlockSpec((1, 2, EDGE, WIDE), lambda j, i: (0, 0, i + 1, j)),
        compiler_params=params(),
        cost_estimate=cost(8 * inner * EDGE * width * rows, 8 * rows * width),
        name="forward_inner",
    )(main, row_op)


def forward_edge_kernel(top, main, bottom, edge_op, whole, out):
    side = pl.program_id(1)

    def run(m_re, m_im):
        out_re, out_im = complex_rows(edge_op[0, 0], edge_op[0, 1], m_re, m_im)
        out[0, 0] = out_re.astype(BF16)
        out[0, 1] = out_im.astype(BF16)

    @pl.when(side == 0)
    def _():
        run(*[jnp.concatenate([top[p], main[p]], axis=0) for p in range(2)])

    @pl.when(side == 1)
    def _():
        run(*[jnp.concatenate([main[p], bottom[p]], axis=0) for p in range(2)])


def forward_edges(top, main, bottom, edge_op, whole):
    _, rows, width = main.shape
    wide = 2 * WIDE
    near = rows // (2 * EDGE) - 1
    far = rows // EDGE - 1
    halo = pl.BlockSpec((2, EDGE, wide), lambda j, i: (0, 0, j))
    return pl.pallas_call(
        forward_edge_kernel,
        out_shape=jax.ShapeDtypeStruct(whole.shape, BF16),
        grid=(width // wide, 2),
        in_specs=[
            halo,
            pl.BlockSpec((2, 2 * EDGE, wide), lambda j, i: (0, i * near, j)),
            halo,
            pl.BlockSpec((1, 2, EDGE, edge_op.shape[3]), lambda j, i: (i, 0, 0, 0)),
            pl.BlockSpec(memory_space=pl.ANY),
        ],
        out_specs=pl.BlockSpec((1, 2, EDGE, wide), lambda j, i: (0, 0, i * far, j)),
        input_output_aliases={4: 0},
        compiler_params=params(),
        cost_estimate=cost(16 * EDGE * width * edge_op.shape[3], 24 * EDGE * width),
        name="forward_edges",
    )(top, main, bottom, edge_op, whole)


def gradient_of(coef, terms, other, rows):
    return (coef[0] * terms[1, rows].astype(F32) - coef[1] * terms[0, rows].astype(F32)) + (
        coef[2] * other[1, rows].astype(F32) - coef[3] * other[0, rows].astype(F32)
    )


def turned(phase, f_re, f_im):
    sine, cosine = sincos(phase)
    f_re, f_im = f_re.astype(F32), f_im.astype(F32)
    return (cosine * f_re - sine * f_im).astype(BF16), (sine * f_re + cosine * f_im).astype(BF16)


def ring_edge_kernel(coef, terms, other, p_top, p_bottom, f_top, f_bottom, op_ref, first, last, ring):
    step = pl.program_id(0)

    @pl.when(step == 0)
    def _():
        ring[3] = jnp.zeros(ring.shape[1:], BF16)

    left, mid, right = (step + 1) % 4, (step + 2) % 4, (step + 3) % 4

    def part(k):
        return jnp.concatenate(
            [ring[left, k, :, WIDE - EDGE :], ring[mid, k], ring[right, k, :, :EDGE]], axis=1
        )

    out_re, out_im = column_product(part(0), part(1), op_ref, False)
    first[0] = out_re[:EDGE]
    first[1] = out_im[:EDGE]
    last[0] = out_re[EDGE:]
    last[1] = out_im[EDGE:]
    for i, (phase, fwd) in enumerate(((p_top, f_top), (p_bottom, f_bottom))):
        span = slice(i * EDGE, (i + 1) * EDGE)
        updated = phase[0] - gradient_of(coef, terms, other, span)
        l_re, l_im = turned(updated, fwd[0, 0], fwd[0, 1])
        ring[step % 4, 0, span] = l_re
        ring[step % 4, 1, span] = l_im


def ring_edges(coef, terms, other, phases, forward, op):
    _, _, rows, width = forward.shape
    groups = width // WIDE
    half = phases.shape[2] // WIDE
    far = rows // EDGE - 1

    def chunk(j):
        return jnp.minimum(j, groups - 1)

    tile = pl.BlockSpec((2, 2 * EDGE, WIDE), lambda j, c: (0, 0, chunk(j)))
    out = pl.BlockSpec((2, EDGE, WIDE), lambda j, c: (0, 0, jnp.maximum(j - 2, 0)))
    shape = jax.ShapeDtypeStruct((2, EDGE, width), BF16)
    return pl.pallas_call(
        ring_edge_kernel,
        out_shape=(shape, shape),
        grid_spec=pltpu.PrefetchScalarGridSpec(
            num_scalar_prefetch=1,
            grid=(groups + 2,),
            in_specs=[
                tile,
                tile,
                pl.BlockSpec((1, EDGE, WIDE), lambda j, c: (chunk(j) // half, 0, chunk(j) % half)),
                pl.BlockSpec((1, EDGE, WIDE), lambda j, c: (chunk(j) // half, far, chunk(j) % half)),
                pl.BlockSpec((1, 2, EDGE, WIDE), lambda j, c: (0, 0, 0, chunk(j))),
                pl.BlockSpec((1, 2, EDGE, WIDE), lambda j, c: (0, 0, far, chunk(j))),
                pl.BlockSpec((1, 2, op.shape[2], WIDE), lambda j, c: (jnp.maximum(j - 2, 0), 0, 0, 0)),
            ],
            out_specs=(out, out),
            scratch_shapes=[pltpu.VMEM((4, 2, 2 * EDGE, WIDE), BF16)],
        ),
        compiler_params=params(),
        cost_estimate=cost(16 * EDGE * width * op.shape[2], 24 * EDGE * width),
        name="ring_edges",
    )(coef, terms, other, phases, phases, forward, forward, op)


def launch_split_kernel(coef, t_in, o_in, t_edge, o_edge, phase, fwd, launched, phase_next):
    rows = phase.shape[1]
    pieces = (
        (t_edge, o_edge, slice(0, EDGE), slice(0, EDGE)),
        (t_in, o_in, slice(0, rows - 2 * EDGE), slice(EDGE, rows - EDGE)),
        (t_edge, o_edge, slice(EDGE, 2 * EDGE), slice(rows - EDGE, rows)),
    )
    for terms, other, span, place in pieces:
        updated = phase[0, place] - gradient_of(coef, terms, other, span)
        phase_next[0, place] = updated
        l_re, l_im = turned(updated, fwd[0, 0, place], fwd[0, 1, place])
        launched[0, place] = l_re
        launched[1, place] = l_im


def launch_split(coef, t_in, o_in, t_edge, o_edge, phases, forward):
    _, _, rows, width = forward.shape
    half = phases.shape[2] // WIDE
    inner = pl.BlockSpec((2, rows - 2 * EDGE, WIDE), lambda j, c: (0, 0, j))
    edge = pl.BlockSpec((2, 2 * EDGE, WIDE), lambda j, c: (0, 0, j))
    plane = pl.BlockSpec((1, rows, WIDE), lambda j, c: (j // half, 0, j % half))
    return pl.pallas_call(
        launch_split_kernel,
        out_shape=(
            jax.ShapeDtypeStruct(forward.shape[1:], BF16),
            jax.ShapeDtypeStruct(phases.shape, F32),
        ),
        grid_spec=pltpu.PrefetchScalarGridSpec(
            num_scalar_prefetch=1,
            grid=(width // WIDE,),
            in_specs=[
                inner,
                inner,
                edge,
                edge,
                plane,
                pl.BlockSpec((1, 2, rows, WIDE), lambda j, c: (0, 0, 0, j)),
            ],
            out_specs=(pl.BlockSpec((2, rows, WIDE), lambda j, c: (0, 0, j)), plane),
        ),
        compiler_params=params(),
        cost_estimate=cost(60 * rows * width, 24 * rows * width),
        name="launch",
    )(coef, t_in, o_in, t_edge, o_edge, phases, forward)


PAD = EDGE
FINISH = 512
MESH = pl.DeviceIdType.MESH


def band_rows(offs, blk, first, base, group, part, total):
    zero = jnp.zeros((BLK, BLK), F32)
    strips = []
    for r in range(group):
        row = base + r
        own = [blk[part, first + r, k].astype(F32) for k in range(blk.shape[2])]
        pieces = [zero] * r
        for d in range(2 * RADIUS + 1):
            place = row + (d - RADIUS)
            inside = (place >= 0) & (place < total)
            piece = zero
            for k, block in enumerate(own):
                piece = jnp.where(inside & (offs[row, k] == d - RADIUS), block, piece)
            pieces.append(piece)
        pieces += [zero] * (group - 1 - r)
        strips.append(jnp.concatenate(pieces, axis=1))
    return jnp.concatenate(strips, axis=0)


def stacked(re, im):
    return jnp.concatenate(
        [jnp.concatenate([re, -im], axis=1), jnp.concatenate([im, re], axis=1)], axis=0
    ).astype(BF16)


def exchange_kernel(
    tiles, offs, blocks, adjoint, forward, phase,
    mid, lau, t_in, o_in, phases, updated, halo2, hop, rin, red,
    halo1, col_op, ends, te, oe, sums, slots, coef,
    ph_sem, s1, r1, q1, f1, ti_sem, te_s, te_r, ar_s, ar_r, s2, r2, q2, f2,
):
    d = lax.axis_index("design")
    t = lax.axis_index("tile")
    m = lax.axis_index("mode")
    peers = 2 * tiles
    me = 2 * t + m
    levels = tiles // 2
    odd = lax.rem(t, 2)
    step = 2 * odd - 1
    level = jnp.where(odd == 1, t // 2, levels - 1 - t // 2)
    beside, across = t - step, t + step
    has_across = level < levels - 1
    rows, width = adjoint.shape[1], adjoint.shape[2]
    groups = width // WIDE
    total = blocks.shape[1]
    own_rows = total // tiles
    send_hops = jnp.where(has_across, groups * (levels - 1 - level) // levels, 0)
    pass_hops = groups * level // levels

    def device(tile, mode):
        return {"tile": tile, "mode": mode}

    def peer(p):
        who = lax.rem(me + p, peers)
        return device(who // 2, lax.rem(who, 2))

    barrier = pltpu.get_barrier_semaphore()
    for p in range(1, peers):
        pl.semaphore_signal(barrier, inc=1, device_id=peer(p), device_id_type=MESH)
    pl.semaphore_wait(barrier, peers - 1)

    def remote(src, dst, send, recv, tile, mode):
        return pltpu.make_async_remote_copy(
            src_ref=src, dst_ref=dst, send_sem=send, recv_sem=recv,
            device_id=device(tile, mode), device_id_type=MESH,
        )

    def cols(c, lead=0, wide=WIDE):
        return pl.ds(pl.multiple_of(c * WIDE + lead, 128), wide)

    near = pl.multiple_of(odd * (rows - EDGE), EDGE)
    far_side = pl.multiple_of((1 - odd) * (rows - EDGE), EDGE)

    def raw(start, c):
        return adjoint.at[:, pl.ds(start, EDGE), cols(c)]

    def land1(side, c):
        return halo1.at[side, :, :, cols(c, PAD)]

    def land2(side, c):
        return halo2.at[side, :, :, cols(c)]

    def made(side, c):
        return ends.at[side, :, :, cols(c)]

    class Trip:
        def __init__(self, phase_no, sent, got, mid_got, passed, near_src, far_src, land):
            self.args = phase_no, sent, got, mid_got, passed, near_src, far_src, land

        def direct(self, c):
            _, sent, got, _, _, src, _, land = self.args
            return remote(src(c), land(1 - odd, c), sent.at[0, c], got.at[0, c], across, m)

        def far(self, c):
            _, sent, got, _, _, _, src, land = self.args
            return remote(src(c), land(odd, c), sent.at[1, c], got.at[1, c], beside, m)

        def first_hop(self, c):
            k, sent, _, mid_got, _, src, _, _ = self.args
            return remote(src(c), hop.at[k, :, :, cols(c)], sent.at[0, c], mid_got.at[c], beside, m)

        def second_hop(self, c):
            k, _, got, _, passed, _, _, land = self.args
            return remote(hop.at[k, :, :, cols(c)], land(odd, c), passed.at[c], got.at[0, c], t - 2 * step, m)

        def got_near(self, c):
            _, sent, got, _, _, src, _, land = self.args
            return remote(src(c), land(odd, c), sent.at[0, c], got.at[0, c], beside, m)

        def got_far(self, c):
            _, sent, got, _, _, _, src, land = self.args
            return remote(src(c), land(1 - odd, c), sent.at[1, c], got.at[1, c], beside, m)

        def send(self, c):
            @pl.when(c < send_hops)
            def _():
                self.first_hop(c).start()

            @pl.when(has_across & (c >= send_hops))
            def _():
                self.direct(c).start()

        def relay(self, c):
            @pl.when(c < pass_hops)
            def _():
                self.first_hop(c).wait_recv()
                self.second_hop(c).start()

        def arrived(self, c):
            self.got_far(c).wait_recv()

            @pl.when(has_across)
            def _():
                self.got_near(c).wait_recv()

        def close(self):
            each(groups, lambda c: self.far(c).wait_send())

            @pl.when(has_across)
            def _():
                each(groups, lambda c: self.direct(c).wait_send())

            each(pass_hops, lambda c: self.second_hop(c).wait_send())

    def each(n, fn):
        def step(c, carry):
            fn(c)
            return carry
        lax.fori_loop(0, n, step, 0)

    trip1 = Trip(0, s1, r1, q1, f1, lambda c: raw(near, c), lambda c: raw(far_side, c), land1)
    trip2 = Trip(1, s2, r2, q2, f2, lambda c: made(odd, c), lambda c: made(1 - odd, c), land2)
    each(send_hops, lambda c: trip1.first_hop(c).start())

    def enter(c):
        trip1.far(c).start()

        @pl.when(has_across & (c >= send_hops))
        def _():
            trip1.direct(c).start()

    each(groups, enter)

    share = remote(phase, phases.at[m], ph_sem.at[0], ph_sem.at[1], t, 1 - m)
    share.start()

    halo1[:, :, :, 0:PAD] = jnp.zeros((2, 2, EDGE, PAD), BF16)
    halo1[:, :, :, PAD + width : PAD + width + PAD] = jnp.zeros((2, 2, EDGE, PAD), BF16)
    sums[...] = jnp.zeros_like(sums)

    def blank(side):
        def step(c, carry):
            halo1[side, :, :, cols(c, PAD)] = jnp.zeros((2, EDGE, WIDE), BF16)
            halo2[side, :, :, cols(c)] = jnp.zeros((2, EDGE, WIDE), BF16)
            return carry
        lax.fori_loop(0, groups, step, 0)

    @pl.when(t == 0)
    def _():
        blank(0)

    @pl.when(t == tiles - 1)
    def _():
        blank(1)

    span_in, per = WIDE + 2 * EDGE, WIDE // BLK

    def build_group(blk, g):
        re, im = [band_rows(offs, blk, 0, g * per, per, part, total).T for part in range(2)]
        col_op[g, :span_in, :WIDE] = re.astype(BF16)
        col_op[g, :span_in, WIDE:] = im.astype(BF16)
        col_op[g, span_in:, :WIDE] = (-im).astype(BF16)
        col_op[g, span_in:, WIDE:] = re.astype(BF16)

    def build_rows(blk, lead):
        base = t * own_rows
        inner = own_rows - 2 * RADIUS
        rin[...] = stacked(*[band_rows(offs, blk, RADIUS, base + RADIUS, inner, p, total) for p in range(2)])
        red[0] = stacked(*[band_rows(offs, blk, 0, base, RADIUS, p, total) for p in range(2)])
        low = own_rows - RADIUS
        red[1] = stacked(*[band_rows(offs, blk, low, base + low, RADIUS, p, total) for p in range(2)])
        build_group(lead, 0)

    bands = blocks.shape[2]
    pltpu.emit_pipeline(
        build_rows, grid=(1,),
        in_specs=[pl.BlockSpec((2, own_rows, bands, BLK, BLK), lambda g: (0, t, 0, 0, 0)),
                  pl.BlockSpec((2, per, bands, BLK, BLK), lambda g: (0, 0, 0, 0, 0))],
    )(blocks, blocks)

    tile = pl.BlockSpec((2, rows, WIDE), lambda j: (0, 0, j))

    def column_step(left, middle, right, j, order):
        x = jnp.concatenate([window(left, middle, right, p) for p in order], axis=1)
        both = dot(x, col_op[j]).astype(BF16)
        mid[0, :, cols(j)], mid[1, :, cols(j)] = both[:, :WIDE], both[:, WIDE:]

    def every_other(trip, j, lead):
        @pl.when(lax.rem(j, 2) == 0)
        def _():
            trip.relay(lead + j // 2)

    def adjoint_columns(left, middle, right, blk):
        j = pl.program_id(0)
        column_step(left, middle, right, j, (1, 0))
        build_group(blk, jnp.minimum(j + 1, groups - 1))
        every_other(trip1, j, 0)

    pltpu.emit_pipeline(
        adjoint_columns, grid=(groups,),
        in_specs=window_specs(rows, groups) + [
            pl.BlockSpec((2, per, bands, BLK, BLK), lambda j: (0, jnp.minimum(j + 1, groups - 1), 0, 0, 0))],
    )(adjoint, adjoint, adjoint, blocks)

    half = phase.shape[1] // WIDE

    def keep(src, dst):
        dst[0] = src[...]

    pltpu.emit_pipeline(
        keep, grid=(half,),
        in_specs=[pl.BlockSpec((rows, WIDE), lambda j: (0, j))],
        out_specs=[pl.BlockSpec((1, rows, WIDE), lambda j: (m, 0, j))],
    )(phase, phases)
    share.wait()
    plane = pl.BlockSpec((1, rows, WIDE), lambda j: (j // half, 0, j % half))
    inner_tile = pl.BlockSpec((2, rows - 2 * EDGE, WIDE), lambda j: (0, 0, j))

    def count(sum_re, sum_im):
        tall = sum_re.shape[0]
        sums[0] += jnp.sum(sum_re.reshape(tall // 8, 8, WIDE), axis=0)
        sums[1] += jnp.sum(sum_im.reshape(tall // 8, 8, WIDE), axis=0)

    def product(both, lit_re, lit_im):
        tall = both.shape[0] // 2
        adj_im = both[:tall].astype(BF16).astype(F32)
        adj_re = both[tall:].astype(BF16).astype(F32)
        lit_re, lit_im = lit_re.astype(F32), lit_im.astype(F32)
        t_re = adj_re * lit_re + adj_im * lit_im
        t_im = adj_re * lit_im - adj_im * lit_re
        count(t_re, t_im)
        return t_re.astype(BF16), t_im.astype(BF16)

    def inner_terms(ph, fwd, out):
        j = pl.program_id(0)
        low, high = EDGE, rows - EDGE
        for i, (a, b) in enumerate(((0, EDGE), (high, rows))):
            ends[i, 0, :, cols(j)], ends[i, 1, :, cols(j)] = turned(
                ph[0, a:b], fwd[0, a:b], fwd[1, a:b])
        lit_re, lit_im = turned(ph[0, low:high], fwd[0, low:high], fwd[1, low:high])
        both = dot(rin[...], jnp.concatenate([mid[0, :, cols(j)], mid[1, :, cols(j)]], axis=0))
        out[0], out[1] = product(both, lit_re, lit_im)
        every_other(trip1, j, groups // 2)

    pltpu.emit_pipeline(
        inner_terms, grid=(groups,), in_specs=[plane, tile], out_specs=[inner_tile],
    )(phases, forward, t_in)

    swap_in = remote(t_in, o_in, ti_sem.at[0], ti_sem.at[1], t, 1 - m)
    swap_in.start()

    def swap_edge(c):
        return remote(te.at[:, :, cols(c)], oe.at[:, :, cols(c)], te_s.at[c], te_r.at[c], t, 1 - m)

    trip1.arrived(0)

    def halo_product(g, order):
        x = jnp.concatenate([
            jnp.concatenate([halo1[s, p, :, cols(g, 0, 2 * WIDE)] for p in order], axis=1) for s in range(2)
        ], axis=0)
        return dot(x, col_op[g]).astype(BF16)

    def edge_terms(j):

        @pl.when(j < groups - 1)
        def _():
            trip1.arrived(j + 1)

        both = halo_product(j, (1, 0))
        h = (both[:, :WIDE], both[:, WIDE:])
        top = jnp.concatenate([h[0][:EDGE], mid[0, : 2 * EDGE, cols(j)], h[1][:EDGE], mid[1, : 2 * EDGE, cols(j)]], axis=0)
        low = rows - 2 * EDGE
        bottom = jnp.concatenate([mid[0, low:, cols(j)], h[0][EDGE:], mid[1, low:, cols(j)], h[1][EDGE:]], axis=0)
        for i, field in enumerate((top, bottom)):
            span = slice(i * EDGE, (i + 1) * EDGE)
            te[0, span, cols(j)], te[1, span, cols(j)] = product(
                dot(red[i], field), ends[i, 0, :, cols(j)], ends[i, 1, :, cols(j)])
        swap_edge(j).start()

    each(groups, edge_terms)

    slots[me] = sums[:, :, :128] + sums[:, :, 128:]

    def report(p):
        who = peer(p)
        return pltpu.make_async_remote_copy(
            src_ref=slots.at[me], dst_ref=slots.at[me], send_sem=ar_s.at[p], recv_sem=ar_r.at[p],
            device_id=who, device_id_type=MESH)

    def heard(p):
        who = lax.rem(me + peers - p, peers)
        return pltpu.make_async_remote_copy(
            src_ref=slots.at[who], dst_ref=slots.at[who], send_sem=ar_s.at[p], recv_sem=ar_r.at[p],
            device_id=peer(p), device_id_type=MESH)

    for p in range(1, peers):
        report(p).start()
    for p in range(1, peers):
        heard(p).wait_recv()
    for i, who in enumerate((m, 1 - m)):
        value = slots[who]
        for k in range(1, tiles):
            value = value + slots[2 * k + who]
        for part in range(2):
            coef[2 * i + part] = jnp.sum(value[part]) * (1.0 / (4.0 * width * 2))

    def gradient(own_re, own_im, other_re, other_im):
        return (coef[0] * own_im.astype(F32) - coef[1] * own_re.astype(F32)) + (
            coef[2] * other_im.astype(F32) - coef[3] * other_re.astype(F32))

    far = rows // EDGE - 1

    def chunk(j):
        return jnp.minimum(j, groups - 1)

    def edge_launch(p_top, p_bottom, f_top, f_bottom):
        j = pl.program_id(0)

        @pl.when(j < groups)
        def _():
            swap_edge(j).wait_recv()
            for i, (ph, fwd) in enumerate(((p_top, f_top), (p_bottom, f_bottom))):
                span = slice(i * EDGE, (i + 1) * EDGE)
                after = ph[0] - gradient(te[0, span, cols(j)], te[1, span, cols(j)],
                                         oe[0, span, cols(j)], oe[1, span, cols(j)])
                halo1[i, 0, :, cols(j, PAD)], halo1[i, 1, :, cols(j, PAD)] = turned(after, fwd[0], fwd[1])

        @pl.when(j > 0)
        def _():
            g = j - 1
            both = halo_product(g, (0, 1))
            o_re, o_im = both[:, :WIDE], both[:, WIDE:]
            for s in range(2):
                ends[s, 0, :, cols(g)] = o_re[s * EDGE : (s + 1) * EDGE]
                ends[s, 1, :, cols(g)] = o_im[s * EDGE : (s + 1) * EDGE]

            trip2.send(g)
            trip2.far(g).start()

    pltpu.emit_pipeline(
        edge_launch, grid=(groups + 1,),
        in_specs=[
            pl.BlockSpec((1, EDGE, WIDE), lambda j: (chunk(j) // half, 0, chunk(j) % half)),
            pl.BlockSpec((1, EDGE, WIDE), lambda j: (chunk(j) // half, far, chunk(j) % half)),
            pl.BlockSpec((2, EDGE, WIDE), lambda j: (0, 0, chunk(j))),
            pl.BlockSpec((2, EDGE, WIDE), lambda j: (0, far, chunk(j))),
        ],
    )(phases, phases, forward, forward)

    swap_in.wait()

    def launch_tile(own, other, ph, fwd, out):
        j = pl.program_id(0)
        for k, (a, b) in enumerate(((0, EDGE), (EDGE, rows - EDGE), (rows - EDGE, rows))):
            if k == 1:
                grad = gradient(own[0], own[1], other[0], other[1])
            else:
                span = slice((k // 2) * EDGE, (k // 2 + 1) * EDGE)
                grad = gradient(te[0, span, cols(j)], te[1, span, cols(j)],
                                oe[0, span, cols(j)], oe[1, span, cols(j)])
            after = ph[0, a:b] - grad
            @pl.when(j // half == m)
            def _(a=a, b=b, after=after):
                updated[a:b, cols(j - m * half)] = after

            out[0, a:b], out[1, a:b] = turned(after, fwd[0, a:b], fwd[1, a:b])
        every_other(trip2, j, 0)

    pltpu.emit_pipeline(
        launch_tile, grid=(groups,),
        in_specs=[inner_tile, inner_tile, plane, tile],
        out_specs=[tile],
    )(t_in, o_in, phases, forward, lau)

    def forward_columns(left, middle, right):
        j = pl.program_id(0)
        column_step(left, middle, right, j, (0, 1))
        every_other(trip2, j, groups // 2)

    pltpu.emit_pipeline(
        forward_columns, grid=(groups,), in_specs=window_specs(rows, groups),
    )(lau, lau, lau)

    for p in range(1, peers):
        report(p).wait_send()
    each(groups, lambda c: swap_edge(c).wait_send())

    each(groups, trip2.arrived)
    trip1.close()
    trip2.close()


def exchange(forward, adjoint, phase, blocks, offsets):
    tiles = lax.axis_size("tile")
    _, rows, width = forward.shape
    half = phase.shape[1]
    groups = width // WIDE
    inner = rows - 2 * EDGE
    hbm = pl.BlockSpec(memory_space=pl.ANY)
    dma = pltpu.SemaphoreType.DMA
    field = jax.ShapeDtypeStruct((2, rows, width), BF16)
    plane = jax.ShapeDtypeStruct((2, rows, half), F32)
    rin = (2 * inner, 2 * rows)
    red = (2, 2 * EDGE, 6 * EDGE)
    edges = (2, 2, EDGE, width)
    shapes = (
        pltpu.VMEM(field.shape, BF16), field,
        jax.ShapeDtypeStruct((2, inner, width), BF16),
        jax.ShapeDtypeStruct((2, inner, width), BF16),
        plane, pltpu.VMEM((rows, half), F32),
        pltpu.VMEM(edges, BF16), jax.ShapeDtypeStruct(edges, BF16),
        pltpu.VMEM(rin, BF16), pltpu.VMEM(red, BF16),
    )
    local = pl.BlockSpec(memory_space=pltpu.VMEM)
    edge = pltpu.VMEM((2, 2 * EDGE, width), BF16)
    peers = 2 * tiles
    out = pl.pallas_call(
        functools.partial(exchange_kernel, tiles),
        out_shape=shapes,
        in_specs=[pl.BlockSpec(memory_space=pltpu.SMEM)] + [hbm] * 4,
        out_specs=(local, hbm, hbm, hbm, hbm, local, local, hbm, local, local),
        scratch_shapes=[
            pltpu.VMEM((2, 2, EDGE, width + 2 * PAD), BF16),
            pltpu.VMEM((groups, 2 * (WIDE + 2 * EDGE), 2 * WIDE), BF16),
            pltpu.VMEM((2, 2, EDGE, width), BF16),
            edge, edge,
            pltpu.VMEM((2, 8, WIDE), F32),
            pltpu.VMEM((peers, 2, 8, 128), F32),
            pltpu.SMEM((4,), F32),
            dma((2,)), dma((2, groups)), dma((2, groups)), dma((groups,)), dma((groups,)), dma((2,)),
            dma((groups,)), dma((groups,)), dma((peers,)), dma((peers,)),
            dma((2, groups)), dma((2, groups)), dma((groups,)), dma((groups,)),
        ],
        compiler_params=pltpu.CompilerParams(
            vmem_limit_bytes=42 * 1024 * 1024, collective_id=0, has_side_effects=True),
        cost_estimate=cost(50 * rows * width * 512, 100 * rows * width),
        name="exchange",
    )(offsets, blocks, adjoint, forward, phase)
    mid, updated, halo2, rin, red = out[0], out[5], out[6], out[8], out[9]
    return mid, updated, halo2, rin, red


def finish_kernel(top, main, bottom, rin, red, after, out, phase_next):
    rows = main.shape[1]
    phase_next[...] = after[...]
    low = rows - 2 * EDGE
    pieces = (
        (EDGE, rin[...], [main[0], main[1]]),
        (0, red[0], [top[0, 0], main[0, : 2 * EDGE], top[0, 1], main[1, : 2 * EDGE]]),
        (rows - EDGE, red[1], [main[0, low:], bottom[0, 0], main[1, low:], bottom[0, 1]]),
    )
    for start, op, parts in pieces:
        both = dot(op, jnp.concatenate(parts, axis=0)).astype(BF16)
        tall = both.shape[0] // 2
        out[0, 0, start : start + tall] = both[:tall]
        out[0, 1, start : start + tall] = both[tall:]


def finish(mid, updated, halo2, rin, red):
    _, rows, width = mid.shape
    groups = width // FINISH
    narrow = updated.shape[1] // groups
    return pl.pallas_call(
        finish_kernel,
        out_shape=(
            jax.ShapeDtypeStruct((1,) + mid.shape, BF16),
            jax.ShapeDtypeStruct(updated.shape, F32),
        ),
        grid=(groups,),
        in_specs=[
                pl.BlockSpec((1, 2, EDGE, FINISH), lambda j: (0, 0, 0, j)),
                pl.BlockSpec((2, rows, FINISH), lambda j: (0, 0, j)),
                pl.BlockSpec((1, 2, EDGE, FINISH), lambda j: (1, 0, 0, j)),
                pl.BlockSpec(rin.shape, lambda j: (0, 0)),
                pl.BlockSpec(red.shape, lambda j: (0, 0, 0)),
                pl.BlockSpec((rows, narrow), lambda j: (0, j)),
            ],
            out_specs=(
                pl.BlockSpec((1, 2, rows, FINISH), lambda j: (0, 0, 0, j)),
                pl.BlockSpec((rows, narrow), lambda j: (0, j)),
            ),
        compiler_params=pltpu.CompilerParams(vmem_limit_bytes=20 * 1024 * 1024),
        cost_estimate=cost(8 * rows * width * 512, 16 * rows * width),
        name="finish",
    )(halo2, mid, halo2, rin, red, updated)


def exchange_edges(first, last):
    tiles = lax.axis_size("tile")
    top = lax.ppermute(last, "tile", [(t, t + 1) for t in range(tiles - 1)])
    bottom = lax.ppermute(first, "tile", [(t + 1, t) for t in range(tiles - 1)])
    return top, bottom


def body(forward, adjoint_next, phase, blocks, offsets):
    block_total = offsets.shape[0]
    tiles = lax.axis_size("tile")
    modes = lax.axis_size("mode")
    mode = lax.axis_index("mode")
    rows, width = forward.shape[2], forward.shape[3]
    adjoint = adjoint_next[0]
    if modes == 2 and tiles % 2 == 0 and rows // BLK == 2 * RADIUS + WIDE // BLK:
        parts = exchange(forward[0], adjoint, phase, blocks, offsets)
        forward_next, phase_next = finish(*parts)
        return phase_next, forward_next
    top, bottom = exchange_edges(adjoint[:, :EDGE], adjoint[:, rows - EDGE :])
    phases = lax.all_gather(phase, "mode", axis=0, tiled=False)

    raw_index = jnp.arange(block_total, dtype=jnp.int32)[:, None] + offsets
    inside = (raw_index >= 0) & (raw_index < block_total)
    pos = jnp.where(inside, offsets + RADIUS, -1).astype(jnp.int32)
    own_blocks = block_total // tiles
    split = own_blocks == 2 * RADIUS + WIDE // BLK
    start = lax.axis_index("tile") * own_blocks
    column_op = build(blocks, pos, WIDE // BLK, True)
    own_part = lax.dynamic_slice_in_dim(blocks, start, own_blocks, 1)
    own_pos = lax.dynamic_slice_in_dim(pos, start, own_blocks, 0)
    if split:
        inner = slice(RADIUS, own_blocks - RADIUS)
        row_op = build(own_part[:, inner], own_pos[inner], WIDE // BLK, False)
        ends = [own_part[:, :RADIUS], own_part[:, own_blocks - RADIUS :]]
        end_pos = [own_pos[:RADIUS], own_pos[own_blocks - RADIUS :]]
        edge_op = build(jnp.concatenate(ends, 1), jnp.concatenate(end_pos, 0), RADIUS, False)
    else:
        row_op = build(own_part, own_pos, min(WIDE // BLK, own_blocks), False)

    back_middle = column_pass(adjoint, column_op, True)
    lit = light(phases, forward)
    swap = [(m, (m + 1) % modes) for m in range(modes)]
    if split:
        t_in, s_in = adjoint_inner(back_middle, row_op, lit)
        o_in = lax.ppermute(t_in, "mode", swap)
        terms, sums = adjoint_edges(top, bottom, column_op, back_middle, edge_op, lit, s_in)
    else:
        terms, sums = adjoint_rows(top, bottom, column_op, back_middle, row_op, lit)
    other = lax.ppermute(terms, "mode", swap)
    own = jnp.sum(sums, axis=(1, 2))
    table = jnp.where(jnp.arange(modes)[:, None] == mode, own[None, :], 0.0)
    table = lax.psum(table, ("tile", "mode"))
    order = jnp.where(mode == 0, table, table[::-1])
    coef = order.reshape(-1) * (1.0 / (4.0 * width * modes))

    if split:
        first, last = ring_edges(coef, terms, other, phases, forward, column_op)
        top, bottom = exchange_edges(first, last)
        launched, updated = launch_split(coef, t_in, o_in, terms, other, phases, forward)
    else:
        edges = launch_edges(coef, terms, other, phases, forward)
        edges = column_pass(edges, column_op, False)
        top, bottom = exchange_edges(edges[:, :EDGE], edges[:, EDGE:])
        launched, updated = launch(coef, terms, other, phases, forward)
    middle = column_pass(launched, column_op, False)
    phase_next = lax.dynamic_index_in_dim(updated, mode, 0, keepdims=False)
    if split:
        whole = forward_inner(middle, row_op)
        return phase_next, forward_edges(top, middle, bottom, edge_op, whole)
    return phase_next, forward_rows(top, middle, bottom, row_op)


def solution(mesh):
    placed = (
        P(("design", "mode"), None, "tile", None),
        P(("design", "mode"), None, "tile", None),
        P(("design", "tile"), "mode"),
        P(None, "design", None, None, None),
        P("design", None),
    )
    return jax.shard_map(
        body,
        mesh=mesh,
        in_specs=placed,
        out_specs=(P(("design", "tile"), "mode"), P(("design", "mode"), None, "tile", None)),
        check_vma=False,
    )
```

```python
import functools

import jax
import jax.numpy as jnp
from jax import lax
from jax.experimental import pallas as pl
from jax.experimental.pallas import tpu as pltpu
from jax.sharding import PartitionSpec as P

BLK = 64
RADIUS = 2
EDGE = RADIUS * BLK
WIDE = 256
VMEM_LIMIT = 44 * 1024 * 1024

F32 = jnp.float32
BF16 = jnp.bfloat16


def params():
    return pltpu.CompilerParams(vmem_limit_bytes=VMEM_LIMIT)


def cost(flops, moved):
    return pl.CostEstimate(flops=int(flops), bytes_accessed=int(moved), transcendentals=0)


def sincos(x):
    turns = jnp.round(x * 0.15915494309189535)
    r = x - turns * 6.28125
    r = r - turns * 1.935307179586232e-3
    z = r * r
    half_sine = r * (0.7071067690849304 + z * (-0.029462767764925957 + z * (
        0.00036827221629209816 + z * (-2.1885971364099532e-06 + z * 7.195012585725635e-09))))
    half_cosine = 1.4142135381698608 + z * (-0.17677634954452515 + z * (
        0.003682573325932026 + z * (-3.0612263799412176e-05 + z * 1.2788676428954204e-07)))
    return half_sine * half_cosine, 1.0 - half_sine * half_sine


def dot(a, b):
    return jnp.dot(a, b, preferred_element_type=F32)


def build_kernel(pos_ref, blk_ref, out_ref, *, group, transposed):
    base = pl.program_id(0) * group
    zero = jnp.zeros((BLK, BLK), F32)
    for part in range(2):
        strips = []
        for r in range(group):
            own = [blk_ref[part, r, k].astype(F32) for k in range(blk_ref.shape[2])]
            pieces = [zero] * r
            for d in range(2 * RADIUS + 1):
                piece = zero
                for k, block in enumerate(own):
                    piece = jnp.where(pos_ref[base + r, k] == d, block, piece)
                pieces.append(piece)
            pieces += [zero] * (group - 1 - r)
            strips.append(jnp.concatenate(pieces, axis=1))
        full = jnp.concatenate(strips, axis=0)
        if transposed:
            full = full.T
        out_ref[0, part] = full.astype(BF16)


def build(blocks, pos, group, transposed):
    _, rows, bands, _, _ = blocks.shape
    tall, wide = group * BLK, (group + 2 * RADIUS) * BLK
    if transposed:
        tall, wide = wide, tall
    count = rows // group
    return pl.pallas_call(
        functools.partial(build_kernel, group=group, transposed=transposed),
        out_shape=jax.ShapeDtypeStruct((count, 2, tall, wide), BF16),
        grid_spec=pltpu.PrefetchScalarGridSpec(
            num_scalar_prefetch=1,
            grid=(count,),
            in_specs=[pl.BlockSpec((2, group, bands, BLK, BLK), lambda g, p: (0, g, 0, 0, 0))],
            out_specs=pl.BlockSpec((1, 2, tall, wide), lambda g, p: (g, 0, 0, 0)),
        ),
        compiler_params=params(),
        cost_estimate=cost(0, 16 * rows * bands * BLK * BLK),
        name="build_operator",
    )(pos, blocks)


def window_specs(rows, groups):
    last = 2 * groups - 1
    return [
        pl.BlockSpec((2, rows, 128), lambda j: (0, 0, jnp.maximum(2 * j - 1, 0))),
        pl.BlockSpec((2, rows, WIDE), lambda j: (0, 0, j)),
        pl.BlockSpec((2, rows, 128), lambda j: (0, 0, jnp.minimum(2 * j + 2, last))),
    ]


def window(left, mid, right, part):
    return jnp.concatenate([left[part], mid[part], right[part]], axis=1)


def column_product(x_re, x_im, op_ref, conj):
    op_re, op_im = op_ref[0, 0], op_ref[0, 1]
    rr, ii = dot(x_re, op_re), dot(x_im, op_im)
    ri, ir = dot(x_re, op_im), dot(x_im, op_re)
    if conj:
        return (rr + ii).astype(BF16), (ri - ir).astype(BF16)
    return (rr - ii).astype(BF16), (ri + ir).astype(BF16)


def column_kernel(left, mid, right, op_ref, out_ref, *, conj):
    out_re, out_im = column_product(
        window(left, mid, right, 0), window(left, mid, right, 1), op_ref, conj
    )
    out_ref[0] = out_re
    out_ref[1] = out_im


def column_pass(field, op, conj):
    _, rows, width = field.shape
    groups = width // WIDE
    return pl.pallas_call(
        functools.partial(column_kernel, conj=conj),
        out_shape=jax.ShapeDtypeStruct(field.shape, BF16),
        grid=(groups,),
        in_specs=window_specs(rows, groups)
        + [pl.BlockSpec((1, 2, op.shape[2], WIDE), lambda j: (j, 0, 0, 0))],
        out_specs=pl.BlockSpec((2, rows, WIDE), lambda j: (0, 0, j)),
        compiler_params=params(),
        cost_estimate=cost(8 * rows * width * op.shape[2], 12 * rows * width + 2 * op.size),
        name="column_pass",
    )(field, field, field, op)


def row_groups(top, main, bottom, row_op):
    whole_re = jnp.concatenate([top[0], main[0], bottom[0]], axis=0)
    whole_im = jnp.concatenate([top[1], main[1], bottom[1]], axis=0)
    count, _, tall, deep = row_op.shape
    for i in range(count):
        m_re = whole_re[i * tall : i * tall + deep]
        m_im = whole_im[i * tall : i * tall + deep]
        op_re, op_im = row_op[i, 0], row_op[i, 1]
        out_re = dot(op_re, m_re) - dot(op_im, m_im)
        out_im = dot(op_re, m_im) + dot(op_im, m_re)
        yield i * tall, tall, out_re, out_im


def adjoint_row_kernel(tl, tm, tr, bl, bm, br, op_ref, main, row_op, lit, terms, sums):
    x_re = jnp.concatenate([window(tl, tm, tr, 0), window(bl, bm, br, 0)], axis=0)
    x_im = jnp.concatenate([window(tl, tm, tr, 1), window(bl, bm, br, 1)], axis=0)
    halo_re, halo_im = column_product(x_re, x_im, op_ref, True)

    @pl.when(pl.program_id(0) == 0)
    def _():
        sums[...] = jnp.zeros_like(sums)

    top = (halo_re[:EDGE], halo_im[:EDGE])
    bottom = (halo_re[EDGE:], halo_im[EDGE:])
    for low, tall, cj_re, cj_im in row_groups(top, main, bottom, row_op):
        cj_re = cj_re.astype(BF16).astype(F32)
        cj_im = cj_im.astype(BF16).astype(F32)
        lit_re = lit[0, low : low + tall].astype(F32)
        lit_im = lit[1, low : low + tall].astype(F32)
        t_re = cj_re * lit_re - cj_im * lit_im
        t_im = cj_re * lit_im + cj_im * lit_re
        terms[0, low : low + tall] = t_re.astype(BF16)
        terms[1, low : low + tall] = t_im.astype(BF16)
        sums[0] += jnp.sum(t_re.reshape(tall // 8, 8, WIDE), axis=0)
        sums[1] += jnp.sum(t_im.reshape(tall // 8, 8, WIDE), axis=0)


def adjoint_rows(top, bottom, op, main, row_op, lit):
    _, rows, width = main.shape
    groups = width // WIDE
    edge = window_specs(EDGE, groups)
    tile = pl.BlockSpec((2, rows, WIDE), lambda j: (0, 0, j))
    return pl.pallas_call(
        adjoint_row_kernel,
        out_shape=(
            jax.ShapeDtypeStruct(main.shape, BF16),
            jax.ShapeDtypeStruct((2, 8, WIDE), F32),
        ),
        grid=(groups,),
        in_specs=edge
        + edge
        + [
            pl.BlockSpec((1, 2, op.shape[2], WIDE), lambda j: (j, 0, 0, 0)),
            tile,
            pl.BlockSpec(row_op.shape, lambda j: (0, 0, 0, 0)),
            tile,
        ],
        out_specs=(tile, pl.BlockSpec((2, 8, WIDE), lambda j: (0, 0, 0))),
        compiler_params=params(),
        cost_estimate=cost(12 * rows * width * op.shape[2], 16 * rows * width),
        name="adjoint_rows",
    )(top, top, top, bottom, bottom, bottom, op, main, row_op, lit)


def forward_row_kernel(top, main, bottom, row_op, out):
    for low, tall, out_re, out_im in row_groups(top, main, bottom, row_op):
        out[0, 0, low : low + tall] = out_re.astype(BF16)
        out[0, 1, low : low + tall] = out_im.astype(BF16)


def forward_rows(top, main, bottom, row_op):
    _, rows, width = main.shape
    groups = width // WIDE
    edge = pl.BlockSpec((2, EDGE, WIDE), lambda j: (0, 0, j))
    return pl.pallas_call(
        forward_row_kernel,
        out_shape=jax.ShapeDtypeStruct((1,) + main.shape, BF16),
        grid=(groups,),
        in_specs=[
            edge,
            pl.BlockSpec((2, rows, WIDE), lambda j: (0, 0, j)),
            edge,
            pl.BlockSpec(row_op.shape, lambda j: (0, 0, 0, 0)),
        ],
        out_specs=pl.BlockSpec((1, 2, rows, WIDE), lambda j: (0, 0, 0, j)),
        compiler_params=params(),
        cost_estimate=cost(8 * rows * width * row_op.shape[3], 10 * rows * width),
        name="forward_rows",
    )(top, main, bottom, row_op)


def lit_kernel(phase, fwd, lit):
    sine, cosine = sincos(phase[0])
    f_re, f_im = fwd[0, 0].astype(F32), fwd[0, 1].astype(F32)
    lit[0] = (cosine * f_re - sine * f_im).astype(BF16)
    lit[1] = (sine * f_re + cosine * f_im).astype(BF16)


def light(phases, forward):
    _, _, rows, width = forward.shape
    half = phases.shape[2] // WIDE
    return pl.pallas_call(
        lit_kernel,
        out_shape=jax.ShapeDtypeStruct(forward.shape[1:], BF16),
        grid=(width // WIDE,),
        in_specs=[
            pl.BlockSpec((1, rows, WIDE), lambda j: (j // half, 0, j % half)),
            pl.BlockSpec((1, 2, rows, WIDE), lambda j: (0, 0, 0, j)),
        ],
        out_specs=pl.BlockSpec((2, rows, WIDE), lambda j: (0, 0, j)),
        compiler_params=params(),
        cost_estimate=cost(60 * rows * width, 12 * rows * width),
        name="light",
    )(phases, forward)


def launch_values(coef, terms, other, phase, fwd, launched):
    gradient = (coef[0] * terms[1].astype(F32) - coef[1] * terms[0].astype(F32)) + (
        coef[2] * other[1].astype(F32) - coef[3] * other[0].astype(F32)
    )
    updated = phase[0] - gradient
    sine, cosine = sincos(updated)
    f_re, f_im = fwd[0, 0].astype(F32), fwd[0, 1].astype(F32)
    launched[0] = (cosine * f_re - sine * f_im).astype(BF16)
    launched[1] = (sine * f_re + cosine * f_im).astype(BF16)
    return updated


def launch_kernel(coef, terms, other, phase, fwd, launched, phase_next):
    phase_next[0] = launch_values(coef, terms, other, phase, fwd, launched)


def launch(coef, terms, other, phases, forward):
    _, _, rows, width = forward.shape
    half = phases.shape[2] // WIDE
    tile = pl.BlockSpec((2, rows, WIDE), lambda j, c: (0, 0, j))
    plane = pl.BlockSpec((1, rows, WIDE), lambda j, c: (j // half, 0, j % half))
    return pl.pallas_call(
        launch_kernel,
        out_shape=(
            jax.ShapeDtypeStruct(forward.shape[1:], BF16),
            jax.ShapeDtypeStruct(phases.shape, F32),
        ),
        grid_spec=pltpu.PrefetchScalarGridSpec(
            num_scalar_prefetch=1,
            grid=(width // WIDE,),
            in_specs=[
                tile,
                tile,
                plane,
                pl.BlockSpec((1, 2, rows, WIDE), lambda j, c: (0, 0, 0, j)),
            ],
            out_specs=(tile, plane),
        ),
        compiler_params=params(),
        cost_estimate=cost(60 * rows * width, 24 * rows * width),
        name="launch",
    )(coef, terms, other, phases, forward)


def launch_edge_kernel(coef, terms, other, phase, fwd, launched):
    launch_values(coef, terms, other, phase, fwd, launched)


def launch_edges(coef, terms, other, phases, forward):
    _, _, rows, width = forward.shape
    wide = 2 * WIDE
    half = phases.shape[2] // wide
    far = rows // EDGE - 1
    tile = pl.BlockSpec((2, EDGE, wide), lambda e, j, c: (0, e * far, j))
    return pl.pallas_call(
        launch_edge_kernel,
        out_shape=jax.ShapeDtypeStruct((2, 2 * EDGE, width), BF16),
        grid_spec=pltpu.PrefetchScalarGridSpec(
            num_scalar_prefetch=1,
            grid=(2, width // wide),
            in_specs=[
                tile,
                tile,
                pl.BlockSpec((1, EDGE, wide), lambda e, j, c: (j // half, e * far, j % half)),
                pl.BlockSpec((1, 2, EDGE, wide), lambda e, j, c: (0, 0, e * far, j)),
            ],
            out_specs=pl.BlockSpec((2, EDGE, wide), lambda e, j, c: (0, e, j)),
        ),
        compiler_params=params(),
        cost_estimate=cost(120 * EDGE * width, 48 * EDGE * width),
        name="launch_edges",
    )(coef, terms, other, phases, forward)


def complex_rows(op_re, op_im, m_re, m_im):
    return dot(op_re, m_re) - dot(op_im, m_im), dot(op_re, m_im) + dot(op_im, m_re)


def add_terms(cj_re, cj_im, lit_re, lit_im, terms, sums, low):
    tall = cj_re.shape[0]
    cj_re = cj_re.astype(BF16).astype(F32)
    cj_im = cj_im.astype(BF16).astype(F32)
    lit_re, lit_im = lit_re.astype(F32), lit_im.astype(F32)
    t_re = cj_re * lit_re - cj_im * lit_im
    t_im = cj_re * lit_im + cj_im * lit_re
    terms[0, low : low + tall] = t_re.astype(BF16)
    terms[1, low : low + tall] = t_im.astype(BF16)
    sums[0] += jnp.sum(t_re.reshape(tall // 8, 8, WIDE), axis=0)
    sums[1] += jnp.sum(t_im.reshape(tall // 8, 8, WIDE), axis=0)


def adjoint_inner_kernel(main, row_op, lit, terms, sums):
    @pl.when(pl.program_id(0) == 0)
    def _():
        sums[...] = jnp.zeros_like(sums)

    rows = main.shape[1]
    cj_re, cj_im = complex_rows(row_op[0, 0], row_op[0, 1], main[0], main[1])
    add_terms(cj_re, cj_im, lit[0, EDGE : rows - EDGE], lit[1, EDGE : rows - EDGE], terms, sums, 0)


def adjoint_inner(main, row_op, lit):
    _, rows, width = main.shape
    inner = rows - 2 * EDGE
    tile = pl.BlockSpec((2, rows, WIDE), lambda j: (0, 0, j))
    return pl.pallas_call(
        adjoint_inner_kernel,
        out_shape=(
            jax.ShapeDtypeStruct((2, inner, width), BF16),
            jax.ShapeDtypeStruct((2, 8, WIDE), F32),
        ),
        grid=(width // WIDE,),
        in_specs=[tile, pl.BlockSpec(row_op.shape, lambda j: (0, 0, 0, 0)), tile],
        out_specs=(
            pl.BlockSpec((2, inner, WIDE), lambda j: (0, 0, j)),
            pl.BlockSpec((2, 8, WIDE), lambda j: (0, 0, 0)),
        ),
        compiler_params=params(),
        cost_estimate=cost(8 * inner * width * rows, 12 * rows * width),
        name="adjoint_inner",
    )(main, row_op, lit)


def edge_windows(main, part, top, bottom):
    rows = main.shape[1]
    return (
        jnp.concatenate([top, main[part, : 2 * EDGE]], axis=0),
        jnp.concatenate([main[part, rows - 2 * EDGE :], bottom], axis=0),
    )


def adjoint_edge_kernel(tl, tm, tr, bl, bm, br, op_ref, main, edge_op, lit, before, terms, sums):
    x_re = jnp.concatenate([window(tl, tm, tr, 0), window(bl, bm, br, 0)], axis=0)
    x_im = jnp.concatenate([window(tl, tm, tr, 1), window(bl, bm, br, 1)], axis=0)
    halo_re, halo_im = column_product(x_re, x_im, op_ref, True)

    @pl.when(pl.program_id(0) == 0)
    def _():
        sums[...] = before[...]

    rows = main.shape[1]
    res = edge_windows(main, 0, halo_re[:EDGE], halo_re[EDGE:])
    ims = edge_windows(main, 1, halo_im[:EDGE], halo_im[EDGE:])
    for i, low in enumerate((0, rows - EDGE)):
        cj_re, cj_im = complex_rows(edge_op[i, 0], edge_op[i, 1], res[i], ims[i])
        add_terms(cj_re, cj_im, lit[0, low : low + EDGE], lit[1, low : low + EDGE], terms, sums, i * EDGE)


def adjoint_edges(top, bottom, op, main, edge_op, lit, before):
    _, rows, width = main.shape
    groups = width // WIDE
    edge = window_specs(EDGE, groups)
    tile = pl.BlockSpec((2, rows, WIDE), lambda j: (0, 0, j))
    return pl.pallas_call(
        adjoint_edge_kernel,
        out_shape=(
            jax.ShapeDtypeStruct((2, 2 * EDGE, width), BF16),
            jax.ShapeDtypeStruct((2, 8, WIDE), F32),
        ),
        grid=(groups,),
        in_specs=edge
        + edge
        + [
            pl.BlockSpec((1, 2, op.shape[2], WIDE), lambda j: (j, 0, 0, 0)),
            tile,
            pl.BlockSpec(edge_op.shape, lambda j: (0, 0, 0, 0)),
            tile,
            pl.BlockSpec((2, 8, WIDE), lambda j: (0, 0, 0)),
        ],
        out_specs=(
            pl.BlockSpec((2, 2 * EDGE, WIDE), lambda j: (0, 0, j)),
            pl.BlockSpec((2, 8, WIDE), lambda j: (0, 0, 0)),
        ),
        compiler_params=params(),
        cost_estimate=cost(32 * EDGE * width * op.shape[2], 16 * rows * width),
        name="adjoint_edges",
    )(top, top, top, bottom, bottom, bottom, op, main, edge_op, lit, before)


def forward_inner_kernel(main, row_op, out):
    out_re, out_im = complex_rows(row_op[0, 0], row_op[0, 1], main[0], main[1])
    out[0, 0] = out_re.astype(BF16)
    out[0, 1] = out_im.astype(BF16)


def forward_inner(main, row_op):
    _, rows, width = main.shape
    inner = rows // EDGE - 2
    deep = row_op.shape[3]
    return pl.pallas_call(
        forward_inner_kernel,
        out_shape=jax.ShapeDtypeStruct((1,) + main.shape, BF16),
        grid=(width // WIDE, inner),
        in_specs=[
            pl.BlockSpec((2, rows, WIDE), lambda j, i: (0, 0, j)),
            pl.BlockSpec((1, 2, EDGE, deep), lambda j, i: (0, 0, i, 0)),
        ],
        out_specs=pl.BlockSpec((1, 2, EDGE, WIDE), lambda j, i: (0, 0, i + 1, j)),
        compiler_params=params(),
        cost_estimate=cost(8 * inner * EDGE * width * rows, 8 * rows * width),
        name="forward_inner",
    )(main, row_op)


def forward_edge_kernel(top, main, bottom, edge_op, whole, out):
    side = pl.program_id(1)

    def run(m_re, m_im):
        out_re, out_im = complex_rows(edge_op[0, 0], edge_op[0, 1], m_re, m_im)
        out[0, 0] = out_re.astype(BF16)
        out[0, 1] = out_im.astype(BF16)

    @pl.when(side == 0)
    def _():
        run(*[jnp.concatenate([top[p], main[p]], axis=0) for p in range(2)])

    @pl.when(side == 1)
    def _():
        run(*[jnp.concatenate([main[p], bottom[p]], axis=0) for p in range(2)])


def forward_edges(top, main, bottom, edge_op, whole):
    _, rows, width = main.shape
    wide = 2 * WIDE
    near = rows // (2 * EDGE) - 1
    far = rows // EDGE - 1
    halo = pl.BlockSpec((2, EDGE, wide), lambda j, i: (0, 0, j))
    return pl.pallas_call(
        forward_edge_kernel,
        out_shape=jax.ShapeDtypeStruct(whole.shape, BF16),
        grid=(width // wide, 2),
        in_specs=[
            halo,
            pl.BlockSpec((2, 2 * EDGE, wide), lambda j, i: (0, i * near, j)),
            halo,
            pl.BlockSpec((1, 2, EDGE, edge_op.shape[3]), lambda j, i: (i, 0, 0, 0)),
            pl.BlockSpec(memory_space=pl.ANY),
        ],
        out_specs=pl.BlockSpec((1, 2, EDGE, wide), lambda j, i: (0, 0, i * far, j)),
        input_output_aliases={4: 0},
        compiler_params=params(),
        cost_estimate=cost(16 * EDGE * width * edge_op.shape[3], 24 * EDGE * width),
        name="forward_edges",
    )(top, main, bottom, edge_op, whole)


def gradient_of(coef, terms, other, rows):
    return (coef[0] * terms[1, rows].astype(F32) - coef[1] * terms[0, rows].astype(F32)) + (
        coef[2] * other[1, rows].astype(F32) - coef[3] * other[0, rows].astype(F32)
    )


def turned(phase, f_re, f_im):
    sine, cosine = sincos(phase)
    f_re, f_im = f_re.astype(F32), f_im.astype(F32)
    return (cosine * f_re - sine * f_im).astype(BF16), (sine * f_re + cosine * f_im).astype(BF16)


def ring_edge_kernel(coef, terms, other, p_top, p_bottom, f_top, f_bottom, op_ref, first, last, ring):
    step = pl.program_id(0)

    @pl.when(step == 0)
    def _():
        ring[3] = jnp.zeros(ring.shape[1:], BF16)

    left, mid, right = (step + 1) % 4, (step + 2) % 4, (step + 3) % 4

    def part(k):
        return jnp.concatenate(
            [ring[left, k, :, WIDE - EDGE :], ring[mid, k], ring[right, k, :, :EDGE]], axis=1
        )

    out_re, out_im = column_product(part(0), part(1), op_ref, False)
    first[0] = out_re[:EDGE]
    first[1] = out_im[:EDGE]
    last[0] = out_re[EDGE:]
    last[1] = out_im[EDGE:]
    for i, (phase, fwd) in enumerate(((p_top, f_top), (p_bottom, f_bottom))):
        span = slice(i * EDGE, (i + 1) * EDGE)
        updated = phase[0] - gradient_of(coef, terms, other, span)
        l_re, l_im = turned(updated, fwd[0, 0], fwd[0, 1])
        ring[step % 4, 0, span] = l_re
        ring[step % 4, 1, span] = l_im


def ring_edges(coef, terms, other, phases, forward, op):
    _, _, rows, width = forward.shape
    groups = width // WIDE
    half = phases.shape[2] // WIDE
    far = rows // EDGE - 1

    def chunk(j):
        return jnp.minimum(j, groups - 1)

    tile = pl.BlockSpec((2, 2 * EDGE, WIDE), lambda j, c: (0, 0, chunk(j)))
    out = pl.BlockSpec((2, EDGE, WIDE), lambda j, c: (0, 0, jnp.maximum(j - 2, 0)))
    shape = jax.ShapeDtypeStruct((2, EDGE, width), BF16)
    return pl.pallas_call(
        ring_edge_kernel,
        out_shape=(shape, shape),
        grid_spec=pltpu.PrefetchScalarGridSpec(
            num_scalar_prefetch=1,
            grid=(groups + 2,),
            in_specs=[
                tile,
                tile,
                pl.BlockSpec((1, EDGE, WIDE), lambda j, c: (chunk(j) // half, 0, chunk(j) % half)),
                pl.BlockSpec((1, EDGE, WIDE), lambda j, c: (chunk(j) // half, far, chunk(j) % half)),
                pl.BlockSpec((1, 2, EDGE, WIDE), lambda j, c: (0, 0, 0, chunk(j))),
                pl.BlockSpec((1, 2, EDGE, WIDE), lambda j, c: (0, 0, far, chunk(j))),
                pl.BlockSpec((1, 2, op.shape[2], WIDE), lambda j, c: (jnp.maximum(j - 2, 0), 0, 0, 0)),
            ],
            out_specs=(out, out),
            scratch_shapes=[pltpu.VMEM((4, 2, 2 * EDGE, WIDE), BF16)],
        ),
        compiler_params=params(),
        cost_estimate=cost(16 * EDGE * width * op.shape[2], 24 * EDGE * width),
        name="ring_edges",
    )(coef, terms, other, phases, phases, forward, forward, op)


def launch_split_kernel(coef, t_in, o_in, t_edge, o_edge, phase, fwd, launched, phase_next):
    rows = phase.shape[1]
    pieces = (
        (t_edge, o_edge, slice(0, EDGE), slice(0, EDGE)),
        (t_in, o_in, slice(0, rows - 2 * EDGE), slice(EDGE, rows - EDGE)),
        (t_edge, o_edge, slice(EDGE, 2 * EDGE), slice(rows - EDGE, rows)),
    )
    for terms, other, span, place in pieces:
        updated = phase[0, place] - gradient_of(coef, terms, other, span)
        phase_next[0, place] = updated
        l_re, l_im = turned(updated, fwd[0, 0, place], fwd[0, 1, place])
        launched[0, place] = l_re
        launched[1, place] = l_im


def launch_split(coef, t_in, o_in, t_edge, o_edge, phases, forward):
    _, _, rows, width = forward.shape
    half = phases.shape[2] // WIDE
    inner = pl.BlockSpec((2, rows - 2 * EDGE, WIDE), lambda j, c: (0, 0, j))
    edge = pl.BlockSpec((2, 2 * EDGE, WIDE), lambda j, c: (0, 0, j))
    plane = pl.BlockSpec((1, rows, WIDE), lambda j, c: (j // half, 0, j % half))
    return pl.pallas_call(
        launch_split_kernel,
        out_shape=(
            jax.ShapeDtypeStruct(forward.shape[1:], BF16),
            jax.ShapeDtypeStruct(phases.shape, F32),
        ),
        grid_spec=pltpu.PrefetchScalarGridSpec(
            num_scalar_prefetch=1,
            grid=(width // WIDE,),
            in_specs=[
                inner,
                inner,
                edge,
                edge,
                plane,
                pl.BlockSpec((1, 2, rows, WIDE), lambda j, c: (0, 0, 0, j)),
            ],
            out_specs=(pl.BlockSpec((2, rows, WIDE), lambda j, c: (0, 0, j)), plane),
        ),
        compiler_params=params(),
        cost_estimate=cost(60 * rows * width, 24 * rows * width),
        name="launch",
    )(coef, t_in, o_in, t_edge, o_edge, phases, forward)


PAD = EDGE
MESH = pl.DeviceIdType.MESH


def band_rows(offs, blk, first, base, group, part, total):
    zero = jnp.zeros((BLK, BLK), F32)
    strips = []
    for r in range(group):
        row = base + r
        own = [blk[part, first + r, k].astype(F32) for k in range(blk.shape[2])]
        pieces = [zero] * r
        for d in range(2 * RADIUS + 1):
            place = row + (d - RADIUS)
            inside = (place >= 0) & (place < total)
            piece = zero
            for k, block in enumerate(own):
                piece = jnp.where(inside & (offs[k, row] == d - RADIUS), block, piece)
            pieces.append(piece)
        pieces += [zero] * (group - 1 - r)
        strips.append(jnp.concatenate(pieces, axis=1))
    return jnp.concatenate(strips, axis=0)


def stacked(re, im):
    return jnp.concatenate(
        [jnp.concatenate([re, -im], axis=1), jnp.concatenate([im, re], axis=1)], axis=0
    ).astype(BF16)


def exchange_kernel(
    tiles, offs, blocks, adjoint, forward, phase,
    mid, lau, t_in, o_in, phases, updated, hop,
    halo1, halo2, col_op, rin, red, ends, te, oe, sums, slots, coef,
    ph_sem, s1, r1, q1, f1, ti_sem, te_s, te_r, ar_s, ar_r, s2, r2, q2, f2,
):
    d = lax.axis_index("design")
    t = lax.axis_index("tile")
    m = lax.axis_index("mode")
    peers = 2 * tiles
    me = 2 * t + m
    levels = tiles // 2
    odd = lax.rem(t, 2)
    step = 2 * odd - 1
    level = jnp.where(odd == 1, t // 2, levels - 1 - t // 2)
    beside, across = t - step, t + step
    has_across = level < levels - 1
    rows, width = adjoint.shape[1], adjoint.shape[2]
    groups = width // WIDE
    total = blocks.shape[1]
    own_rows = total // tiles
    send_hops = jnp.where(has_across, groups * (levels - 1 - level) // levels, 0)
    pass_hops = groups * level // levels

    def device(tile, mode):
        return {"tile": tile, "mode": mode}

    def peer(p):
        who = lax.rem(me + p, peers)
        return device(who // 2, lax.rem(who, 2))

    barrier = pltpu.get_barrier_semaphore()
    for p in range(1, peers):
        pl.semaphore_signal(barrier, inc=1, device_id=peer(p), device_id_type=MESH)
    pl.semaphore_wait(barrier, peers - 1)

    def remote(src, dst, send, recv, tile, mode):
        return pltpu.make_async_remote_copy(
            src_ref=src, dst_ref=dst, send_sem=send, recv_sem=recv,
            device_id=device(tile, mode), device_id_type=MESH,
        )

    def cols(c, lead=0, wide=WIDE):
        return pl.ds(pl.multiple_of(c * WIDE + lead, 128), wide)

    near = pl.multiple_of(odd * (rows - EDGE), EDGE)
    far_side = pl.multiple_of((1 - odd) * (rows - EDGE), EDGE)

    def raw(start, c):
        return adjoint.at[:, pl.ds(start, EDGE), cols(c)]

    def land1(side, c):
        return halo1.at[side, :, :, cols(c, PAD)]

    def land2(side, c):
        return halo2.at[side, :, :, cols(c)]

    def made(side, c):
        return ends.at[side, :, :, cols(c)]

    class Trip:
        def __init__(self, phase_no, sent, got, mid_got, passed, near_src, far_src, land):
            self.args = phase_no, sent, got, mid_got, passed, near_src, far_src, land

        def direct(self, c):
            _, sent, got, _, _, src, _, land = self.args
            return remote(src(c), land(1 - odd, c), sent.at[0, c], got.at[0, c], across, m)

        def far(self, c):
            _, sent, got, _, _, _, src, land = self.args
            return remote(src(c), land(odd, c), sent.at[1, c], got.at[1, c], beside, m)

        def first_hop(self, c):
            k, sent, _, mid_got, _, src, _, _ = self.args
            return remote(src(c), hop.at[k, :, :, cols(c)], sent.at[0, c], mid_got.at[c], beside, m)

        def second_hop(self, c):
            k, _, got, _, passed, _, _, land = self.args
            return remote(hop.at[k, :, :, cols(c)], land(odd, c), passed.at[c], got.at[0, c], t - 2 * step, m)

        def got_near(self, c):
            _, sent, got, _, _, src, _, land = self.args
            return remote(src(c), land(odd, c), sent.at[0, c], got.at[0, c], beside, m)

        def got_far(self, c):
            _, sent, got, _, _, _, src, land = self.args
            return remote(src(c), land(1 - odd, c), sent.at[1, c], got.at[1, c], beside, m)

        def send(self, c):
            @pl.when(c < send_hops)
            def _():
                self.first_hop(c).start()

            @pl.when(has_across & (c >= send_hops))
            def _():
                self.direct(c).start()

        def relay(self, c):
            @pl.when(c < pass_hops)
            def _():
                self.first_hop(c).wait_recv()
                self.second_hop(c).start()

        def arrived(self, c):
            self.got_far(c).wait_recv()

            @pl.when(has_across)
            def _():
                self.got_near(c).wait_recv()

        def close(self):
            each(groups, lambda c: self.far(c).wait_send())

            @pl.when(has_across)
            def _():
                each(groups, lambda c: self.direct(c).wait_send())

            each(pass_hops, lambda c: self.second_hop(c).wait_send())

    def each(n, fn):
        def step(c, carry):
            fn(c)
            return carry
        lax.fori_loop(0, n, step, 0)

    trip1 = Trip(0, s1, r1, q1, f1, lambda c: raw(near, c), lambda c: raw(far_side, c), land1)
    trip2 = Trip(1, s2, r2, q2, f2, lambda c: made(odd, c), lambda c: made(1 - odd, c), land2)
    each(send_hops, lambda c: trip1.first_hop(c).start())

    def enter(c):
        trip1.far(c).start()

        @pl.when(has_across & (c >= send_hops))
        def _():
            trip1.direct(c).start()

    each(groups, enter)

    share = remote(phase, phases.at[m], ph_sem.at[0], ph_sem.at[1], t, 1 - m)
    share.start()

    halo1[:, :, :, 0:PAD] = jnp.zeros((2, 2, EDGE, PAD), BF16)
    halo1[:, :, :, PAD + width : PAD + width + PAD] = jnp.zeros((2, 2, EDGE, PAD), BF16)
    sums[...] = jnp.zeros_like(sums)

    def blank(side):
        def step(c, carry):
            halo1[side, :, :, cols(c, PAD)] = jnp.zeros((2, EDGE, WIDE), BF16)
            halo2[side, :, :, cols(c)] = jnp.zeros((2, EDGE, WIDE), BF16)
            return carry
        lax.fori_loop(0, groups, step, 0)

    @pl.when(t == 0)
    def _():
        blank(0)

    @pl.when(t == tiles - 1)
    def _():
        blank(1)

    span_in, per = WIDE + 2 * EDGE, WIDE // BLK

    def build_group(blk, g):
        re, im = [band_rows(offs, blk, 0, g * per, per, part, total).T for part in range(2)]
        col_op[g, :span_in, :WIDE] = re.astype(BF16)
        col_op[g, :span_in, WIDE:] = im.astype(BF16)
        col_op[g, span_in:, :WIDE] = (-im).astype(BF16)
        col_op[g, span_in:, WIDE:] = re.astype(BF16)

    def build_rows(blk, lead):
        base = t * own_rows
        inner = own_rows - 2 * RADIUS
        rin[...] = stacked(*[band_rows(offs, blk, RADIUS, base + RADIUS, inner, p, total) for p in range(2)])
        red[0] = stacked(*[band_rows(offs, blk, 0, base, RADIUS, p, total) for p in range(2)])
        low = own_rows - RADIUS
        red[1] = stacked(*[band_rows(offs, blk, low, base + low, RADIUS, p, total) for p in range(2)])
        build_group(lead, 0)

    bands = blocks.shape[2]
    pltpu.emit_pipeline(
        build_rows, grid=(1,),
        in_specs=[pl.BlockSpec((2, own_rows, bands, BLK, BLK), lambda g: (0, t, 0, 0, 0)),
                  pl.BlockSpec((2, per, bands, BLK, BLK), lambda g: (0, 0, 0, 0, 0))],
    )(blocks, blocks)

    tile = pl.BlockSpec((2, rows, WIDE), lambda j: (0, 0, j))

    def column_step(left, middle, right, j, order):
        x = jnp.concatenate([window(left, middle, right, p) for p in order], axis=1)
        both = dot(x, col_op[j]).astype(BF16)
        mid[0, :, cols(j)], mid[1, :, cols(j)] = both[:, :WIDE], both[:, WIDE:]

    def now_and_then(trip, j, every, at, lead):
        @pl.when(lax.rem(j, every) == at)
        def _():
            trip.relay(lead + j // every)

    def adjoint_columns(left, middle, right, blk):
        j = pl.program_id(0)
        column_step(left, middle, right, j, (1, 0))
        build_group(blk, jnp.minimum(j + 1, groups - 1))
        now_and_then(trip1, j, 4, 3, 0)

    pltpu.emit_pipeline(
        adjoint_columns, grid=(groups,),
        in_specs=window_specs(rows, groups) + [
            pl.BlockSpec((2, per, bands, BLK, BLK), lambda j: (0, jnp.minimum(j + 1, groups - 1), 0, 0, 0))],
    )(adjoint, adjoint, adjoint, blocks)

    half = phase.shape[1] // WIDE

    def keep(src, dst):
        dst[0] = src[...]

    pltpu.emit_pipeline(
        keep, grid=(half,),
        in_specs=[pl.BlockSpec((rows, WIDE), lambda j: (0, j))],
        out_specs=[pl.BlockSpec((1, rows, WIDE), lambda j: (m, 0, j))],
    )(phase, phases)
    share.wait()
    plane = pl.BlockSpec((1, rows, WIDE), lambda j: (j // half, 0, j % half))
    inner_tile = pl.BlockSpec((2, rows - 2 * EDGE, WIDE), lambda j: (0, 0, j))

    def count(sum_re, sum_im):
        tall = sum_re.shape[0]
        sums[0] += jnp.sum(sum_re.reshape(tall // 8, 8, WIDE), axis=0)
        sums[1] += jnp.sum(sum_im.reshape(tall // 8, 8, WIDE), axis=0)

    def product(both, lit_re, lit_im):
        tall = both.shape[0] // 2
        adj_im = both[:tall].astype(BF16).astype(F32)
        adj_re = both[tall:].astype(BF16).astype(F32)
        lit_re, lit_im = lit_re.astype(F32), lit_im.astype(F32)
        t_re = adj_re * lit_re + adj_im * lit_im
        t_im = adj_re * lit_im - adj_im * lit_re
        count(t_re, t_im)
        return t_re.astype(BF16), t_im.astype(BF16)

    def inner_terms(ph, fwd, out):
        j = pl.program_id(0)
        low, high = EDGE, rows - EDGE
        for i, (a, b) in enumerate(((0, EDGE), (high, rows))):
            ends[i, 0, :, cols(j)], ends[i, 1, :, cols(j)] = turned(
                ph[0, a:b], fwd[0, a:b], fwd[1, a:b])
        lit_re, lit_im = turned(ph[0, low:high], fwd[0, low:high], fwd[1, low:high])
        both = dot(rin[...], jnp.concatenate([mid[0, :, cols(j)], mid[1, :, cols(j)]], axis=0))
        out[0], out[1] = product(both, lit_re, lit_im)
        now_and_then(trip1, j, 4, 3, 4)

    pltpu.emit_pipeline(
        inner_terms, grid=(groups,), in_specs=[plane, tile], out_specs=[inner_tile],
    )(phases, forward, t_in)

    swap_in = remote(t_in, o_in, ti_sem.at[0], ti_sem.at[1], t, 1 - m)
    swap_in.start()

    def swap_edge(c):
        return remote(te.at[:, :, cols(c)], oe.at[:, :, cols(c)], te_s.at[c], te_r.at[c], t, 1 - m)

    trip1.arrived(0)

    def halo_product(g, order):
        x = jnp.concatenate([
            jnp.concatenate([halo1[s, p, :, cols(g, 0, 2 * WIDE)] for p in order], axis=1) for s in range(2)
        ], axis=0)
        return dot(x, col_op[g]).astype(BF16)

    def edge_terms(j):
        now_and_then(trip1, j, 3, 0, 8)


        @pl.when(j < groups - 1)
        def _():
            trip1.arrived(j + 1)

        both = halo_product(j, (1, 0))
        h = (both[:, :WIDE], both[:, WIDE:])
        top = jnp.concatenate([h[0][:EDGE], mid[0, : 2 * EDGE, cols(j)], h[1][:EDGE], mid[1, : 2 * EDGE, cols(j)]], axis=0)
        low = rows - 2 * EDGE
        bottom = jnp.concatenate([mid[0, low:, cols(j)], h[0][EDGE:], mid[1, low:, cols(j)], h[1][EDGE:]], axis=0)
        for i, field in enumerate((top, bottom)):
            span = slice(i * EDGE, (i + 1) * EDGE)
            te[0, span, cols(j)], te[1, span, cols(j)] = product(
                dot(red[i], field), ends[i, 0, :, cols(j)], ends[i, 1, :, cols(j)])
        swap_edge(j).start()

    each(groups, edge_terms)

    slots[me] = sums[:, :, :128] + sums[:, :, 128:]

    def report(p):
        who = peer(p)
        return pltpu.make_async_remote_copy(
            src_ref=slots.at[me], dst_ref=slots.at[me], send_sem=ar_s.at[p], recv_sem=ar_r.at[p],
            device_id=who, device_id_type=MESH)

    def heard(p):
        who = lax.rem(me + peers - p, peers)
        return pltpu.make_async_remote_copy(
            src_ref=slots.at[who], dst_ref=slots.at[who], send_sem=ar_s.at[p], recv_sem=ar_r.at[p],
            device_id=peer(p), device_id_type=MESH)

    for p in range(1, peers):
        report(p).start()
    def settle():
        for p in range(1, peers):
            heard(p).wait_recv()
        for i, who in enumerate((m, 1 - m)):
            value = slots[who]
            for k in range(1, tiles):
                value = value + slots[2 * k + who]
            for part in range(2):
                coef[2 * i + part] = jnp.sum(value[part]) * (1.0 / (4.0 * width * 2))

    def gradient(own_re, own_im, other_re, other_im):
        return (coef[0] * own_im.astype(F32) - coef[1] * own_re.astype(F32)) + (
            coef[2] * other_im.astype(F32) - coef[3] * other_re.astype(F32))

    far = rows // EDGE - 1

    def chunk(j):
        return jnp.minimum(j, groups - 1)

    def edge_launch(p_top, p_bottom, f_top, f_bottom):
        j = pl.program_id(0)

        pl.when(j == 0)(settle)

        @pl.when(j < groups)
        def _():
            swap_edge(j).wait_recv()
            for i, (ph, fwd) in enumerate(((p_top, f_top), (p_bottom, f_bottom))):
                span = slice(i * EDGE, (i + 1) * EDGE)
                after = ph[0] - gradient(te[0, span, cols(j)], te[1, span, cols(j)],
                                         oe[0, span, cols(j)], oe[1, span, cols(j)])
                halo1[i, 0, :, cols(j, PAD)], halo1[i, 1, :, cols(j, PAD)] = turned(after, fwd[0], fwd[1])

        @pl.when(j > 0)
        def _():
            g = j - 1
            both = halo_product(g, (0, 1))
            o_re, o_im = both[:, :WIDE], both[:, WIDE:]
            for s in range(2):
                ends[s, 0, :, cols(g)] = o_re[s * EDGE : (s + 1) * EDGE]
                ends[s, 1, :, cols(g)] = o_im[s * EDGE : (s + 1) * EDGE]

            trip2.send(g)
            trip2.far(g).start()

    pltpu.emit_pipeline(
        edge_launch, grid=(groups + 1,),
        in_specs=[
            pl.BlockSpec((1, EDGE, WIDE), lambda j: (chunk(j) // half, 0, chunk(j) % half)),
            pl.BlockSpec((1, EDGE, WIDE), lambda j: (chunk(j) // half, far, chunk(j) % half)),
            pl.BlockSpec((2, EDGE, WIDE), lambda j: (0, 0, chunk(j))),
            pl.BlockSpec((2, EDGE, WIDE), lambda j: (0, far, chunk(j))),
        ],
    )(phases, phases, forward, forward)

    swap_in.wait()

    def launch_tile(own, other, ph, fwd, out):
        j = pl.program_id(0)
        for k, (a, b) in enumerate(((0, EDGE), (EDGE, rows - EDGE), (rows - EDGE, rows))):
            if k == 1:
                grad = gradient(own[0], own[1], other[0], other[1])
            else:
                span = slice((k // 2) * EDGE, (k // 2 + 1) * EDGE)
                grad = gradient(te[0, span, cols(j)], te[1, span, cols(j)],
                                oe[0, span, cols(j)], oe[1, span, cols(j)])
            after = ph[0, a:b] - grad
            @pl.when(j // half == m)
            def _(a=a, b=b, after=after):
                updated[a:b, cols(j - m * half)] = after

            out[0, a:b], out[1, a:b] = turned(after, fwd[0, a:b], fwd[1, a:b])
        now_and_then(trip2, j, 3, 2, 0)

    pltpu.emit_pipeline(
        launch_tile, grid=(groups,),
        in_specs=[inner_tile, inner_tile, plane, tile],
        out_specs=[tile],
    )(t_in, o_in, phases, forward, lau)

    def forward_columns(left, middle, right):
        j = pl.program_id(0)
        column_step(left, middle, right, j, (0, 1))
        now_and_then(trip2, j, 4, 3, 5)

    pltpu.emit_pipeline(
        forward_columns, grid=(groups,), in_specs=window_specs(rows, groups),
    )(lau, lau, lau)

    for p in range(1, peers):
        report(p).wait_send()
    each(groups, lambda c: swap_edge(c).wait_send())

    def last_rows(c):
        now_and_then(trip2, c, 3, 0, 9)
        trip2.arrived(c)
        low = rows - 2 * EDGE
        own = [mid[p, :, cols(c)] for p in range(2)]
        near_by = [[halo2[s, p, :, cols(c)] for p in range(2)] for s in range(2)]
        pieces = (
            (EDGE, rin[...], own),
            (0, red[0], [near_by[0][0], own[0][: 2 * EDGE], near_by[0][1], own[1][: 2 * EDGE]]),
            (rows - EDGE, red[1], [own[0][low:], near_by[1][0], own[1][low:], near_by[1][1]]),
        )
        done = [(start, dot(op, jnp.concatenate(parts, axis=0)).astype(BF16)) for start, op, parts in pieces]
        for start, both in done:
            tall = both.shape[0] // 2
            mid[0, start : start + tall, cols(c)] = both[:tall]
            mid[1, start : start + tall, cols(c)] = both[tall:]

    each(groups, last_rows)
    trip1.close()
    trip2.close()


def exchange(forward, adjoint, phase, blocks, offsets):
    tiles = lax.axis_size("tile")
    _, rows, width = forward.shape
    half = phase.shape[1]
    groups = width // WIDE
    inner = rows - 2 * EDGE
    hbm = pl.BlockSpec(memory_space=pl.ANY)
    dma = pltpu.SemaphoreType.DMA
    field = jax.ShapeDtypeStruct((2, rows, width), BF16)
    plane = jax.ShapeDtypeStruct((2, rows, half), F32)
    rin = (2 * inner, 2 * rows)
    red = (2, 2 * EDGE, 6 * EDGE)
    edges = (2, 2, EDGE, width)
    shapes = (
        pltpu.VMEM(field.shape, BF16), field,
        jax.ShapeDtypeStruct((2, inner, width), BF16),
        jax.ShapeDtypeStruct((2, inner, width), BF16),
        plane, pltpu.VMEM((rows, half), F32),
        jax.ShapeDtypeStruct(edges, BF16),
    )
    local = pl.BlockSpec(memory_space=pltpu.VMEM)
    edge = pltpu.VMEM((2, 2 * EDGE, width), BF16)
    peers = 2 * tiles
    out = pl.pallas_call(
        functools.partial(exchange_kernel, tiles),
        out_shape=shapes,
        in_specs=[pl.BlockSpec(memory_space=pltpu.SMEM)] + [hbm] * 4,
        out_specs=(local, hbm, hbm, hbm, hbm, local, hbm),
        scratch_shapes=[
            pltpu.VMEM((2, 2, EDGE, width + 2 * PAD), BF16),
            pltpu.VMEM(edges, BF16),
            pltpu.VMEM((groups, 2 * (WIDE + 2 * EDGE), 2 * WIDE), BF16),
            pltpu.VMEM(rin, BF16), pltpu.VMEM(red, BF16),
            pltpu.VMEM((2, 2, EDGE, width), BF16),
            edge, edge,
            pltpu.VMEM((2, 8, WIDE), F32),
            pltpu.VMEM((peers, 2, 8, 128), F32),
            pltpu.SMEM((4,), F32),
            dma((2,)), dma((2, groups)), dma((2, groups)), dma((groups,)), dma((groups,)), dma((2,)),
            dma((groups,)), dma((groups,)), dma((peers,)), dma((peers,)),
            dma((2, groups)), dma((2, groups)), dma((groups,)), dma((groups,)),
        ],
        compiler_params=pltpu.CompilerParams(
            vmem_limit_bytes=49 * 1024 * 1024, collective_id=0, has_side_effects=True),
        cost_estimate=cost(50 * rows * width * 512, 100 * rows * width),
        name="exchange",
    )(offsets.T, blocks, adjoint, forward, phase)
    return out[0], out[5]


def exchange_edges(first, last):
    tiles = lax.axis_size("tile")
    top = lax.ppermute(last, "tile", [(t, t + 1) for t in range(tiles - 1)])
    bottom = lax.ppermute(first, "tile", [(t + 1, t) for t in range(tiles - 1)])
    return top, bottom


def body(forward, adjoint_next, phase, blocks, offsets):
    block_total = offsets.shape[0]
    tiles = lax.axis_size("tile")
    modes = lax.axis_size("mode")
    mode = lax.axis_index("mode")
    rows, width = forward.shape[2], forward.shape[3]
    adjoint = adjoint_next[0]
    if modes == 2 and tiles == 8 and width == 16 * WIDE and rows // BLK == 2 * RADIUS + WIDE // BLK:
        forward_next, phase_next = exchange(forward[0], adjoint, phase, blocks, offsets)
        return phase_next, forward_next[None]
    top, bottom = exchange_edges(adjoint[:, :EDGE], adjoint[:, rows - EDGE :])
    phases = lax.all_gather(phase, "mode", axis=0, tiled=False)

    raw_index = jnp.arange(block_total, dtype=jnp.int32)[:, None] + offsets
    inside = (raw_index >= 0) & (raw_index < block_total)
    pos = jnp.where(inside, offsets + RADIUS, -1).astype(jnp.int32)
    own_blocks = block_total // tiles
    split = own_blocks == 2 * RADIUS + WIDE // BLK
    start = lax.axis_index("tile") * own_blocks
    column_op = build(blocks, pos, WIDE // BLK, True)
    own_part = lax.dynamic_slice_in_dim(blocks, start, own_blocks, 1)
    own_pos = lax.dynamic_slice_in_dim(pos, start, own_blocks, 0)
    if split:
        inner = slice(RADIUS, own_blocks - RADIUS)
        row_op = build(own_part[:, inner], own_pos[inner], WIDE // BLK, False)
        ends = [own_part[:, :RADIUS], own_part[:, own_blocks - RADIUS :]]
        end_pos = [own_pos[:RADIUS], own_pos[own_blocks - RADIUS :]]
        edge_op = build(jnp.concatenate(ends, 1), jnp.concatenate(end_pos, 0), RADIUS, False)
    else:
        row_op = build(own_part, own_pos, min(WIDE // BLK, own_blocks), False)

    back_middle = column_pass(adjoint, column_op, True)
    lit = light(phases, forward)
    swap = [(m, (m + 1) % modes) for m in range(modes)]
    if split:
        t_in, s_in = adjoint_inner(back_middle, row_op, lit)
        o_in = lax.ppermute(t_in, "mode", swap)
        terms, sums = adjoint_edges(top, bottom, column_op, back_middle, edge_op, lit, s_in)
    else:
        terms, sums = adjoint_rows(top, bottom, column_op, back_middle, row_op, lit)
    other = lax.ppermute(terms, "mode", swap)
    own = jnp.sum(sums, axis=(1, 2))
    table = jnp.where(jnp.arange(modes)[:, None] == mode, own[None, :], 0.0)
    table = lax.psum(table, ("tile", "mode"))
    order = jnp.where(mode == 0, table, table[::-1])
    coef = order.reshape(-1) * (1.0 / (4.0 * width * modes))

    if split:
        first, last = ring_edges(coef, terms, other, phases, forward, column_op)
        top, bottom = exchange_edges(first, last)
        launched, updated = launch_split(coef, t_in, o_in, terms, other, phases, forward)
    else:
        edges = launch_edges(coef, terms, other, phases, forward)
        edges = column_pass(edges, column_op, False)
        top, bottom = exchange_edges(edges[:, :EDGE], edges[:, EDGE:])
        launched, updated = launch(coef, terms, other, phases, forward)
    middle = column_pass(launched, column_op, False)
    phase_next = lax.dynamic_index_in_dim(updated, mode, 0, keepdims=False)
    if split:
        whole = forward_inner(middle, row_op)
        return phase_next, forward_edges(top, middle, bottom, edge_op, whole)
    return phase_next, forward_rows(top, middle, bottom, row_op)


def solution(mesh):
    placed = (
        P(("design", "mode"), None, "tile", None),
        P(("design", "mode"), None, "tile", None),
        P(("design", "tile"), "mode"),
        P(None, "design", None, None, None),
        P("design", None),
    )
    return jax.shard_map(
        body,
        mesh=mesh,
        in_specs=placed,
        out_specs=(P(("design", "tile"), "mode"), P(("design", "mode"), None, "tile", None)),
        check_vma=False,
    )
```

```python
import functools

import jax
import jax.numpy as jnp
from jax import lax
from jax.experimental import pallas as pl
from jax.experimental.pallas import tpu as pltpu
from jax.sharding import PartitionSpec as P

BLK = 64
RADIUS = 2
EDGE = RADIUS * BLK
WIDE = 256
VMEM_LIMIT = 44 * 1024 * 1024

F32 = jnp.float32
BF16 = jnp.bfloat16


def params():
    return pltpu.CompilerParams(vmem_limit_bytes=VMEM_LIMIT)


def cost(flops, moved):
    return pl.CostEstimate(flops=int(flops), bytes_accessed=int(moved), transcendentals=0)


def sincos(x):
    turns = jnp.round(x * 0.15915494309189535)
    r = x - turns * 6.28125
    r = r - turns * 1.935307179586232e-3
    z = r * r
    half_sine = r * (0.7071067690849304 + z * (-0.029462767764925957 + z * (
        0.00036827221629209816 + z * (-2.1885971364099532e-06 + z * 7.195012585725635e-09))))
    half_cosine = 1.4142135381698608 + z * (-0.17677634954452515 + z * (
        0.003682573325932026 + z * (-3.0612263799412176e-05 + z * 1.2788676428954204e-07)))
    return half_sine * half_cosine, 1.0 - half_sine * half_sine


def dot(a, b):
    return jnp.dot(a, b, preferred_element_type=F32)


def build_kernel(pos_ref, blk_ref, out_ref, *, group, transposed):
    base = pl.program_id(0) * group
    zero = jnp.zeros((BLK, BLK), F32)
    for part in range(2):
        strips = []
        for r in range(group):
            own = [blk_ref[part, r, k].astype(F32) for k in range(blk_ref.shape[2])]
            pieces = [zero] * r
            for d in range(2 * RADIUS + 1):
                piece = zero
                for k, block in enumerate(own):
                    piece = jnp.where(pos_ref[base + r, k] == d, block, piece)
                pieces.append(piece)
            pieces += [zero] * (group - 1 - r)
            strips.append(jnp.concatenate(pieces, axis=1))
        full = jnp.concatenate(strips, axis=0)
        if transposed:
            full = full.T
        out_ref[0, part] = full.astype(BF16)


def build(blocks, pos, group, transposed):
    _, rows, bands, _, _ = blocks.shape
    tall, wide = group * BLK, (group + 2 * RADIUS) * BLK
    if transposed:
        tall, wide = wide, tall
    count = rows // group
    return pl.pallas_call(
        functools.partial(build_kernel, group=group, transposed=transposed),
        out_shape=jax.ShapeDtypeStruct((count, 2, tall, wide), BF16),
        grid_spec=pltpu.PrefetchScalarGridSpec(
            num_scalar_prefetch=1,
            grid=(count,),
            in_specs=[pl.BlockSpec((2, group, bands, BLK, BLK), lambda g, p: (0, g, 0, 0, 0))],
            out_specs=pl.BlockSpec((1, 2, tall, wide), lambda g, p: (g, 0, 0, 0)),
        ),
        compiler_params=params(),
        cost_estimate=cost(0, 16 * rows * bands * BLK * BLK),
        name="build_operator",
    )(pos, blocks)


def window_specs(rows, groups):
    last = 2 * groups - 1
    return [
        pl.BlockSpec((2, rows, 128), lambda j: (0, 0, jnp.maximum(2 * j - 1, 0))),
        pl.BlockSpec((2, rows, WIDE), lambda j: (0, 0, j)),
        pl.BlockSpec((2, rows, 128), lambda j: (0, 0, jnp.minimum(2 * j + 2, last))),
    ]


def window(left, mid, right, part):
    return jnp.concatenate([left[part], mid[part], right[part]], axis=1)


def column_product(x_re, x_im, op_ref, conj):
    op_re, op_im = op_ref[0, 0], op_ref[0, 1]
    rr, ii = dot(x_re, op_re), dot(x_im, op_im)
    ri, ir = dot(x_re, op_im), dot(x_im, op_re)
    if conj:
        return (rr + ii).astype(BF16), (ri - ir).astype(BF16)
    return (rr - ii).astype(BF16), (ri + ir).astype(BF16)


def column_kernel(left, mid, right, op_ref, out_ref, *, conj):
    out_re, out_im = column_product(
        window(left, mid, right, 0), window(left, mid, right, 1), op_ref, conj
    )
    out_ref[0] = out_re
    out_ref[1] = out_im


def column_pass(field, op, conj):
    _, rows, width = field.shape
    groups = width // WIDE
    return pl.pallas_call(
        functools.partial(column_kernel, conj=conj),
        out_shape=jax.ShapeDtypeStruct(field.shape, BF16),
        grid=(groups,),
        in_specs=window_specs(rows, groups)
        + [pl.BlockSpec((1, 2, op.shape[2], WIDE), lambda j: (j, 0, 0, 0))],
        out_specs=pl.BlockSpec((2, rows, WIDE), lambda j: (0, 0, j)),
        compiler_params=params(),
        cost_estimate=cost(8 * rows * width * op.shape[2], 12 * rows * width + 2 * op.size),
        name="column_pass",
    )(field, field, field, op)


def row_groups(top, main, bottom, row_op):
    whole_re = jnp.concatenate([top[0], main[0], bottom[0]], axis=0)
    whole_im = jnp.concatenate([top[1], main[1], bottom[1]], axis=0)
    count, _, tall, deep = row_op.shape
    for i in range(count):
        m_re = whole_re[i * tall : i * tall + deep]
        m_im = whole_im[i * tall : i * tall + deep]
        op_re, op_im = row_op[i, 0], row_op[i, 1]
        out_re = dot(op_re, m_re) - dot(op_im, m_im)
        out_im = dot(op_re, m_im) + dot(op_im, m_re)
        yield i * tall, tall, out_re, out_im


def adjoint_row_kernel(tl, tm, tr, bl, bm, br, op_ref, main, row_op, lit, terms, sums):
    x_re = jnp.concatenate([window(tl, tm, tr, 0), window(bl, bm, br, 0)], axis=0)
    x_im = jnp.concatenate([window(tl, tm, tr, 1), window(bl, bm, br, 1)], axis=0)
    halo_re, halo_im = column_product(x_re, x_im, op_ref, True)

    @pl.when(pl.program_id(0) == 0)
    def _():
        sums[...] = jnp.zeros_like(sums)

    top = (halo_re[:EDGE], halo_im[:EDGE])
    bottom = (halo_re[EDGE:], halo_im[EDGE:])
    for low, tall, cj_re, cj_im in row_groups(top, main, bottom, row_op):
        cj_re = cj_re.astype(BF16).astype(F32)
        cj_im = cj_im.astype(BF16).astype(F32)
        lit_re = lit[0, low : low + tall].astype(F32)
        lit_im = lit[1, low : low + tall].astype(F32)
        t_re = cj_re * lit_re - cj_im * lit_im
        t_im = cj_re * lit_im + cj_im * lit_re
        terms[0, low : low + tall] = t_re.astype(BF16)
        terms[1, low : low + tall] = t_im.astype(BF16)
        sums[0] += jnp.sum(t_re.reshape(tall // 8, 8, WIDE), axis=0)
        sums[1] += jnp.sum(t_im.reshape(tall // 8, 8, WIDE), axis=0)


def adjoint_rows(top, bottom, op, main, row_op, lit):
    _, rows, width = main.shape
    groups = width // WIDE
    edge = window_specs(EDGE, groups)
    tile = pl.BlockSpec((2, rows, WIDE), lambda j: (0, 0, j))
    return pl.pallas_call(
        adjoint_row_kernel,
        out_shape=(
            jax.ShapeDtypeStruct(main.shape, BF16),
            jax.ShapeDtypeStruct((2, 8, WIDE), F32),
        ),
        grid=(groups,),
        in_specs=edge
        + edge
        + [
            pl.BlockSpec((1, 2, op.shape[2], WIDE), lambda j: (j, 0, 0, 0)),
            tile,
            pl.BlockSpec(row_op.shape, lambda j: (0, 0, 0, 0)),
            tile,
        ],
        out_specs=(tile, pl.BlockSpec((2, 8, WIDE), lambda j: (0, 0, 0))),
        compiler_params=params(),
        cost_estimate=cost(12 * rows * width * op.shape[2], 16 * rows * width),
        name="adjoint_rows",
    )(top, top, top, bottom, bottom, bottom, op, main, row_op, lit)


def forward_row_kernel(top, main, bottom, row_op, out):
    for low, tall, out_re, out_im in row_groups(top, main, bottom, row_op):
        out[0, 0, low : low + tall] = out_re.astype(BF16)
        out[0, 1, low : low + tall] = out_im.astype(BF16)


def forward_rows(top, main, bottom, row_op):
    _, rows, width = main.shape
    groups = width // WIDE
    edge = pl.BlockSpec((2, EDGE, WIDE), lambda j: (0, 0, j))
    return pl.pallas_call(
        forward_row_kernel,
        out_shape=jax.ShapeDtypeStruct((1,) + main.shape, BF16),
        grid=(groups,),
        in_specs=[
            edge,
            pl.BlockSpec((2, rows, WIDE), lambda j: (0, 0, j)),
            edge,
            pl.BlockSpec(row_op.shape, lambda j: (0, 0, 0, 0)),
        ],
        out_specs=pl.BlockSpec((1, 2, rows, WIDE), lambda j: (0, 0, 0, j)),
        compiler_params=params(),
        cost_estimate=cost(8 * rows * width * row_op.shape[3], 10 * rows * width),
        name="forward_rows",
    )(top, main, bottom, row_op)


def lit_kernel(phase, fwd, lit):
    sine, cosine = sincos(phase[0])
    f_re, f_im = fwd[0, 0].astype(F32), fwd[0, 1].astype(F32)
    lit[0] = (cosine * f_re - sine * f_im).astype(BF16)
    lit[1] = (sine * f_re + cosine * f_im).astype(BF16)


def light(phases, forward):
    _, _, rows, width = forward.shape
    half = phases.shape[2] // WIDE
    return pl.pallas_call(
        lit_kernel,
        out_shape=jax.ShapeDtypeStruct(forward.shape[1:], BF16),
        grid=(width // WIDE,),
        in_specs=[
            pl.BlockSpec((1, rows, WIDE), lambda j: (j // half, 0, j % half)),
            pl.BlockSpec((1, 2, rows, WIDE), lambda j: (0, 0, 0, j)),
        ],
        out_specs=pl.BlockSpec((2, rows, WIDE), lambda j: (0, 0, j)),
        compiler_params=params(),
        cost_estimate=cost(60 * rows * width, 12 * rows * width),
        name="light",
    )(phases, forward)


def launch_values(coef, terms, other, phase, fwd, launched):
    gradient = (coef[0] * terms[1].astype(F32) - coef[1] * terms[0].astype(F32)) + (
        coef[2] * other[1].astype(F32) - coef[3] * other[0].astype(F32)
    )
    updated = phase[0] - gradient
    sine, cosine = sincos(updated)
    f_re, f_im = fwd[0, 0].astype(F32), fwd[0, 1].astype(F32)
    launched[0] = (cosine * f_re - sine * f_im).astype(BF16)
    launched[1] = (sine * f_re + cosine * f_im).astype(BF16)
    return updated


def launch_kernel(coef, terms, other, phase, fwd, launched, phase_next):
    phase_next[0] = launch_values(coef, terms, other, phase, fwd, launched)


def launch(coef, terms, other, phases, forward):
    _, _, rows, width = forward.shape
    half = phases.shape[2] // WIDE
    tile = pl.BlockSpec((2, rows, WIDE), lambda j, c: (0, 0, j))
    plane = pl.BlockSpec((1, rows, WIDE), lambda j, c: (j // half, 0, j % half))
    return pl.pallas_call(
        launch_kernel,
        out_shape=(
            jax.ShapeDtypeStruct(forward.shape[1:], BF16),
            jax.ShapeDtypeStruct(phases.shape, F32),
        ),
        grid_spec=pltpu.PrefetchScalarGridSpec(
            num_scalar_prefetch=1,
            grid=(width // WIDE,),
            in_specs=[
                tile,
                tile,
                plane,
                pl.BlockSpec((1, 2, rows, WIDE), lambda j, c: (0, 0, 0, j)),
            ],
            out_specs=(tile, plane),
        ),
        compiler_params=params(),
        cost_estimate=cost(60 * rows * width, 24 * rows * width),
        name="launch",
    )(coef, terms, other, phases, forward)


def launch_edge_kernel(coef, terms, other, phase, fwd, launched):
    launch_values(coef, terms, other, phase, fwd, launched)


def launch_edges(coef, terms, other, phases, forward):
    _, _, rows, width = forward.shape
    wide = 2 * WIDE
    half = phases.shape[2] // wide
    far = rows // EDGE - 1
    tile = pl.BlockSpec((2, EDGE, wide), lambda e, j, c: (0, e * far, j))
    return pl.pallas_call(
        launch_edge_kernel,
        out_shape=jax.ShapeDtypeStruct((2, 2 * EDGE, width), BF16),
        grid_spec=pltpu.PrefetchScalarGridSpec(
            num_scalar_prefetch=1,
            grid=(2, width // wide),
            in_specs=[
                tile,
                tile,
                pl.BlockSpec((1, EDGE, wide), lambda e, j, c: (j // half, e * far, j % half)),
                pl.BlockSpec((1, 2, EDGE, wide), lambda e, j, c: (0, 0, e * far, j)),
            ],
            out_specs=pl.BlockSpec((2, EDGE, wide), lambda e, j, c: (0, e, j)),
        ),
        compiler_params=params(),
        cost_estimate=cost(120 * EDGE * width, 48 * EDGE * width),
        name="launch_edges",
    )(coef, terms, other, phases, forward)


def complex_rows(op_re, op_im, m_re, m_im):
    return dot(op_re, m_re) - dot(op_im, m_im), dot(op_re, m_im) + dot(op_im, m_re)


def add_terms(cj_re, cj_im, lit_re, lit_im, terms, sums, low):
    tall = cj_re.shape[0]
    cj_re = cj_re.astype(BF16).astype(F32)
    cj_im = cj_im.astype(BF16).astype(F32)
    lit_re, lit_im = lit_re.astype(F32), lit_im.astype(F32)
    t_re = cj_re * lit_re - cj_im * lit_im
    t_im = cj_re * lit_im + cj_im * lit_re
    terms[0, low : low + tall] = t_re.astype(BF16)
    terms[1, low : low + tall] = t_im.astype(BF16)
    sums[0] += jnp.sum(t_re.reshape(tall // 8, 8, WIDE), axis=0)
    sums[1] += jnp.sum(t_im.reshape(tall // 8, 8, WIDE), axis=0)


def adjoint_inner_kernel(main, row_op, lit, terms, sums):
    @pl.when(pl.program_id(0) == 0)
    def _():
        sums[...] = jnp.zeros_like(sums)

    rows = main.shape[1]
    cj_re, cj_im = complex_rows(row_op[0, 0], row_op[0, 1], main[0], main[1])
    add_terms(cj_re, cj_im, lit[0, EDGE : rows - EDGE], lit[1, EDGE : rows - EDGE], terms, sums, 0)


def adjoint_inner(main, row_op, lit):
    _, rows, width = main.shape
    inner = rows - 2 * EDGE
    tile = pl.BlockSpec((2, rows, WIDE), lambda j: (0, 0, j))
    return pl.pallas_call(
        adjoint_inner_kernel,
        out_shape=(
            jax.ShapeDtypeStruct((2, inner, width), BF16),
            jax.ShapeDtypeStruct((2, 8, WIDE), F32),
        ),
        grid=(width // WIDE,),
        in_specs=[tile, pl.BlockSpec(row_op.shape, lambda j: (0, 0, 0, 0)), tile],
        out_specs=(
            pl.BlockSpec((2, inner, WIDE), lambda j: (0, 0, j)),
            pl.BlockSpec((2, 8, WIDE), lambda j: (0, 0, 0)),
        ),
        compiler_params=params(),
        cost_estimate=cost(8 * inner * width * rows, 12 * rows * width),
        name="adjoint_inner",
    )(main, row_op, lit)


def edge_windows(main, part, top, bottom):
    rows = main.shape[1]
    return (
        jnp.concatenate([top, main[part, : 2 * EDGE]], axis=0),
        jnp.concatenate([main[part, rows - 2 * EDGE :], bottom], axis=0),
    )


def adjoint_edge_kernel(tl, tm, tr, bl, bm, br, op_ref, main, edge_op, lit, before, terms, sums):
    x_re = jnp.concatenate([window(tl, tm, tr, 0), window(bl, bm, br, 0)], axis=0)
    x_im = jnp.concatenate([window(tl, tm, tr, 1), window(bl, bm, br, 1)], axis=0)
    halo_re, halo_im = column_product(x_re, x_im, op_ref, True)

    @pl.when(pl.program_id(0) == 0)
    def _():
        sums[...] = before[...]

    rows = main.shape[1]
    res = edge_windows(main, 0, halo_re[:EDGE], halo_re[EDGE:])
    ims = edge_windows(main, 1, halo_im[:EDGE], halo_im[EDGE:])
    for i, low in enumerate((0, rows - EDGE)):
        cj_re, cj_im = complex_rows(edge_op[i, 0], edge_op[i, 1], res[i], ims[i])
        add_terms(cj_re, cj_im, lit[0, low : low + EDGE], lit[1, low : low + EDGE], terms, sums, i * EDGE)


def adjoint_edges(top, bottom, op, main, edge_op, lit, before):
    _, rows, width = main.shape
    groups = width // WIDE
    edge = window_specs(EDGE, groups)
    tile = pl.BlockSpec((2, rows, WIDE), lambda j: (0, 0, j))
    return pl.pallas_call(
        adjoint_edge_kernel,
        out_shape=(
            jax.ShapeDtypeStruct((2, 2 * EDGE, width), BF16),
            jax.ShapeDtypeStruct((2, 8, WIDE), F32),
        ),
        grid=(groups,),
        in_specs=edge
        + edge
        + [
            pl.BlockSpec((1, 2, op.shape[2], WIDE), lambda j: (j, 0, 0, 0)),
            tile,
            pl.BlockSpec(edge_op.shape, lambda j: (0, 0, 0, 0)),
            tile,
            pl.BlockSpec((2, 8, WIDE), lambda j: (0, 0, 0)),
        ],
        out_specs=(
            pl.BlockSpec((2, 2 * EDGE, WIDE), lambda j: (0, 0, j)),
            pl.BlockSpec((2, 8, WIDE), lambda j: (0, 0, 0)),
        ),
        compiler_params=params(),
        cost_estimate=cost(32 * EDGE * width * op.shape[2], 16 * rows * width),
        name="adjoint_edges",
    )(top, top, top, bottom, bottom, bottom, op, main, edge_op, lit, before)


def forward_inner_kernel(main, row_op, out):
    out_re, out_im = complex_rows(row_op[0, 0], row_op[0, 1], main[0], main[1])
    out[0, 0] = out_re.astype(BF16)
    out[0, 1] = out_im.astype(BF16)


def forward_inner(main, row_op):
    _, rows, width = main.shape
    inner = rows // EDGE - 2
    deep = row_op.shape[3]
    return pl.pallas_call(
        forward_inner_kernel,
        out_shape=jax.ShapeDtypeStruct((1,) + main.shape, BF16),
        grid=(width // WIDE, inner),
        in_specs=[
            pl.BlockSpec((2, rows, WIDE), lambda j, i: (0, 0, j)),
            pl.BlockSpec((1, 2, EDGE, deep), lambda j, i: (0, 0, i, 0)),
        ],
        out_specs=pl.BlockSpec((1, 2, EDGE, WIDE), lambda j, i: (0, 0, i + 1, j)),
        compiler_params=params(),
        cost_estimate=cost(8 * inner * EDGE * width * rows, 8 * rows * width),
        name="forward_inner",
    )(main, row_op)


def forward_edge_kernel(top, main, bottom, edge_op, whole, out):
    side = pl.program_id(1)

    def run(m_re, m_im):
        out_re, out_im = complex_rows(edge_op[0, 0], edge_op[0, 1], m_re, m_im)
        out[0, 0] = out_re.astype(BF16)
        out[0, 1] = out_im.astype(BF16)

    @pl.when(side == 0)
    def _():
        run(*[jnp.concatenate([top[p], main[p]], axis=0) for p in range(2)])

    @pl.when(side == 1)
    def _():
        run(*[jnp.concatenate([main[p], bottom[p]], axis=0) for p in range(2)])


def forward_edges(top, main, bottom, edge_op, whole):
    _, rows, width = main.shape
    wide = 2 * WIDE
    near = rows // (2 * EDGE) - 1
    far = rows // EDGE - 1
    halo = pl.BlockSpec((2, EDGE, wide), lambda j, i: (0, 0, j))
    return pl.pallas_call(
        forward_edge_kernel,
        out_shape=jax.ShapeDtypeStruct(whole.shape, BF16),
        grid=(width // wide, 2),
        in_specs=[
            halo,
            pl.BlockSpec((2, 2 * EDGE, wide), lambda j, i: (0, i * near, j)),
            halo,
            pl.BlockSpec((1, 2, EDGE, edge_op.shape[3]), lambda j, i: (i, 0, 0, 0)),
            pl.BlockSpec(memory_space=pl.ANY),
        ],
        out_specs=pl.BlockSpec((1, 2, EDGE, wide), lambda j, i: (0, 0, i * far, j)),
        input_output_aliases={4: 0},
        compiler_params=params(),
        cost_estimate=cost(16 * EDGE * width * edge_op.shape[3], 24 * EDGE * width),
        name="forward_edges",
    )(top, main, bottom, edge_op, whole)


def gradient_of(coef, terms, other, rows):
    return (coef[0] * terms[1, rows].astype(F32) - coef[1] * terms[0, rows].astype(F32)) + (
        coef[2] * other[1, rows].astype(F32) - coef[3] * other[0, rows].astype(F32)
    )


def turned(phase, f_re, f_im):
    sine, cosine = sincos(phase)
    f_re, f_im = f_re.astype(F32), f_im.astype(F32)
    return (cosine * f_re - sine * f_im).astype(BF16), (sine * f_re + cosine * f_im).astype(BF16)


def ring_edge_kernel(coef, terms, other, p_top, p_bottom, f_top, f_bottom, op_ref, first, last, ring):
    step = pl.program_id(0)

    @pl.when(step == 0)
    def _():
        ring[3] = jnp.zeros(ring.shape[1:], BF16)

    left, mid, right = (step + 1) % 4, (step + 2) % 4, (step + 3) % 4

    def part(k):
        return jnp.concatenate(
            [ring[left, k, :, WIDE - EDGE :], ring[mid, k], ring[right, k, :, :EDGE]], axis=1
        )

    out_re, out_im = column_product(part(0), part(1), op_ref, False)
    first[0] = out_re[:EDGE]
    first[1] = out_im[:EDGE]
    last[0] = out_re[EDGE:]
    last[1] = out_im[EDGE:]
    for i, (phase, fwd) in enumerate(((p_top, f_top), (p_bottom, f_bottom))):
        span = slice(i * EDGE, (i + 1) * EDGE)
        updated = phase[0] - gradient_of(coef, terms, other, span)
        l_re, l_im = turned(updated, fwd[0, 0], fwd[0, 1])
        ring[step % 4, 0, span] = l_re
        ring[step % 4, 1, span] = l_im


def ring_edges(coef, terms, other, phases, forward, op):
    _, _, rows, width = forward.shape
    groups = width // WIDE
    half = phases.shape[2] // WIDE
    far = rows // EDGE - 1

    def chunk(j):
        return jnp.minimum(j, groups - 1)

    tile = pl.BlockSpec((2, 2 * EDGE, WIDE), lambda j, c: (0, 0, chunk(j)))
    out = pl.BlockSpec((2, EDGE, WIDE), lambda j, c: (0, 0, jnp.maximum(j - 2, 0)))
    shape = jax.ShapeDtypeStruct((2, EDGE, width), BF16)
    return pl.pallas_call(
        ring_edge_kernel,
        out_shape=(shape, shape),
        grid_spec=pltpu.PrefetchScalarGridSpec(
            num_scalar_prefetch=1,
            grid=(groups + 2,),
            in_specs=[
                tile,
                tile,
                pl.BlockSpec((1, EDGE, WIDE), lambda j, c: (chunk(j) // half, 0, chunk(j) % half)),
                pl.BlockSpec((1, EDGE, WIDE), lambda j, c: (chunk(j) // half, far, chunk(j) % half)),
                pl.BlockSpec((1, 2, EDGE, WIDE), lambda j, c: (0, 0, 0, chunk(j))),
                pl.BlockSpec((1, 2, EDGE, WIDE), lambda j, c: (0, 0, far, chunk(j))),
                pl.BlockSpec((1, 2, op.shape[2], WIDE), lambda j, c: (jnp.maximum(j - 2, 0), 0, 0, 0)),
            ],
            out_specs=(out, out),
            scratch_shapes=[pltpu.VMEM((4, 2, 2 * EDGE, WIDE), BF16)],
        ),
        compiler_params=params(),
        cost_estimate=cost(16 * EDGE * width * op.shape[2], 24 * EDGE * width),
        name="ring_edges",
    )(coef, terms, other, phases, phases, forward, forward, op)


def launch_split_kernel(coef, t_in, o_in, t_edge, o_edge, phase, fwd, launched, phase_next):
    rows = phase.shape[1]
    pieces = (
        (t_edge, o_edge, slice(0, EDGE), slice(0, EDGE)),
        (t_in, o_in, slice(0, rows - 2 * EDGE), slice(EDGE, rows - EDGE)),
        (t_edge, o_edge, slice(EDGE, 2 * EDGE), slice(rows - EDGE, rows)),
    )
    for terms, other, span, place in pieces:
        updated = phase[0, place] - gradient_of(coef, terms, other, span)
        phase_next[0, place] = updated
        l_re, l_im = turned(updated, fwd[0, 0, place], fwd[0, 1, place])
        launched[0, place] = l_re
        launched[1, place] = l_im


def launch_split(coef, t_in, o_in, t_edge, o_edge, phases, forward):
    _, _, rows, width = forward.shape
    half = phases.shape[2] // WIDE
    inner = pl.BlockSpec((2, rows - 2 * EDGE, WIDE), lambda j, c: (0, 0, j))
    edge = pl.BlockSpec((2, 2 * EDGE, WIDE), lambda j, c: (0, 0, j))
    plane = pl.BlockSpec((1, rows, WIDE), lambda j, c: (j // half, 0, j % half))
    return pl.pallas_call(
        launch_split_kernel,
        out_shape=(
            jax.ShapeDtypeStruct(forward.shape[1:], BF16),
            jax.ShapeDtypeStruct(phases.shape, F32),
        ),
        grid_spec=pltpu.PrefetchScalarGridSpec(
            num_scalar_prefetch=1,
            grid=(width // WIDE,),
            in_specs=[
                inner,
                inner,
                edge,
                edge,
                plane,
                pl.BlockSpec((1, 2, rows, WIDE), lambda j, c: (0, 0, 0, j)),
            ],
            out_specs=(pl.BlockSpec((2, rows, WIDE), lambda j, c: (0, 0, j)), plane),
        ),
        compiler_params=params(),
        cost_estimate=cost(60 * rows * width, 24 * rows * width),
        name="launch",
    )(coef, t_in, o_in, t_edge, o_edge, phases, forward)


PAD = EDGE
MESH = pl.DeviceIdType.MESH


def band_rows(offs, blk, first, base, group, part, total):
    zero = jnp.zeros((BLK, BLK), F32)
    strips = []
    for r in range(group):
        row = base + r
        own = [blk[part, first + r, k].astype(F32) for k in range(blk.shape[2])]
        pieces = [zero] * r
        for d in range(2 * RADIUS + 1):
            place = row + (d - RADIUS)
            inside = (place >= 0) & (place < total)
            piece = zero
            for k, block in enumerate(own):
                piece = jnp.where(inside & (offs[k, row] == d - RADIUS), block, piece)
            pieces.append(piece)
        pieces += [zero] * (group - 1 - r)
        strips.append(jnp.concatenate(pieces, axis=1))
    return jnp.concatenate(strips, axis=0)


def stacked(re, im):
    return jnp.concatenate(
        [jnp.concatenate([re, -im], axis=1), jnp.concatenate([im, re], axis=1)], axis=0
    ).astype(BF16)


def exchange_kernel(
    tiles, offs, blocks, adjoint, forward, phase,
    mid, lau, t_in, o_in, phases, updated, hop,
    halo1, halo2, col_op, rin, red, ends, te, oe, sums, slots, coef,
    ph_sem, s1, r1, q1, f1, ti_sem, te_s, te_r, ar_s, ar_r, s2, r2, q2, f2,
):
    d = lax.axis_index("design")
    t = lax.axis_index("tile")
    m = lax.axis_index("mode")
    peers = 2 * tiles
    me = 2 * t + m
    levels = tiles // 2
    odd = lax.rem(t, 2)
    step = 2 * odd - 1
    level = jnp.where(odd == 1, t // 2, levels - 1 - t // 2)
    beside, across = t - step, t + step
    has_across = level < levels - 1
    rows, width = adjoint.shape[1], adjoint.shape[2]
    groups = width // WIDE
    total = blocks.shape[1]
    own_rows = total // tiles
    send_hops = jnp.where(has_across, groups * (levels - 1 - level) // levels, 0)
    pass_hops = groups * level // levels

    def device(tile, mode):
        return {"tile": tile, "mode": mode}

    def peer(p):
        who = lax.rem(me + p, peers)
        return device(who // 2, lax.rem(who, 2))

    barrier = pltpu.get_barrier_semaphore()
    for p in range(1, peers):
        pl.semaphore_signal(barrier, inc=1, device_id=peer(p), device_id_type=MESH)
    pl.semaphore_wait(barrier, peers - 1)

    def remote(src, dst, send, recv, tile, mode):
        return pltpu.make_async_remote_copy(
            src_ref=src, dst_ref=dst, send_sem=send, recv_sem=recv,
            device_id=device(tile, mode), device_id_type=MESH,
        )

    def cols(c, lead=0, wide=WIDE):
        start = c * WIDE + lead
        return pl.ds(start if isinstance(start, int) else pl.multiple_of(start, 128), wide)

    near = pl.multiple_of(odd * (rows - EDGE), EDGE)
    far_side = pl.multiple_of((1 - odd) * (rows - EDGE), EDGE)

    def raw(start, c):
        return adjoint.at[:, pl.ds(start, EDGE), cols(c)]

    def land1(side, c):
        return halo1.at[side, :, :, cols(c, PAD)]

    def land2(side, c):
        return halo2.at[side, :, :, cols(c)]

    def made(side, c):
        return ends.at[side, :, :, cols(c)]

    class Trip:
        def __init__(self, phase_no, sent, got, mid_got, passed, near_src, far_src, land):
            self.args = phase_no, sent, got, mid_got, passed, near_src, far_src, land

        def direct(self, c):
            _, sent, got, _, _, src, _, land = self.args
            return remote(src(c), land(1 - odd, c), sent.at[0, c], got.at[0, c], across, m)

        def far(self, c):
            _, sent, got, _, _, _, src, land = self.args
            return remote(src(c), land(odd, c), sent.at[1, c], got.at[1, c], beside, m)

        def first_hop(self, c):
            k, sent, _, mid_got, _, src, _, _ = self.args
            return remote(src(c), hop.at[k, :, :, cols(c)], sent.at[0, c], mid_got.at[c], beside, m)

        def second_hop(self, c):
            k, _, got, _, passed, _, _, land = self.args
            return remote(hop.at[k, :, :, cols(c)], land(odd, c), passed.at[c], got.at[0, c], t - 2 * step, m)

        def got_near(self, c):
            _, sent, got, _, _, src, _, land = self.args
            return remote(src(c), land(odd, c), sent.at[0, c], got.at[0, c], beside, m)

        def got_far(self, c):
            _, sent, got, _, _, _, src, land = self.args
            return remote(src(c), land(1 - odd, c), sent.at[1, c], got.at[1, c], beside, m)

        def send(self, c):
            @pl.when(c < send_hops)
            def _():
                self.first_hop(c).start()

            @pl.when(has_across & (c >= send_hops))
            def _():
                self.direct(c).start()

        def relay(self, c):
            @pl.when(c < pass_hops)
            def _():
                self.first_hop(c).wait_recv()
                self.second_hop(c).start()

        def arrived(self, c):
            self.got_far(c).wait_recv()

            @pl.when(has_across)
            def _():
                self.got_near(c).wait_recv()

        def close(self):
            each(groups, lambda c: self.far(c).wait_send())

            @pl.when(has_across)
            def _():
                each(groups, lambda c: self.direct(c).wait_send())

            each(pass_hops, lambda c: self.second_hop(c).wait_send())

    def each(n, fn):
        def step(c, carry):
            fn(c)
            return carry
        lax.fori_loop(0, n, step, 0)

    trip1 = Trip(0, s1, r1, q1, f1, lambda c: raw(near, c), lambda c: raw(far_side, c), land1)
    trip2 = Trip(1, s2, r2, q2, f2, lambda c: made(odd, c), lambda c: made(1 - odd, c), land2)
    each(send_hops, lambda c: trip1.first_hop(c).start())

    def enter(c):
        trip1.far(c).start()

        @pl.when(has_across & (c >= send_hops))
        def _():
            trip1.direct(c).start()

    each(groups, enter)

    share = remote(phase, phases.at[m], ph_sem.at[0], ph_sem.at[1], t, 1 - m)
    share.start()

    halo1[:, :, :, 0:PAD] = jnp.zeros((2, 2, EDGE, PAD), BF16)
    halo1[:, :, :, PAD + width : PAD + width + PAD] = jnp.zeros((2, 2, EDGE, PAD), BF16)
    sums[...] = jnp.zeros_like(sums)

    def blank(side):
        def step(c, carry):
            halo1[side, :, :, cols(c, PAD)] = jnp.zeros((2, EDGE, WIDE), BF16)
            halo2[side, :, :, cols(c)] = jnp.zeros((2, EDGE, WIDE), BF16)
            return carry
        lax.fori_loop(0, groups, step, 0)

    @pl.when(t == 0)
    def _():
        blank(0)

    @pl.when(t == tiles - 1)
    def _():
        blank(1)

    span_in, per = WIDE + 2 * EDGE, WIDE // BLK

    def build_group(blk, g):
        re, im = [band_rows(offs, blk, 0, g * per, per, part, total).T for part in range(2)]
        col_op[g, :span_in, :WIDE] = re.astype(BF16)
        col_op[g, :span_in, WIDE:] = im.astype(BF16)
        col_op[g, span_in:, :WIDE] = (-im).astype(BF16)
        col_op[g, span_in:, WIDE:] = re.astype(BF16)

    def build_rows(blk, lead):
        base = t * own_rows
        inner = own_rows - 2 * RADIUS
        rin[...] = stacked(*[band_rows(offs, blk, RADIUS, base + RADIUS, inner, p, total) for p in range(2)])
        red[0] = stacked(*[band_rows(offs, blk, 0, base, RADIUS, p, total) for p in range(2)])
        low = own_rows - RADIUS
        red[1] = stacked(*[band_rows(offs, blk, low, base + low, RADIUS, p, total) for p in range(2)])
        build_group(lead, 0)

    bands = blocks.shape[2]
    pltpu.emit_pipeline(
        build_rows, grid=(1,),
        in_specs=[pl.BlockSpec((2, own_rows, bands, BLK, BLK), lambda g: (0, t, 0, 0, 0)),
                  pl.BlockSpec((2, per, bands, BLK, BLK), lambda g: (0, 0, 0, 0, 0))],
    )(blocks, blocks)

    tile = pl.BlockSpec((2, rows, WIDE), lambda j: (0, 0, j))

    def column_step(left, middle, right, j, order):
        x = jnp.concatenate([window(left, middle, right, p) for p in order], axis=1)
        both = dot(x, col_op[j]).astype(BF16)
        mid[0, :, cols(j)], mid[1, :, cols(j)] = both[:, :WIDE], both[:, WIDE:]

    def now_and_then(trip, j, every, at, lead):
        @pl.when(lax.rem(j, every) == at)
        def _():
            trip.relay(lead + j // every)

    def adjoint_columns(left, middle, right, blk):
        j = pl.program_id(0)
        column_step(left, middle, right, j, (1, 0))
        build_group(blk, jnp.minimum(j + 1, groups - 1))
        now_and_then(trip1, j, 4, 3, 0)

    pltpu.emit_pipeline(
        adjoint_columns, grid=(groups,),
        in_specs=window_specs(rows, groups) + [
            pl.BlockSpec((2, per, bands, BLK, BLK), lambda j: (0, jnp.minimum(j + 1, groups - 1), 0, 0, 0))],
    )(adjoint, adjoint, adjoint, blocks)

    half = phase.shape[1] // WIDE

    def keep(src, dst):
        dst[0] = src[...]

    pltpu.emit_pipeline(
        keep, grid=(half,),
        in_specs=[pl.BlockSpec((rows, WIDE), lambda j: (0, j))],
        out_specs=[pl.BlockSpec((1, rows, WIDE), lambda j: (m, 0, j))],
    )(phase, phases)
    share.wait()
    plane = pl.BlockSpec((1, rows, WIDE), lambda j: (j // half, 0, j % half))
    inner_tile = pl.BlockSpec((2, rows - 2 * EDGE, WIDE), lambda j: (0, 0, j))

    def count(sum_re, sum_im):
        tall = sum_re.shape[0]
        sums[0] += jnp.sum(sum_re.reshape(tall // 8, 8, WIDE), axis=0)
        sums[1] += jnp.sum(sum_im.reshape(tall // 8, 8, WIDE), axis=0)

    def product(both, lit_re, lit_im):
        tall = both.shape[0] // 2
        adj_im = both[:tall].astype(BF16).astype(F32)
        adj_re = both[tall:].astype(BF16).astype(F32)
        lit_re, lit_im = lit_re.astype(F32), lit_im.astype(F32)
        t_re = adj_re * lit_re + adj_im * lit_im
        t_im = adj_re * lit_im - adj_im * lit_re
        count(t_re, t_im)
        return t_re.astype(BF16), t_im.astype(BF16)

    def inner_terms(ph, fwd, out):
        j = pl.program_id(0)
        low, high = EDGE, rows - EDGE
        for i, (a, b) in enumerate(((0, EDGE), (high, rows))):
            ends[i, 0, :, cols(j)], ends[i, 1, :, cols(j)] = turned(
                ph[0, a:b], fwd[0, a:b], fwd[1, a:b])
        lit_re, lit_im = turned(ph[0, low:high], fwd[0, low:high], fwd[1, low:high])
        both = dot(rin[...], jnp.concatenate([mid[0, :, cols(j)], mid[1, :, cols(j)]], axis=0))
        out[0], out[1] = product(both, lit_re, lit_im)
        now_and_then(trip1, j, 4, 3, 4)

    pltpu.emit_pipeline(
        inner_terms, grid=(groups,), in_specs=[plane, tile], out_specs=[inner_tile],
    )(phases, forward, t_in)

    swap_in = remote(t_in, o_in, ti_sem.at[0], ti_sem.at[1], t, 1 - m)
    swap_in.start()

    def swap_edge(c):
        return remote(te.at[:, :, cols(c)], oe.at[:, :, cols(c)], te_s.at[c], te_r.at[c], t, 1 - m)

    trip1.arrived(0)

    def halo_product(g, order):
        x = jnp.concatenate([
            jnp.concatenate([halo1[s, p, :, cols(g, 0, 2 * WIDE)] for p in order], axis=1) for s in range(2)
        ], axis=0)
        return dot(x, col_op[g]).astype(BF16)

    def edge_terms(j):
        both = halo_product(j, (1, 0))
        h = (both[:, :WIDE], both[:, WIDE:])
        top = jnp.concatenate([h[0][:EDGE], mid[0, : 2 * EDGE, cols(j)], h[1][:EDGE], mid[1, : 2 * EDGE, cols(j)]], axis=0)
        low = rows - 2 * EDGE
        bottom = jnp.concatenate([mid[0, low:, cols(j)], h[0][EDGE:], mid[1, low:, cols(j)], h[1][EDGE:]], axis=0)
        for i, field in enumerate((top, bottom)):
            span = slice(i * EDGE, (i + 1) * EDGE)
            te[0, span, cols(j)], te[1, span, cols(j)] = product(
                dot(red[i], field), ends[i, 0, :, cols(j)], ends[i, 1, :, cols(j)])
        swap_edge(j).start()

    def next_edge(j):
        now_and_then(trip1, j, 3, 0, 8)
        trip1.arrived(j + 1)
        edge_terms(j)

    each(groups - 2, next_edge)
    trip1.arrived(groups - 1)
    edge_terms(groups - 2)
    edge_terms(groups - 1)

    slots[me] = jnp.sum(sums[:, :, :128] + sums[:, :, 128:], axis=1)

    def report(p):
        who = peer(p)
        return pltpu.make_async_remote_copy(
            src_ref=slots.at[me], dst_ref=slots.at[me], send_sem=ar_s.at[p], recv_sem=ar_r.at[p],
            device_id=who, device_id_type=MESH)

    def heard(p):
        who = lax.rem(me + peers - p, peers)
        return pltpu.make_async_remote_copy(
            src_ref=slots.at[who], dst_ref=slots.at[who], send_sem=ar_s.at[p], recv_sem=ar_r.at[p],
            device_id=peer(p), device_id_type=MESH)

    for p in range(1, peers):
        report(p).start()
    def settle():
        for p in range(1, peers):
            heard(p).wait_recv()
        for i, who in enumerate((m, 1 - m)):
            value = slots[who]
            for k in range(1, tiles):
                value = value + slots[2 * k + who]
            for part in range(2):
                coef[2 * i + part] = jnp.sum(value[part : part + 1]) * (1.0 / (4.0 * width * 2))

    def gradient(own_re, own_im, other_re, other_im):
        return (coef[0] * own_im.astype(F32) - coef[1] * own_re.astype(F32)) + (
            coef[2] * other_im.astype(F32) - coef[3] * other_re.astype(F32))

    far = rows // EDGE - 1

    def chunk(j):
        return jnp.minimum(j, groups - 1)

    def edge_launch(p_top, p_bottom, f_top, f_bottom):
        j = pl.program_id(0)

        pl.when(j == 0)(settle)

        @pl.when(j < groups)
        def _():
            swap_edge(j).wait_recv()
            for i, (ph, fwd) in enumerate(((p_top, f_top), (p_bottom, f_bottom))):
                span = slice(i * EDGE, (i + 1) * EDGE)
                after = ph[0] - gradient(te[0, span, cols(j)], te[1, span, cols(j)],
                                         oe[0, span, cols(j)], oe[1, span, cols(j)])
                halo1[i, 0, :, cols(j, PAD)], halo1[i, 1, :, cols(j, PAD)] = turned(after, fwd[0], fwd[1])

        @pl.when(j > 0)
        def _():
            g = j - 1
            both = halo_product(g, (0, 1))
            o_re, o_im = both[:, :WIDE], both[:, WIDE:]
            for s in range(2):
                ends[s, 0, :, cols(g)] = o_re[s * EDGE : (s + 1) * EDGE]
                ends[s, 1, :, cols(g)] = o_im[s * EDGE : (s + 1) * EDGE]

            trip2.send(g)
            trip2.far(g).start()

    pltpu.emit_pipeline(
        edge_launch, grid=(groups + 1,),
        in_specs=[
            pl.BlockSpec((1, EDGE, WIDE), lambda j: (chunk(j) // half, 0, chunk(j) % half)),
            pl.BlockSpec((1, EDGE, WIDE), lambda j: (chunk(j) // half, far, chunk(j) % half)),
            pl.BlockSpec((2, EDGE, WIDE), lambda j: (0, 0, chunk(j))),
            pl.BlockSpec((2, EDGE, WIDE), lambda j: (0, far, chunk(j))),
        ],
    )(phases, phases, forward, forward)

    swap_in.wait()

    def launch_tile(own, other, ph, fwd, out):
        j = pl.program_id(0)
        for k, (a, b) in enumerate(((0, EDGE), (EDGE, rows - EDGE), (rows - EDGE, rows))):
            if k == 1:
                grad = gradient(own[0], own[1], other[0], other[1])
            else:
                span = slice((k // 2) * EDGE, (k // 2 + 1) * EDGE)
                grad = gradient(te[0, span, cols(j)], te[1, span, cols(j)],
                                oe[0, span, cols(j)], oe[1, span, cols(j)])
            after = ph[0, a:b] - grad
            @pl.when(j // half == m)
            def _(a=a, b=b, after=after):
                updated[a:b, cols(j - m * half)] = after

            out[0, a:b], out[1, a:b] = turned(after, fwd[0, a:b], fwd[1, a:b])
        now_and_then(trip2, j, 3, 2, 0)

    pltpu.emit_pipeline(
        launch_tile, grid=(groups,),
        in_specs=[inner_tile, inner_tile, plane, tile],
        out_specs=[tile],
    )(t_in, o_in, phases, forward, lau)

    def forward_columns(left, middle, right):
        j = pl.program_id(0)
        column_step(left, middle, right, j, (0, 1))
        now_and_then(trip2, j, 4, 3, 5)

    pltpu.emit_pipeline(
        forward_columns, grid=(groups,), in_specs=window_specs(rows, groups),
    )(lau, lau, lau)

    for p in range(1, peers):
        report(p).wait_send()
    each(groups, lambda c: swap_edge(c).wait_send())

    def last_rows(c):
        now_and_then(trip2, c, 3, 0, 9)
        trip2.arrived(c)
        low = rows - 2 * EDGE
        own = [mid[p, :, cols(c)] for p in range(2)]
        near_by = [[halo2[s, p, :, cols(c)] for p in range(2)] for s in range(2)]
        pieces = (
            (EDGE, rin[...], own),
            (0, red[0], [near_by[0][0], own[0][: 2 * EDGE], near_by[0][1], own[1][: 2 * EDGE]]),
            (rows - EDGE, red[1], [own[0][low:], near_by[1][0], own[1][low:], near_by[1][1]]),
        )
        done = [(start, dot(op, jnp.concatenate(parts, axis=0)).astype(BF16)) for start, op, parts in pieces]
        for start, both in done:
            tall = both.shape[0] // 2
            mid[0, start : start + tall, cols(c)] = both[:tall]
            mid[1, start : start + tall, cols(c)] = both[tall:]

    each(groups, last_rows)
    trip1.close()
    trip2.close()


def exchange(forward, adjoint, phase, blocks, offsets):
    tiles = lax.axis_size("tile")
    _, rows, width = forward.shape
    half = phase.shape[1]
    groups = width // WIDE
    inner = rows - 2 * EDGE
    hbm = pl.BlockSpec(memory_space=pl.ANY)
    dma = pltpu.SemaphoreType.DMA
    field = jax.ShapeDtypeStruct((2, rows, width), BF16)
    plane = jax.ShapeDtypeStruct((2, rows, half), F32)
    rin = (2 * inner, 2 * rows)
    red = (2, 2 * EDGE, 6 * EDGE)
    edges = (2, 2, EDGE, width)
    shapes = (
        pltpu.VMEM(field.shape, BF16), field,
        jax.ShapeDtypeStruct((2, inner, width), BF16),
        jax.ShapeDtypeStruct((2, inner, width), BF16),
        plane, pltpu.VMEM((rows, half), F32),
        jax.ShapeDtypeStruct(edges, BF16),
    )
    local = pl.BlockSpec(memory_space=pltpu.VMEM)
    edge = pltpu.VMEM((2, 2 * EDGE, width), BF16)
    peers = 2 * tiles
    out = pl.pallas_call(
        functools.partial(exchange_kernel, tiles),
        out_shape=shapes,
        in_specs=[pl.BlockSpec(memory_space=pltpu.SMEM)] + [hbm] * 4,
        out_specs=(local, hbm, hbm, hbm, hbm, local, hbm),
        scratch_shapes=[
            pltpu.VMEM((2, 2, EDGE, width + 2 * PAD), BF16),
            pltpu.VMEM(edges, BF16),
            pltpu.VMEM((groups, 2 * (WIDE + 2 * EDGE), 2 * WIDE), BF16),
            pltpu.VMEM(rin, BF16), pltpu.VMEM(red, BF16),
            pltpu.VMEM((2, 2, EDGE, width), BF16),
            edge, edge,
            pltpu.VMEM((2, 8, WIDE), F32),
            pltpu.VMEM((peers, 2, 128), F32),
            pltpu.SMEM((4,), F32),
            dma((2,)), dma((2, groups)), dma((2, groups)), dma((groups,)), dma((groups,)), dma((2,)),
            dma((groups,)), dma((groups,)), dma((peers,)), dma((peers,)),
            dma((2, groups)), dma((2, groups)), dma((groups,)), dma((groups,)),
        ],
        compiler_params=pltpu.CompilerParams(
            vmem_limit_bytes=49 * 1024 * 1024, collective_id=0, has_side_effects=True),
        cost_estimate=cost(50 * rows * width * 512, 100 * rows * width),
        name="exchange",
    )(offsets.T, blocks, adjoint, forward, phase)
    return out[0], out[5]


def exchange_edges(first, last):
    tiles = lax.axis_size("tile")
    top = lax.ppermute(last, "tile", [(t, t + 1) for t in range(tiles - 1)])
    bottom = lax.ppermute(first, "tile", [(t + 1, t) for t in range(tiles - 1)])
    return top, bottom


def body(forward, adjoint_next, phase, blocks, offsets):
    block_total = offsets.shape[0]
    tiles = lax.axis_size("tile")
    modes = lax.axis_size("mode")
    mode = lax.axis_index("mode")
    rows, width = forward.shape[2], forward.shape[3]
    adjoint = adjoint_next[0]
    if modes == 2 and tiles == 8 and width == 16 * WIDE and rows // BLK == 2 * RADIUS + WIDE // BLK:
        forward_next, phase_next = exchange(forward[0], adjoint, phase, blocks, offsets)
        return phase_next, forward_next[None]
    top, bottom = exchange_edges(adjoint[:, :EDGE], adjoint[:, rows - EDGE :])
    phases = lax.all_gather(phase, "mode", axis=0, tiled=False)

    raw_index = jnp.arange(block_total, dtype=jnp.int32)[:, None] + offsets
    inside = (raw_index >= 0) & (raw_index < block_total)
    pos = jnp.where(inside, offsets + RADIUS, -1).astype(jnp.int32)
    own_blocks = block_total // tiles
    split = own_blocks == 2 * RADIUS + WIDE // BLK
    start = lax.axis_index("tile") * own_blocks
    column_op = build(blocks, pos, WIDE // BLK, True)
    own_part = lax.dynamic_slice_in_dim(blocks, start, own_blocks, 1)
    own_pos = lax.dynamic_slice_in_dim(pos, start, own_blocks, 0)
    if split:
        inner = slice(RADIUS, own_blocks - RADIUS)
        row_op = build(own_part[:, inner], own_pos[inner], WIDE // BLK, False)
        ends = [own_part[:, :RADIUS], own_part[:, own_blocks - RADIUS :]]
        end_pos = [own_pos[:RADIUS], own_pos[own_blocks - RADIUS :]]
        edge_op = build(jnp.concatenate(ends, 1), jnp.concatenate(end_pos, 0), RADIUS, False)
    else:
        row_op = build(own_part, own_pos, min(WIDE // BLK, own_blocks), False)

    back_middle = column_pass(adjoint, column_op, True)
    lit = light(phases, forward)
    swap = [(m, (m + 1) % modes) for m in range(modes)]
    if split:
        t_in, s_in = adjoint_inner(back_middle, row_op, lit)
        o_in = lax.ppermute(t_in, "mode", swap)
        terms, sums = adjoint_edges(top, bottom, column_op, back_middle, edge_op, lit, s_in)
    else:
        terms, sums = adjoint_rows(top, bottom, column_op, back_middle, row_op, lit)
    other = lax.ppermute(terms, "mode", swap)
    own = jnp.sum(sums, axis=(1, 2))
    table = jnp.where(jnp.arange(modes)[:, None] == mode, own[None, :], 0.0)
    table = lax.psum(table, ("tile", "mode"))
    order = jnp.where(mode == 0, table, table[::-1])
    coef = order.reshape(-1) * (1.0 / (4.0 * width * modes))

    if split:
        first, last = ring_edges(coef, terms, other, phases, forward, column_op)
        top, bottom = exchange_edges(first, last)
        launched, updated = launch_split(coef, t_in, o_in, terms, other, phases, forward)
    else:
        edges = launch_edges(coef, terms, other, phases, forward)
        edges = column_pass(edges, column_op, False)
        top, bottom = exchange_edges(edges[:, :EDGE], edges[:, EDGE:])
        launched, updated = launch(coef, terms, other, phases, forward)
    middle = column_pass(launched, column_op, False)
    phase_next = lax.dynamic_index_in_dim(updated, mode, 0, keepdims=False)
    if split:
        whole = forward_inner(middle, row_op)
        return phase_next, forward_edges(top, middle, bottom, edge_op, whole)
    return phase_next, forward_rows(top, middle, bottom, row_op)


def solution(mesh):
    placed = (
        P(("design", "mode"), None, "tile", None),
        P(("design", "mode"), None, "tile", None),
        P(("design", "tile"), "mode"),
        P(None, "design", None, None, None),
        P("design", None),
    )
    return jax.shard_map(
        body,
        mesh=mesh,
        in_specs=placed,
        out_specs=(P(("design", "tile"), "mode"), P(("design", "mode"), None, "tile", None)),
        check_vma=False,
    )
```
